32 devices in a mesh: grow: 4 (over z), gy: 4 (over x, core), gz: 2 (over y).
Axes of the slice: x: 2, y: 2, z: 4, core: 2. Of those that a mesh axis runs over, the one named last changes fastest.
Arguments:
- labels: int32 [128, 32, 256], P('grow', 'gy', 'gz'), may hold values from 0 to 3
- potential: float32 [2, 128, 32, 256], P(None, 'grow', 'gy', 'gz'), may hold values from -3 to 3
- melt_codes: int32 [16, 32, 256], P(None, 'gy', 'gz'), may hold values from 0 to 7
- melt_table: float32 [2, 8], replicated, may hold values from -1 to 1
Outputs:
- phases: float32 [4, 128, 32, 256], P(None, 'grow', 'gy', 'gz')
- potentials: float32 [2, 128, 32, 256], P(None, 'grow', 'gy', 'gz')
The draws below stay inside these ranges and needn't reach their ends.
All inputs are finite; a program needn't handle non-finite values.
Results may differ from the reference program's by a relative error of at most 0.0001.
Values sent between devices are 32-bit elements; how exact they have to be, the bound alone decides.
A program may use at most 64 MiB of HBM per device.

```python
import jax
import jax.numpy as jnp
from jax import lax

SHIFT = 16
LEVELS = 8
STEPS_BEFORE = 3
STEPS_AFTER = 2
NG = 128
NY = 32
NZ = 256


def plant(values, stream_key, smallest, largest):
    place = [jax.random.randint(jax.random.fold_in(stream_key, axis), (), 0, length) for axis, length in enumerate(values.shape)]
    longest = values.shape.index(max(values.shape))
    next_to = place[:longest] + [(place[longest] + 1) % values.shape[longest]] + place[longest + 1:]
    return values.at[tuple(place)].set(smallest).at[tuple(next_to)].set(largest)


def block_levels(own_key, shape, cuts, low, top_value):
    level = 1.0
    for position, parts in cuts:
        draws = jax.random.uniform(jax.random.fold_in(jax.random.fold_in(own_key, 6), position), (parts,), jnp.float32, low / len(cuts), top_value / len(cuts))
        level = level * jnp.repeat(jnp.exp(draws), shape[position] // parts).reshape((-1,) + (1,) * (len(shape) - 1 - position))
    return level


def scatter_about(stream_key, shape, scale, limit, cuts=(), held_as=jnp.bfloat16):
    entries = scale * jax.random.normal(stream_key, shape, jnp.float32)
    if cuts:
        entries = entries * block_levels(stream_key, shape, cuts, -0.22, 0.18)
    return jnp.clip(entries, -limit, limit).astype(held_as)


def setup_inputs(seed: int = 0) -> dict:
    keys = jax.random.split(jax.random.key(seed), 5)
    labels = plant(jax.random.randint(keys[0], (NG, NY, NZ), 0, 4), jax.random.fold_in(keys[0], 1), 0, 3).astype(jnp.int32)
    potential = scatter_about(keys[1], (2, NG, NY, NZ), 0.5, 3.0, ((1, 4), (2, 4), (3, 2)), jnp.float32)
    melt_codes = plant(jax.random.randint(keys[2], (SHIFT, NY, NZ), 0, LEVELS), jax.random.fold_in(keys[2], 1), 0, LEVELS - 1).astype(jnp.int32)
    melt_table = jnp.clip(jax.random.uniform(keys[3], (2, LEVELS), jnp.float32, -1.0, 1.0), -1.0, 1.0)
    return {"labels": labels, "potential": potential, "melt_codes": melt_codes, "melt_table": melt_table}


comp_table = ((0.8, 0.1), (0.1, 0.8), (0.1, 0.1), (0.35, 0.35))
free_energy = (-0.05, -0.05, -0.05, 0.0)
diffusivity = (0.05, 0.05, 0.05, 1.0)
grad_rate = 0.12
well_rate = 0.3
drive_rate = 0.5
diff_rate = 0.15


def laplacian(fields, grow_padded, side_padded):
    total = grow_padded[:, 2:] + grow_padded[:, :-2]
    total = total + (side_padded[:, :, 2:, 1:-1] + side_padded[:, :, :-2, 1:-1])
    total = total + (side_padded[:, :, 1:-1, 2:] + side_padded[:, :, 1:-1, :-2])
    return total - 6.0 * fields


def advance(fields, grow_padded, side_padded):
    phases = fields[:4]
    chem_pot = fields[4:]
    laplace = laplacian(fields, grow_padded, side_padded)
    comp = jnp.array(comp_table, jnp.float32)
    comp_first = comp[:, 0].reshape(4, 1, 1, 1)
    comp_second = comp[:, 1].reshape(4, 1, 1, 1)
    energy = jnp.array(free_energy, jnp.float32).reshape(4, 1, 1, 1)
    spread = jnp.array(diffusivity, jnp.float32).reshape(4, 1, 1, 1)
    grand_pot = energy - (chem_pot[0:1] * comp_first + chem_pot[1:2] * comp_second)
    squares = phases * phases
    others = jnp.sum(squares, axis=0, keepdims=True) - squares
    slope = 6.0 * phases * (1.0 - phases)
    increment = grad_rate * laplace[:4] - 2.0 * well_rate * phases * others - drive_rate * slope * grand_pot
    increment = increment - jnp.mean(increment, axis=0, keepdims=True)
    clipped = jnp.clip(phases + increment, 0.0, 1.0)
    new_phases = clipped / jnp.sum(clipped, axis=0, keepdims=True)
    change = new_phases * new_phases * (3.0 - 2.0 * new_phases) - phases * phases * (3.0 - 2.0 * phases)
    mobility = jnp.sum(phases * spread, axis=0, keepdims=True)
    release = jnp.concatenate([jnp.sum(change * comp_first, axis=0, keepdims=True), jnp.sum(change * comp_second, axis=0, keepdims=True)], axis=0)
    new_chem = chem_pot + diff_rate * mobility * laplace[4:] - release
    return jnp.concatenate([new_phases, new_chem], axis=0)


def pad_faces(fields):
    grow_padded = jnp.concatenate([fields[:, :1], fields, fields[:, -1:]], axis=1)
    side_padded = jnp.concatenate([fields[:, :, -1:], fields, fields[:, :, :1]], axis=2)
    side_padded = jnp.concatenate([side_padded[:, :, :, -1:], side_padded, side_padded[:, :, :, :1]], axis=3)
    return grow_padded, side_padded


def melt_planes(melt_codes, melt_table):
    levels = melt_table.shape[1]
    onehot = (melt_codes[None] == jnp.arange(levels, dtype=jnp.int32).reshape(levels, 1, 1, 1)).astype(jnp.float32)
    chem_pot = jnp.einsum("ik,kabc->iabc", melt_table.astype(jnp.float32), onehot, precision=lax.Precision.HIGHEST)
    liquid = (jnp.arange(4, dtype=jnp.int32) == 3).astype(jnp.float32).reshape(4, 1, 1, 1)
    phases = jnp.broadcast_to(liquid, (4,) + melt_codes.shape)
    return jnp.concatenate([phases, chem_pot], axis=0)


def reference(labels, potential, melt_codes, melt_table):
    phases = (labels[None] == jnp.arange(4, dtype=jnp.int32).reshape(4, 1, 1, 1)).astype(jnp.float32)
    fields = jnp.concatenate([phases, potential], axis=0)
    for iteration in range(STEPS_BEFORE):
        grow_padded, side_padded = pad_faces(fields)
        fields = advance(fields, grow_padded, side_padded)
    fields = jnp.concatenate([fields[:, SHIFT:], melt_planes(melt_codes, melt_table)], axis=1)
    for iteration in range(STEPS_AFTER):
        grow_padded, side_padded = pad_faces(fields)
        fields = advance(fields, grow_padded, side_padded)
    return fields[:4], fields[4:]
```

```python
import functools

import jax
import jax.numpy as jnp
from jax import lax
from jax.experimental import pallas as pl
from jax.experimental.pallas import tpu as pltpu
from jax.sharding import PartitionSpec as P

STEPS_BEFORE = 3
STEPS_AFTER = 2
STEPS = STEPS_BEFORE + STEPS_AFTER
HALF = 9
SLOT = 2 * HALF
GROUPS = 3
FIELDS = 11
MOVING = 5
PAD = 8
MESH = pl.DeviceIdType.MESH

LAM = 0.12
BETA = 5.0 / LAM**2
MU = 17.5 / (LAM * BETA)
OWN = (1.0 / LAM - 6.0) / BETA
TILT = 1.25 / (LAM * BETA)
BACK = 0.2 * MU / LAM**3


class Plan:
    def __init__(self, planes, rows, shift):
        self.planes, self.rows, self.shift = planes, rows, shift
        self.low = shift - STEPS + 1
        self.chunks = planes // 8 + 1
        self.deep = 8 * (self.chunks + 2)
        self.above = shift + STEPS
        self.tall = rows + 2 * STEPS

    def at(self, plane):
        return plane - self.low + PAD


def phase_state(label, pot):
    q = [jnp.where(label == float(a), LAM, 0.0) for a in range(3)]
    y = [jnp.where(label == float(a), LAM * BETA * OWN, 0.0) for a in range(3)]
    liquid = label == 3.0
    mob = jnp.where(liquid, 0.15, 0.0075)
    u = [MU * v for v in pot]
    comp = [jnp.where(liquid, 0.35 * MU, jnp.where(label == float(i), 0.8 * MU, 0.1 * MU)) for i in range(2)]
    rest = [(u[i] + comp[i]) - (6.0 * mob) * u[i] for i in range(2)]
    return q + u + y + rest + [mob]


def clip_step(sums, y):
    x = [sums[a] + y[a] for a in range(3)]
    x.append(1.0 - (x[0] + x[1] + x[2]))
    held = [jnp.clip(v, 0.0, 1.0) for v in x]
    return held, 1.0 / ((held[0] + held[1]) + (held[2] + held[3]))


def cell_step(sums, y, rest, mob):
    held, inverse = clip_step(sums, y)
    total = [rest[i] + mob * sums[3 + i] for i in range(2)]
    scaled = LAM * inverse
    q = [v * scaled for v in held]
    square = [v * v for v in q]
    h = [square[a] * (1.5 * LAM - q[a]) for a in range(4)]
    shared = BACK * ((h[0] + h[1]) + (h[2] + 3.5 * h[3]))
    u = [(total[i] - shared) - (7.0 * BACK) * h[i] for i in range(2)]
    both = u[0] + u[1]
    third = both * (1.0 / 7.0) + TILT
    pull = [third + u[0], third + u[1], third, 0.5 * both]
    well = OWN - ((square[0] + square[1]) + (square[2] + square[3]))
    local = [q[a] * ((well + square[a]) + pull[a] * (LAM - q[a])) for a in range(4)]
    mean = 0.25 * ((local[0] + local[1]) + (local[2] + local[3])) - 0.07 / BETA
    y = [BETA * (local[a] - mean) for a in range(3)]
    mob = 0.0075 + (0.1425 / LAM) * q[3]
    six = 6.0 * mob
    rest = [total[i] - six * u[i] for i in range(2)]
    return q[:3] + u + y + rest + [mob]


def last_step(sums, y, rest, mob):
    held, inverse = clip_step(sums, y)
    p = [v * inverse for v in held]
    h = [v * v * (1.5 - v) for v in p]
    shared = 0.2 * ((h[0] + h[1]) + (h[2] + 3.5 * h[3]))
    total = [(rest[i] + mob * sums[3 + i]) * (1.0 / MU) for i in range(2)]
    return p, [(total[i] - shared) - 1.4 * h[i] for i in range(2)]


def lanes():
    return lax.broadcasted_iota(jnp.int32, (8, 128), 1)


def load(ref, *index):
    return ref[index]


def main_sums(state, near, row, low, at_left, at_right):
    slot, group = (row // GROUPS, row % GROUPS) if isinstance(row, int) else (lax.div(row, GROUPS), lax.rem(row, GROUPS))
    turn = 128 - (SLOT * slot + HALF // 2 + 1)
    sums = []
    for f in range(MOVING):
        v = state[f, row, pl.ds(low, 8), :]
        edge = pltpu.roll(near[f, group, pl.ds(low, 8), :], turn, 1)
        right = pltpu.roll(jnp.where(at_left, edge, v), 127, 1)
        left = pltpu.roll(jnp.where(at_right, edge, v), 1, 1)
        grow = state[f, row, pl.ds(low + 1, 8), :] + state[f, row, pl.ds(low - 1, 8), :]
        side = state[f, row + 1, pl.ds(low, 8), :] + state[f, row - 1, pl.ds(low, 8), :]
        sums.append((grow + side) + (right + left))
    return sums


def center(state, row, low):
    y = [state[MOVING + a, row, pl.ds(low, 8), :] for a in range(3)]
    rest = [state[MOVING + 3 + i, row, pl.ds(low, 8), :] for i in range(2)]
    return y, rest, state[FIELDS - 1, row, pl.ds(low, 8), :]


def near_of(v, swap):
    return jnp.where(swap, pltpu.roll(v, 128 - (HALF - 1), 1), v)


def front_kernel(
    plan, mesh_shape, levels, lab, pot, codes, table, last_state, last_near,
    lab_up, pot_up, raw, pack, strip, states, strips, nears,
    g_send, g_recv, y_send, y_recv, z_send, z_recv,
):
    g, y, z = lax.axis_index("grow"), lax.axis_index("gy"), lax.axis_index("gz")
    count_g, count_y, count_z = mesh_shape
    rows, tall, planes, shift = plan.rows, plan.tall, plan.planes, plan.shift
    has_below, has_above = g > 0, g < count_g - 1
    is_first, is_last = g == 0, g == count_g - 1
    y_up, y_down = lax.rem(y + 1, count_y), lax.rem(y + count_y - 1, count_y)
    z_other = lax.rem(z + 1, count_z)
    chunks = plan.chunks

    barrier = pltpu.get_barrier_semaphore()

    def greet(target):
        pl.semaphore_signal(barrier, inc=1, device_id=target, device_id_type=MESH)

    @pl.when(has_below)
    def _():
        greet((g - 1, y, z))

    @pl.when(has_above)
    def _():
        greet((g + 1, y, z))

    greet((g, y_up, z))
    greet((g, y_down, z))
    greet((g, y, z_other))
    pl.semaphore_wait(barrier, 3 + has_below.astype(jnp.int32) + has_above.astype(jnp.int32))

    first_up = (planes - plan.low) // 8
    cut = 8 * (first_up + 1) - (planes - plan.low)
    splits = [0] + list(range(cut, plan.above - 1, 8)) + [plan.above]
    pieces = len(splits) - 1

    def g_copies(piece):
        begin, end = splits[piece], splits[piece + 1]
        at = pl.ds(begin * rows, (end - begin) * rows)
        copies = []
        for i in range(3):
            src, dst = (lab.at[at], lab_up.at[at]) if i == 0 else (pot.at[i - 1, at], pot_up.at[i - 1, at])
            sem = 3 * piece + i
            copies.append(pltpu.make_async_remote_copy(
                src_ref=src, dst_ref=dst, send_sem=g_send.at[sem], recv_sem=g_recv.at[sem],
                device_id=(g - 1, y, z), device_id_type=MESH))
        return copies

    @pl.when(has_below)
    def _():
        for piece in range(pieces):
            for copy in g_copies(piece):
                copy.start()

    def y_copies(chunk):
        copies = []
        for up in range(2):
            src, dst, target = (rows, 0, y_up) if up else (STEPS, STEPS + rows, y_down)
            sem = 2 * chunk + up
            at = pl.ds(PAD + 8 * chunk, 8)
            copies.append(pltpu.make_async_remote_copy(
                src_ref=raw.at[:, pl.ds(src, STEPS), at], dst_ref=raw.at[:, pl.ds(dst, STEPS), at],
                send_sem=y_send.at[sem], recv_sem=y_recv.at[sem],
                device_id=(g, target, z), device_id_type=MESH))
        return copies

    def z_copy(chunk):
        at = pl.ds(PAD + 8 * chunk, 8)
        return pltpu.make_async_remote_copy(
            src_ref=pack.at[:, :, at], dst_ref=strip.at[:, :, at],
            send_sem=z_send.at[chunk], recv_sem=z_recv.at[chunk],
            device_id=(g, y, z_other), device_id_type=MESH)

    def row_of(labels, pots, i, row, begin, size):
        at = pl.ds(begin * rows + row, size, stride=rows)
        return labels[at].astype(jnp.float32) if i == 0 else pots[i - 1, at]

    def fill(labels, pots, begin, size, to):
        for i in range(3):
            for row in range(rows):
                raw[i, STEPS + row, to : to + size] = row_of(labels, pots, i, row, begin, size)

    def fill_melt(begin, size, to, copies=1):
        for row in range(rows):
            at = pl.ds(to, size * copies)
            code = codes[pl.ds(begin * rows + row, size, stride=rows)]
            raw[0, STEPS + row, at] = jnp.full((size * copies, 128), 3.0, jnp.float32)
            for i in range(2):
                value = jnp.zeros((size, 128), jnp.float32)
                for level in range(levels):
                    value = jnp.where(code == level, table[i, level], value)
                raw[1 + i, STEPS + row, at] = jnp.broadcast_to(value, (size * copies, 128))

    def enter(piece):
        begin, end = splits[piece], splits[piece + 1]
        to = plan.at(planes + begin)

        @pl.when(has_above)
        def _():
            for copy in g_copies(piece):
                copy.wait_recv()
            size = min(end - begin, 8)
            fill(lab_up, pot_up, begin, size, to)
            if end - begin > 8:
                fill(lab_up, pot_up, end - 1, 1, to + 8)

        @pl.when(is_last)
        def _():
            if piece == 0:
                fill(lab, pot, planes - 1, 1, to)
                fill_melt(0, end - 1, to + 1)
            else:
                size = min(end - 1, shift) - (begin - 1)
                fill_melt(begin - 1, size, to)
                if end - begin > size:
                    fill_melt(shift - 1, 1, to + size, end - begin - size)

    def pack_chunk(chunk):
        at = pl.ds(PAD + 8 * chunk, 8)
        lane = lanes()
        for i in range(3):
            for group in range(GROUPS):
                packed = jnp.zeros((8, 128), jnp.float32)
                for slot in range(tall // GROUPS):
                    v = raw[i, GROUPS * slot + group, at]
                    first = SLOT * slot
                    packed = jnp.where(lane >= first, pltpu.roll(v, first + HALF // 2 + 1, 1), packed)
                    packed = jnp.where(lane >= first + HALF, pltpu.roll(v, first + HALF + HALF // 2, 1), packed)
                pack[i, group, at] = packed

    def send_z(chunk):
        for copy in y_copies(chunk):
            copy.wait_recv()
        pack_chunk(chunk)
        z_copy(chunk).start()

    def send_y(chunk):
        for copy in y_copies(chunk):
            copy.start()

    place = lanes() % SLOT
    from_other = (place < HALF // 2 + 1) | (place >= SLOT - HALF // 2 - 1)
    swap = place == HALF // 2 + 1

    def unpack_rows(to, begin, end):
        def body(row, carry):
            at = pl.ds(to, 8)
            new = phase_state(raw[0, row, at], [raw[1, row, at], raw[2, row, at]])
            for f in range(FIELDS):
                states[0, f, row, at] = new[f]
            return carry

        lax.fori_loop(begin, end, body, 0)

    def unpack_strips(source_low, target_low, state, near):
        for group in range(GROUPS):
            at = pl.ds(source_low, 8)
            value = [jnp.where(from_other, strip[i, group, at], pack[i, group, at]) for i in range(3)]
            new = phase_state(value[0], value[1:])
            to = pl.ds(target_low, 8)
            for f in range(FIELDS):
                state[f, group, to] = new[f]
            for f in range(MOVING):
                near[f, group, to] = near_of(new[f], swap)

    def unpack(chunk):
        z_copy(chunk).wait_recv()
        to = PAD + 8 * chunk
        unpack_rows(to, 0, tall)
        unpack_strips(to, to, strips.at[0], nears.at[0])

    at_left, at_right = lanes() == 0, lanes() == 127

    def near_ref(step):
        return nears.at[step] if step < STEPS - 1 else last_near

    def state_ref(step):
        return states.at[step] if step < STEPS - 1 else last_state

    def strip_step(step, low):
        src = strips.at[step - 1]
        at = pl.ds(low, 8)
        for group in range(GROUPS):
            sums = []
            for f in range(MOVING):
                v = src[f, group, at]
                up = src[f, (group + 1) % GROUPS, at]
                down = src[f, (group + 2) % GROUPS, at]
                if group == 0:
                    down = pltpu.roll(down, SLOT, 1)
                if group == GROUPS - 1:
                    up = pltpu.roll(up, 128 - SLOT, 1)
                total = src[f, group, pl.ds(low + 1, 8)] + src[f, group, pl.ds(low - 1, 8)]
                sums.append((total + (up + down)) + (pltpu.roll(v, 127, 1) + pltpu.roll(v, 1, 1)))
            new = cell_step(sums, *center(src, group, low))
            if step < STEPS - 1:
                for f in range(FIELDS):
                    strips[step, f, group, at] = new[f]
            for f in range(MOVING):
                near_ref(step)[f, group, at] = near_of(new[f], swap)

    def row_step(step, row, low):
        src, near = states.at[step - 1], nears.at[step - 1]
        sums = main_sums(src, near, row, low, at_left, at_right)
        new = cell_step(sums, *center(src, row, low))
        for f in range(FIELDS):
            state_ref(step)[f, row, pl.ds(low, 8), :] = new[f]

    def copy_plane(step, begin, end):
        def body(row, carry):
            for f in range(MOVING):
                state_ref(step)[f, row, pl.ds(end, 1)] = state_ref(step)[f, row, pl.ds(begin, 1)]
            return carry

        lax.fori_loop(step, tall - step, body, 0)
        if step < STEPS - 1:
            for group in range(GROUPS):
                for f in range(MOVING):
                    strips[step, f, group, pl.ds(end, 1)] = strips[step, f, group, pl.ds(begin, 1)]
        for group in range(GROUPS):
            for f in range(MOVING):
                near_ref(step)[f, group, pl.ds(end, 1)] = near_ref(step)[f, group, pl.ds(begin, 1)]

    def melt_fill(low):
        step = STEPS_BEFORE

        def body(row, carry):
            at = pl.ds(low + 1, 8)
            new = phase_state(raw[0, row, at], [raw[1, row, at], raw[2, row, at]])
            for f in range(FIELDS):
                states[step, f, row, pl.ds(low, 8)] = new[f]
            return carry

        lax.fori_loop(step, tall - step, body, 0)
        unpack_strips(low + 1, low, strips.at[step], nears.at[step])

    def advance(step, low):
        strip_step(step, low)
        count = (tall - 2 * step) // 2

        def body(half, carry):
            for part in range(count):
                row_step(step, step + count * half + part, low)
            return carry

        lax.fori_loop(0, 2, body, 0)

    first_plane, top_plane = plan.at(shift), plan.at(planes)

    def prologue():
        fill(lab, pot, plan.low - PAD, 8, 0)
        for chunk in range(first_up):
            fill(lab, pot, plan.low + 8 * chunk, 8, PAD + 8 * chunk)
            send_y(chunk)
        done = plan.low + 8 * first_up
        fill(lab, pot, done, planes - done, PAD + 8 * first_up)
        unpack_rows(0, STEPS, STEPS + rows)

    prologue()

    def before(stage):
        if stage == 0:
            for chunk in range(first_up):
                send_z(chunk)
            for piece in range(pieces):
                enter(piece)
                send_y(first_up + piece)
            send_z(first_up)
            unpack(0)
        unpack(stage + 1)

    def middle(stage):
        chunk = first_up + 1 + stage
        if chunk < chunks:
            send_z(chunk)

    def stage_body(stage, carry):
        def run_at(action):
            for at in range(chunks):
                @pl.when(stage == at)
                def _():
                    action(at)

        def before_or_end(at):
            if at < chunks - 1:
                before(at)
            else:
                unpack_rows(PAD + 8 * chunks, STEPS, STEPS + rows)

        run_at(before_or_end)
        for step in range(1, STEPS):
            low = PAD + 1 + 8 * stage - step
            if step <= STEPS_BEFORE:
                top = (top_plane - (PAD + 1 - step)) // 8
                pl.when((stage <= top) | jnp.logical_not(is_last))(functools.partial(advance, step, low))
            else:
                advance(step, low)

            def planes_at(plane):
                return (plane - (PAD + 1 - step)) // 8

            if step < STEPS_BEFORE:
                @pl.when(is_last & (stage == planes_at(top_plane)))
                def _():
                    copy_plane(step, top_plane - 1, top_plane)
            if step == STEPS_BEFORE:
                @pl.when(is_first & (stage == planes_at(first_plane)))
                def _():
                    copy_plane(step, first_plane, first_plane - 1)

                @pl.when(is_last & (stage == planes_at(top_plane)))
                def _():
                    melt_fill(top_plane)

                @pl.when(is_last & (stage > planes_at(top_plane)))
                def _():
                    melt_fill(jnp.minimum(low, top_plane + shift + 1 - 8))
            if step == STEPS - 1:
                @pl.when(is_first & (stage == planes_at(first_plane)))
                def _():
                    copy_plane(step, first_plane, first_plane - 1)

                @pl.when(is_last & (stage == planes_at(first_plane + planes)))
                def _():
                    copy_plane(step, first_plane + planes - 1, first_plane + planes)
            if step == 2:
                run_at(middle)
        return carry

    lax.fori_loop(0, chunks, stage_body, 0)

    for chunk in range(chunks):
        for copy in y_copies(chunk):
            copy.wait_send()
        z_copy(chunk).wait_send()

    @pl.when(has_below)
    def _():
        for piece in range(pieces):
            for copy in g_copies(piece):
                copy.wait_send()


def last_kernel(plan, state, near, phases, potentials, p_out, m_out, sems):
    rows, planes = plan.rows, plan.planes
    at_left, at_right = lanes() == 0, lanes() == 127
    copies = []
    for tile in range(planes // 8):
        low = plan.at(plan.shift) + 8 * tile
        for row in range(rows):
            sums = main_sums(state, near, STEPS + row, low, at_left, at_right)
            p, m = last_step(sums, *center(state, STEPS + row, low))
            at = pl.ds(8 * tile * rows + row, 8, stride=rows)
            for f in range(4):
                p_out[f, at, :] = p[f]
            for i in range(2):
                m_out[i, at, :] = m[i]
        at = pl.ds(8 * tile * rows, 8 * rows)
        for i, (src, dst) in enumerate(((p_out, phases), (m_out, potentials))):
            copy = pltpu.make_async_copy(src.at[:, at], dst.at[:, at], sems.at[2 * tile + i])
            copy.start()
            copies.append(copy)
    for copy in copies:
        copy.wait()


def on_device(mesh_shape, labels, potential, melt_codes, melt_table):
    planes, rows, width = labels.shape
    shift, levels = melt_codes.shape[0], melt_table.shape[1]
    plan = Plan(planes, rows, shift)
    flat = planes * rows
    vmem = pl.BlockSpec(memory_space=pltpu.VMEM)
    smem = pl.BlockSpec(memory_space=pltpu.SMEM)
    hbm = pl.BlockSpec(memory_space=pl.ANY)
    f32 = jnp.float32
    dma = pltpu.SemaphoreType.DMA
    deep, tall, chunks = plan.deep, plan.tall, plan.chunks
    state, near = pl.pallas_call(
        functools.partial(front_kernel, plan, mesh_shape, levels),
        out_shape=(
            pltpu.VMEM((FIELDS, tall, deep, width), f32),
            pltpu.VMEM((MOVING, GROUPS, deep, width), f32),
        ),
        in_specs=[vmem, vmem, vmem, smem],
        out_specs=(vmem, vmem),
        scratch_shapes=[
            pltpu.VMEM((plan.above * rows, width), jnp.int32),
            pltpu.VMEM((2, plan.above * rows, width), f32),
            pltpu.VMEM((3, tall, deep, width), f32),
            pltpu.VMEM((3, GROUPS, deep, width), f32),
            pltpu.VMEM((3, GROUPS, deep, width), f32),
            pltpu.VMEM((STEPS - 1, FIELDS, tall, deep, width), f32),
            pltpu.VMEM((STEPS - 1, FIELDS, GROUPS, deep, width), f32),
            pltpu.VMEM((STEPS - 1, MOVING, GROUPS, deep, width), f32),
            dma((3 * chunks,)), dma((3 * chunks,)), dma((2 * chunks,)), dma((2 * chunks,)), dma((chunks,)), dma((chunks,)),
        ],
        compiler_params=pltpu.CompilerParams(collective_id=0, has_side_effects=True, vmem_limit_bytes=48 << 20),
        name="front",
    )(labels.reshape(flat, width), potential.reshape(2, flat, width), melt_codes.reshape(shift * rows, width), melt_table)
    state, near = (pltpu.with_memory_space_constraint(v, pltpu.VMEM) for v in (state, near))
    phases, potentials = pl.pallas_call(
        functools.partial(last_kernel, plan),
        out_shape=(
            jax.ShapeDtypeStruct((4, flat, width), f32),
            jax.ShapeDtypeStruct((2, flat, width), f32),
        ),
        in_specs=[vmem, vmem],
        out_specs=(hbm, hbm),
        scratch_shapes=[
            pltpu.VMEM((4, flat, width), f32),
            pltpu.VMEM((2, flat, width), f32),
            dma((2 * (planes // 8),)),
        ],
        compiler_params=pltpu.CompilerParams(vmem_limit_bytes=8 << 20),
        name="last",
    )(state, near)
    return phases.reshape(4, planes, rows, width), potentials.reshape(2, planes, rows, width)


def solution(mesh):
    mesh_shape = tuple(mesh.shape[axis] for axis in ("grow", "gy", "gz"))
    return jax.shard_map(
        functools.partial(on_device, mesh_shape),
        mesh=mesh,
        in_specs=(P("grow", "gy", "gz"), P(None, "grow", "gy", "gz"), P(None, "gy", "gz"), P()),
        out_specs=(P(None, "grow", "gy", "gz"), P(None, "grow", "gy", "gz")),
        check_vma=False,
    )
```

```python
import functools

import jax
import jax.numpy as jnp
from jax import lax
from jax.experimental import pallas as pl
from jax.experimental.pallas import tpu as pltpu
from jax.sharding import PartitionSpec as P

STEPS_BEFORE = 3
STEPS_AFTER = 2
STEPS = STEPS_BEFORE + STEPS_AFTER
HALF = 9
SLOT = 2 * HALF
GROUPS = 3
FIELDS = 11
MOVING = 5
PAD = 8
MESH = pl.DeviceIdType.MESH

LAM = 0.12
BETA = 5.0 / LAM**2
MU = 17.5 / (LAM * BETA)
OWN = (1.0 / LAM - 6.0) / BETA
TILT = 1.25 / (LAM * BETA)
BACK = 0.2 * MU / LAM**3


class Plan:
    def __init__(self, planes, rows, shift):
        self.planes, self.rows, self.shift = planes, rows, shift
        self.low = shift - STEPS + 1
        self.chunks = planes // 8 + 1
        self.deep = 8 * (self.chunks + 2)
        self.above = shift + STEPS
        self.tall = rows + 2 * STEPS

    def at(self, plane):
        return plane - self.low + PAD


def phase_state(label, pot):
    q = [jnp.where(label == float(a), LAM, 0.0) for a in range(3)]
    y = [jnp.where(label == float(a), LAM * BETA * OWN, 0.0) for a in range(3)]
    liquid = label == 3.0
    mob = jnp.where(liquid, 0.15, 0.0075)
    u = [MU * v for v in pot]
    comp = [jnp.where(liquid, 0.35 * MU, jnp.where(label == float(i), 0.8 * MU, 0.1 * MU)) for i in range(2)]
    rest = [(u[i] + comp[i]) - (6.0 * mob) * u[i] for i in range(2)]
    return q + u + y + rest + [mob]


def clip_step(sums, y):
    x = [sums[a] + y[a] for a in range(3)]
    x.append(1.0 - (x[0] + x[1] + x[2]))
    held = [jnp.clip(v, 0.0, 1.0) for v in x]
    return held, 1.0 / ((held[0] + held[1]) + (held[2] + held[3]))


def cell_step(sums, y, rest, mob):
    held, inverse = clip_step(sums, y)
    total = [rest[i] + mob * sums[3 + i] for i in range(2)]
    scaled = LAM * inverse
    q = [v * scaled for v in held]
    square = [v * v for v in q]
    h = [square[a] * (1.5 * LAM - q[a]) for a in range(4)]
    shared = BACK * ((h[0] + h[1]) + (h[2] + 3.5 * h[3]))
    u = [(total[i] - shared) - (7.0 * BACK) * h[i] for i in range(2)]
    both = u[0] + u[1]
    third = both * (1.0 / 7.0) + TILT
    pull = [third + u[0], third + u[1], third, 0.5 * both]
    well = OWN - ((square[0] + square[1]) + (square[2] + square[3]))
    local = [q[a] * ((well + square[a]) + pull[a] * (LAM - q[a])) for a in range(4)]
    mean = 0.25 * ((local[0] + local[1]) + (local[2] + local[3])) - 0.07 / BETA
    y = [BETA * (local[a] - mean) for a in range(3)]
    mob = 0.0075 + (0.1425 / LAM) * q[3]
    six = 6.0 * mob
    rest = [total[i] - six * u[i] for i in range(2)]
    return q[:3] + u + y + rest + [mob]


def last_step(sums, y, rest, mob):
    held, inverse = clip_step(sums, y)
    p = [v * inverse for v in held]
    h = [v * v * (1.5 - v) for v in p]
    shared = 0.2 * ((h[0] + h[1]) + (h[2] + 3.5 * h[3]))
    total = [(rest[i] + mob * sums[3 + i]) * (1.0 / MU) for i in range(2)]
    return p, [(total[i] - shared) - 1.4 * h[i] for i in range(2)]


def lanes():
    return lax.broadcasted_iota(jnp.int32, (8, 128), 1)


def main_sums(state, near, row, low, at_left, at_right):
    slot, group = (row // GROUPS, row % GROUPS) if isinstance(row, int) else (lax.div(row, GROUPS), lax.rem(row, GROUPS))
    turn = 128 - (SLOT * slot + HALF // 2 + 1)
    sums = []
    for f in range(MOVING):
        v = state[f, row, pl.ds(low, 8), :]
        edge = pltpu.roll(near[f, group, pl.ds(low, 8), :], turn, 1)
        right = pltpu.roll(jnp.where(at_left, edge, v), 127, 1)
        left = pltpu.roll(jnp.where(at_right, edge, v), 1, 1)
        grow = state[f, row, pl.ds(low + 1, 8), :] + state[f, row, pl.ds(low - 1, 8), :]
        side = state[f, row + 1, pl.ds(low, 8), :] + state[f, row - 1, pl.ds(low, 8), :]
        sums.append((grow + side) + (right + left))
    return sums


def center(state, row, low):
    y = [state[MOVING + a, row, pl.ds(low, 8), :] for a in range(3)]
    rest = [state[MOVING + 3 + i, row, pl.ds(low, 8), :] for i in range(2)]
    return y, rest, state[FIELDS - 1, row, pl.ds(low, 8), :]


def near_of(v, swap):
    return jnp.where(swap, pltpu.roll(v, 128 - (HALF - 1), 1), v)


def front_kernel(
    plan, mesh_shape, levels, lab_hbm, pot_hbm, codes_hbm, table_hbm, even, even_near,
    lab, pot, codes, table, lab_up, pot_up, raw, pack, strip, odd, odd_near, even_strip, odd_strip,
    in_sems, g_send, g_recv, y_send, y_recv, z_send, z_recv,
):
    g, y, z = lax.axis_index("grow"), lax.axis_index("gy"), lax.axis_index("gz")
    count_g, count_y, count_z = mesh_shape
    rows, tall, planes, shift = plan.rows, plan.tall, plan.planes, plan.shift
    has_below, has_above = g > 0, g < count_g - 1
    is_first, is_last = g == 0, g == count_g - 1
    y_up, y_down = lax.rem(y + 1, count_y), lax.rem(y + count_y - 1, count_y)
    z_other = lax.rem(z + 1, count_z)
    chunks = plan.chunks
    own_chunks = (planes - plan.low) // 8
    lead = (planes - plan.low) % 8

    loads = [
        pltpu.make_async_copy(lab_hbm, lab, in_sems.at[0]),
        pltpu.make_async_copy(pot_hbm, pot, in_sems.at[1]),
    ]
    melt_loads = [
        pltpu.make_async_copy(codes_hbm, codes, in_sems.at[2]),
        pltpu.make_async_copy(table_hbm, table, in_sems.at[3]),
    ]
    for copy in loads:
        copy.start()

    @pl.when(is_last)
    def _():
        for copy in melt_loads:
            copy.start()

    barrier = pltpu.get_barrier_semaphore()

    def greet(target):
        pl.semaphore_signal(barrier, inc=1, device_id=target, device_id_type=MESH)

    @pl.when(has_below)
    def _():
        greet((g - 1, y, z))

    @pl.when(has_above)
    def _():
        greet((g + 1, y, z))

    greet((g, y_up, z))
    greet((g, y_down, z))
    greet((g, y, z_other))

    splits = [0] + list(range(8 - lead, plan.above - 1, 8)) + [plan.above]
    pieces = len(splits) - 1

    def g_copies(piece):
        begin, end = splits[piece], splits[piece + 1]
        src, dst = pl.ds(begin * rows, (end - begin) * rows), pl.ds((lead + begin) * rows, (end - begin) * rows)
        copies = []
        for i in range(3):
            source, target = (lab.at[src], lab_up.at[dst]) if i == 0 else (pot.at[i - 1, src], pot_up.at[i - 1, dst])
            sem = 3 * piece + i
            copies.append(pltpu.make_async_remote_copy(
                src_ref=source, dst_ref=target, send_sem=g_send.at[sem], recv_sem=g_recv.at[sem],
                device_id=(g - 1, y, z), device_id_type=MESH))
        return copies

    def y_copies(chunk):
        copies = []
        for up in range(2):
            src, dst, target = (rows, 0, y_up) if up else (STEPS, STEPS + rows, y_down)
            sem = 2 * chunk + up
            at = pl.ds(PAD + 8 * chunk, 8)
            copies.append(pltpu.make_async_remote_copy(
                src_ref=raw.at[:, pl.ds(src, STEPS), at], dst_ref=raw.at[:, pl.ds(dst, STEPS), at],
                send_sem=y_send.at[sem], recv_sem=y_recv.at[sem],
                device_id=(g, target, z), device_id_type=MESH))
        return copies

    def z_copy(chunk):
        at = pl.ds(PAD + 8 * chunk, 8)
        return pltpu.make_async_remote_copy(
            src_ref=pack.at[:, :, at], dst_ref=strip.at[:, :, at],
            send_sem=z_send.at[chunk], recv_sem=z_recv.at[chunk],
            device_id=(g, y, z_other), device_id_type=MESH)

    def fill(labels, pots, begin, to):
        for row in range(rows):
            at = pl.ds(begin * rows + row, 8, stride=rows)
            raw[0, STEPS + row, pl.ds(to, 8)] = labels[at].astype(jnp.float32)
            for i in range(2):
                raw[1 + i, STEPS + row, pl.ds(to, 8)] = pots[i, at]

    def send_y(chunk):
        for copy in y_copies(chunk):
            copy.start()

    lane = lanes()

    def send_z(chunk):
        for copy in y_copies(chunk):
            copy.wait_recv()
        at = pl.ds(PAD + 8 * chunk, 8)

        def pack_field(i, carry):
            for group in range(GROUPS):
                packed = jnp.zeros((8, 128), jnp.float32)
                for slot in range(tall // GROUPS):
                    v = raw[i, GROUPS * slot + group, at]
                    first = SLOT * slot
                    packed = jnp.where(lane >= first, pltpu.roll(v, first + HALF // 2 + 1, 1), packed)
                    packed = jnp.where(lane >= first + HALF, pltpu.roll(v, first + HALF + HALF // 2, 1), packed)
                pack[i, group, at] = packed
            return carry

        lax.fori_loop(0, 3, pack_field, 0)
        z_copy(chunk).start()

    place = lane % SLOT
    from_other = (place < HALF // 2 + 1) | (place >= SLOT - HALF // 2 - 1)
    swap = place == HALF // 2 + 1
    at_left, at_right = lane == 0, lane == 127

    def unpack_row(state, slot, row, source, target):
        at = pl.ds(source, 8)
        new = phase_state(raw[0, row, at], [raw[1, row, at], raw[2, row, at]])
        for f in range(FIELDS):
            state[slot, f, row, pl.ds(target, 8)] = new[f]

    def unpack_strips(state, near, slot, source, target):
        at, to = pl.ds(source, 8), pl.ds(target, 8)
        for group in range(GROUPS):
            value = [jnp.where(from_other, strip[i, group, at], pack[i, group, at]) for i in range(3)]
            new = phase_state(value[0], value[1:])
            for f in range(FIELDS):
                state[slot, f, group, to] = new[f]
            for f in range(MOVING):
                near[slot, f, group, to] = near_of(new[f], swap)

    def unpack(chunk):
        to = PAD + 8 * chunk

        def body(part, carry):
            for row in range(tall // GROUPS):
                unpack_row(even, 0, tall // GROUPS * part + row, to, to)
            return carry

        lax.fori_loop(0, GROUPS, body, 0)
        unpack_strips(even_strip, even_near, 0, to, to)

    def strip_step(src, src_slot, dst, near, dst_slot, low):
        at = pl.ds(low, 8)
        for group in range(GROUPS):
            sums = []
            for f in range(MOVING):
                v = src[src_slot, f, group, at]
                up = src[src_slot, f, (group + 1) % GROUPS, at]
                down = src[src_slot, f, (group + 2) % GROUPS, at]
                if group == 0:
                    down = pltpu.roll(down, SLOT, 1)
                if group == GROUPS - 1:
                    up = pltpu.roll(up, 128 - SLOT, 1)
                total = src[src_slot, f, group, pl.ds(low + 1, 8)] + src[src_slot, f, group, pl.ds(low - 1, 8)]
                sums.append((total + (up + down)) + (pltpu.roll(v, 127, 1) + pltpu.roll(v, 1, 1)))
            new = cell_step(sums, *center(src.at[src_slot], group, low))
            for f in range(FIELDS):
                dst[dst_slot, f, group, at] = new[f]
            for f in range(MOVING):
                near[dst_slot, f, group, at] = near_of(new[f], swap)

    def row_steps(src, src_near, src_slot, dst, dst_slot, low, begin, width, count):
        def body(part, carry):
            for i in range(width):
                row = begin + width * part + i
                sums = main_sums(src.at[src_slot], src_near.at[src_slot], row, low, at_left, at_right)
                new = cell_step(sums, *center(src.at[src_slot], row, low))
                for f in range(FIELDS):
                    dst[dst_slot, f, row, pl.ds(low, 8), :] = new[f]
            return carry

        lax.fori_loop(0, count, body, 0)

    def copy_plane(state, strips, near, slot, source, target):
        src, dst = pl.ds(source, 1), pl.ds(target, 1)

        def body(row, carry):
            for f in range(MOVING):
                state[slot, f, row, dst] = state[slot, f, row, src]
            return carry

        lax.fori_loop(0, tall, body, 0)
        for group in range(GROUPS):
            for f in range(MOVING):
                strips[slot, f, group, dst] = strips[slot, f, group, src]
                near[slot, f, group, dst] = near[slot, f, group, src]

    def melt_fill(low):
        def body(row, carry):
            unpack_row(odd, 1, row, low + 1, low)
            return carry

        lax.fori_loop(STEPS_BEFORE, tall - STEPS_BEFORE, body, 0)
        unpack_strips(odd_strip, odd_near, 1, low + 1, low)

    first_plane, top_plane = plan.at(shift), plan.at(planes)
    last_plane = first_plane + planes - 1

    def stage_of(plane, step):
        return (plane - (PAD + 1 - step)) // 8

    def compute(stage):
        def two_steps(t, carry):
            step = 2 * t + 1
            low = PAD + 1 + 8 * stage - step
            top = stage_of(top_plane, STEPS_BEFORE)
            below_melt = (stage <= top) | jnp.logical_not(is_last)

            @pl.when(below_melt)
            def _():
                strip_step(even_strip, t, odd_strip, odd_near, t, low)
                row_steps(even, even_near, t, odd, t, low, step, 4, 4 - t)

            @pl.when(is_last & (t == 0) & (stage == stage_of(top_plane, 1)))
            def _():
                copy_plane(odd, odd_strip, odd_near, 0, top_plane - 1, top_plane)

            @pl.when(is_first & (t == 1) & (stage == stage_of(first_plane, 3)))
            def _():
                copy_plane(odd, odd_strip, odd_near, 1, first_plane, first_plane - 1)

            @pl.when(is_last & (t == 1) & (stage >= top))
            def _():
                melt_fill(jnp.clip(low, top_plane, top_plane + shift + 1 - 8))

            @pl.when(below_melt | (t == 1))
            def _():
                strip_step(odd_strip, t, even_strip, even_near, t + 1, low - 1)
                row_steps(odd, odd_near, t, even, t + 1, low - 1, step + 1, 5, 3 - t)

            @pl.when(is_last & (t == 0) & (stage == stage_of(top_plane, 2)))
            def _():
                copy_plane(even, even_strip, even_near, 1, top_plane - 1, top_plane)

            @pl.when(is_first & (t == 1) & (stage == stage_of(first_plane, 4)))
            def _():
                copy_plane(even, even_strip, even_near, 2, first_plane, first_plane - 1)

            @pl.when(is_last & (t == 1) & (stage == stage_of(last_plane, 4)))
            def _():
                copy_plane(even, even_strip, even_near, 2, last_plane, last_plane + 1)

            return carry

        lax.fori_loop(0, 2, two_steps, 0)

    for copy in loads:
        copy.wait()

    def fill_own(chunk, carry):
        fill(lab, pot, plan.low - PAD + 8 * chunk, 8 * chunk)
        return carry

    lax.fori_loop(0, own_chunks + 1, fill_own, 0)
    tail = pl.ds((planes - lead) * rows, lead * rows)
    lab_up[0 : lead * rows] = lab[tail]
    for i in range(2):
        pot_up[i, 0 : lead * rows] = pot[i, tail]

    @pl.when(is_last)
    def _():
        for copy in melt_loads:
            copy.wait()
        plane = pl.ds((planes - 1) * rows, rows)
        at = pl.ds(lead * rows, rows)
        lab_up[at] = lab[plane]
        for i in range(2):
            pot_up[i, at] = pot[i, plane]

        def melt_plane(k, carry):
            code = codes[pl.ds(pl.multiple_of(jnp.minimum(k, shift - 1) * rows, rows), rows)]
            at = pl.ds(pl.multiple_of((lead + 1 + k) * rows, rows), rows)
            lab_up[at] = jnp.full((rows, 128), 3, jnp.int32)
            for i in range(2):
                value = jnp.zeros((rows, 128), jnp.float32)
                for level in range(levels):
                    value = jnp.where(code == level, table[i, level], value)
                pot_up[i, at] = value
            return carry

        lax.fori_loop(0, plan.above - 1, melt_plane, 0)

    pl.semaphore_wait(barrier, 3 + has_below.astype(jnp.int32) + has_above.astype(jnp.int32))

    @pl.when(has_below)
    def _():
        for piece in range(pieces):
            for copy in g_copies(piece):
                copy.start()

    def first_sends(chunk, carry):
        send_y(chunk)
        return carry

    lax.fori_loop(0, own_chunks, first_sends, 0)

    def beat(it, carry):
        @pl.when(it < chunks)
        def _():
            send_z(it)

        for piece in range(pieces):
            @pl.when(has_above & (it == piece))
            def _():
                for copy in g_copies(piece):
                    copy.wait_recv()

        @pl.when(it < pieces)
        def _():
            fill(lab_up, pot_up, 8 * it, PAD + 8 * (own_chunks + it))
            send_y(own_chunks + it)

        @pl.when(it == pieces)
        def _():
            fill(lab_up, pot_up, 8 * it, PAD + 8 * (own_chunks + it))

        @pl.when((it >= 1) & (it <= chunks))
        def _():
            z_copy(it - 1).wait_recv()

        unpack(it - 1)

        @pl.when(it >= 2)
        def _():
            compute(it - 2)

        return carry

    lax.fori_loop(0, chunks + 2, beat, 0)

    def drain(chunk, carry):
        for copy in y_copies(chunk):
            copy.wait_send()
        z_copy(chunk).wait_send()
        return carry

    lax.fori_loop(0, chunks, drain, 0)

    @pl.when(has_below)
    def _():
        for piece in range(pieces):
            for copy in g_copies(piece):
                copy.wait_send()


def last_kernel(plan, state, near, phases, potentials, p_out, m_out, sems):
    rows, planes = plan.rows, plan.planes
    at_left, at_right = lanes() == 0, lanes() == 127
    slot = STEPS // 2

    def out_copies(tile):
        at = pl.ds(8 * tile * rows, 8 * rows)
        return [
            pltpu.make_async_copy(src.at[:, at], dst.at[:, at], sems.at[2 * tile + i])
            for i, (src, dst) in enumerate(((p_out, phases), (m_out, potentials)))
        ]

    def body(tile, carry):
        low = plan.at(plan.shift) + 8 * tile
        for row in range(rows):
            sums = main_sums(state.at[slot], near.at[slot], STEPS + row, low, at_left, at_right)
            p, m = last_step(sums, *center(state.at[slot], STEPS + row, low))
            at = pl.ds(8 * tile * rows + row, 8, stride=rows)
            for f in range(4):
                p_out[f, at, :] = p[f]
            for i in range(2):
                m_out[i, at, :] = m[i]
        for copy in out_copies(tile):
            copy.start()
        return carry

    lax.fori_loop(0, planes // 8, body, 0)
    for tile in range(planes // 8):
        for copy in out_copies(tile):
            copy.wait()


def on_device(mesh_shape, labels, potential, melt_codes, melt_table):
    planes, rows, width = labels.shape
    shift, levels = melt_codes.shape[0], melt_table.shape[1]
    plan = Plan(planes, rows, shift)
    flat = planes * rows
    vmem = pl.BlockSpec(memory_space=pltpu.VMEM)
    hbm = pl.BlockSpec(memory_space=pltpu.HBM)
    f32 = jnp.float32
    dma = pltpu.SemaphoreType.DMA
    deep, tall, chunks = plan.deep, plan.tall, plan.chunks
    evens, odds = STEPS // 2 + 1, STEPS // 2
    upper = 8 * (plan.above // 8 + 2) * rows
    state, near = pl.pallas_call(
        functools.partial(front_kernel, plan, mesh_shape, levels),
        out_shape=(
            pltpu.VMEM((evens, FIELDS, tall, deep, width), f32),
            pltpu.VMEM((evens, MOVING, GROUPS, deep, width), f32),
        ),
        in_specs=[hbm, hbm, hbm, hbm],
        out_specs=(vmem, vmem),
        scratch_shapes=[
            pltpu.VMEM((flat, width), jnp.int32),
            pltpu.VMEM((2, flat, width), f32),
            pltpu.VMEM((shift * rows, width), jnp.int32),
            pltpu.SMEM((2, levels), f32),
            pltpu.VMEM((upper, width), jnp.int32),
            pltpu.VMEM((2, upper, width), f32),
            pltpu.VMEM((3, tall, deep, width), f32),
            pltpu.VMEM((3, GROUPS, deep, width), f32),
            pltpu.VMEM((3, GROUPS, deep, width), f32),
            pltpu.VMEM((odds, FIELDS, tall, deep, width), f32),
            pltpu.VMEM((odds, MOVING, GROUPS, deep, width), f32),
            pltpu.VMEM((evens, FIELDS, GROUPS, deep, width), f32),
            pltpu.VMEM((odds, FIELDS, GROUPS, deep, width), f32),
            dma((4,)), dma((3 * chunks,)), dma((3 * chunks,)),
            dma((2 * chunks,)), dma((2 * chunks,)), dma((chunks,)), dma((chunks,)),
        ],
        compiler_params=pltpu.CompilerParams(collective_id=0, has_side_effects=True, vmem_limit_bytes=40 << 20),
        name="front",
    )(labels.reshape(flat, width), potential.reshape(2, flat, width), melt_codes.reshape(shift * rows, width), melt_table)
    state, near = (pltpu.with_memory_space_constraint(v, pltpu.VMEM) for v in (state, near))
    phases, potentials = pl.pallas_call(
        functools.partial(last_kernel, plan),
        out_shape=(
            jax.ShapeDtypeStruct((4, flat, width), f32),
            jax.ShapeDtypeStruct((2, flat, width), f32),
        ),
        in_specs=[vmem, vmem],
        out_specs=(hbm, hbm),
        scratch_shapes=[
            pltpu.VMEM((4, flat, width), f32),
            pltpu.VMEM((2, flat, width), f32),
            dma((2 * (planes // 8),)),
        ],
        compiler_params=pltpu.CompilerParams(vmem_limit_bytes=8 << 20),
        name="last",
    )(state, near)
    return phases.reshape(4, planes, rows, width), potentials.reshape(2, planes, rows, width)


def solution(mesh):
    mesh_shape = tuple(mesh.shape[axis] for axis in ("grow", "gy", "gz"))
    return jax.shard_map(
        functools.partial(on_device, mesh_shape),
        mesh=mesh,
        in_specs=(P("grow", "gy", "gz"), P(None, "grow", "gy", "gz"), P(None, "gy", "gz"), P()),
        out_specs=(P(None, "grow", "gy", "gz"), P(None, "grow", "gy", "gz")),
        check_vma=False,
    )
```

```python
import functools

import jax
import jax.numpy as jnp
from jax import lax
from jax.experimental import pallas as pl
from jax.experimental.pallas import tpu as pltpu
from jax.sharding import PartitionSpec as P

STEPS_BEFORE = 3
STEPS_AFTER = 2
STEPS = STEPS_BEFORE + STEPS_AFTER
HALF = 9
SLOT = 2 * HALF
GROUPS = 3
BATCH = 6
FIELDS = 11
MOVING = 5
VMEM_BYTES = 67043328
MESH = pl.DeviceIdType.MESH

LAM = 0.12
BETA = 5.0 / LAM**2
MU = 17.5 / (LAM * BETA)
OWN = (1.0 / LAM - 6.0) / BETA
TILT = 1.25 / (LAM * BETA)
BACK = 0.2 * MU / LAM**3


class Plan:
    def __init__(self, planes, rows, shift):
        self.planes, self.rows, self.shift = planes, rows, shift
        self.base = shift - STEPS + 2 - 8
        self.chunks = planes // 8 + 2
        self.stages = self.chunks - 1
        self.deep = 8 * self.chunks
        self.above = shift + STEPS
        self.tall = rows + 2 * STEPS
        self.own_chunks, self.lead = divmod(planes - self.base, 8)
        self.pieces = self.chunks - self.own_chunks

    def at(self, plane):
        return plane - self.base

    def low(self, stage, step):
        return 8 + 8 * stage - step


def phase_state(label, pot):
    q = [jnp.where(label == float(a), LAM, 0.0) for a in range(3)]
    y = [jnp.where(label == float(a), LAM * BETA * OWN, 0.0) for a in range(3)]
    liquid = label == 3.0
    mob = jnp.where(liquid, 0.15, 0.0075)
    u = [MU * v for v in pot]
    comp = [jnp.where(liquid, 0.35 * MU, jnp.where(label == float(i), 0.8 * MU, 0.1 * MU)) for i in range(2)]
    rest = [(u[i] + comp[i]) - (6.0 * mob) * u[i] for i in range(2)]
    return q + u + y + rest + [mob]


def clip_step(sums, y):
    x = [sums[a] + y[a] for a in range(3)]
    x.append(1.0 - (x[0] + x[1] + x[2]))
    held = [jnp.clip(v, 0.0, 1.0) for v in x]
    return held, 1.0 / ((held[0] + held[1]) + (held[2] + held[3]))


def cell_step(sums, y, rest, mob, tick=lambda: None):
    held, inverse = clip_step(sums, y)
    tick()
    total = [rest[i] + mob * sums[3 + i] for i in range(2)]
    tick()
    scaled = LAM * inverse
    q = [v * scaled for v in held]
    tick()
    square = [v * v for v in q]
    tick()
    h = [square[a] * (1.5 * LAM - q[a]) for a in range(4)]
    tick()
    shared = BACK * ((h[0] + h[1]) + (h[2] + 3.5 * h[3]))
    tick()
    u = [(total[i] - shared) - (7.0 * BACK) * h[i] for i in range(2)]
    tick()
    both = u[0] + u[1]
    well = OWN - ((square[0] + square[1]) + (square[2] + square[3]))
    tick()
    third = both * (1.0 / 7.0) + TILT
    pull = [third + u[0], third + u[1], third, 0.5 * both]
    tick()
    mob = 0.0075 + (0.1425 / LAM) * q[3]
    six = 6.0 * mob
    rest = [total[i] - six * u[i] for i in range(2)]
    tick()
    local = []
    for a in range(4):
        local.append(q[a] * ((well + square[a]) + pull[a] * (LAM - q[a])))
        tick()
    mean = 0.25 * ((local[0] + local[1]) + (local[2] + local[3])) - 0.07 / BETA
    tick()
    y = [BETA * (local[a] - mean) for a in range(3)]
    tick()
    return q[:3] + u + y + rest + [mob]


def last_step(sums, y, rest, mob):
    held, inverse = clip_step(sums, y)
    p = [v * inverse for v in held]
    h = [v * v * (1.5 - v) for v in p]
    shared = 0.2 * ((h[0] + h[1]) + (h[2] + 3.5 * h[3]))
    total = [(rest[i] + mob * sums[3 + i]) * (1.0 / MU) for i in range(2)]
    return p, [(total[i] - shared) - 1.4 * h[i] for i in range(2)]


def lanes():
    return lax.broadcasted_iota(jnp.int32, (8, 128), 1)


def side_sums(state, near, row, low, at_left, at_right, first=0):
    slot = (row + first) // GROUPS if isinstance(row, int) else lax.shift_right_logical(row * 43, 7)
    group = row + first - GROUPS * slot
    turn = 128 - (SLOT * slot + HALF // 2 + 1)
    sums = []
    for f in range(MOVING):
        v = state[f, row, pl.ds(low, 8), :]
        edge = pltpu.roll(near[f, group, pl.ds(low, 8), :], turn, 1)
        right = pltpu.roll(jnp.where(at_left, edge, v), 127, 1)
        left = pltpu.roll(jnp.where(at_right, edge, v), 1, 1)
        sums.append(right + left)
    return sums


def main_sums(state, row, low, sides):
    sums = []
    for f in range(MOVING):
        grow = state[f, row, pl.ds(low + 1, 8), :] + state[f, row, pl.ds(low - 1, 8), :]
        side = state[f, row + 1, pl.ds(low, 8), :] + state[f, row - 1, pl.ds(low, 8), :]
        sums.append((grow + side) + sides[f])
    return sums


def center(state, row, low):
    y = [state[MOVING + a, row, pl.ds(low, 8), :] for a in range(3)]
    rest = [state[MOVING + 3 + i, row, pl.ds(low, 8), :] for i in range(2)]
    return y, rest, state[FIELDS - 1, row, pl.ds(low, 8), :]


def near_of(v, swap):
    return jnp.where(swap, pltpu.roll(v, 128 - (HALF - 1), 1), v)


def front_kernel(
    plan, mesh_shape, levels, lab_hbm, pot_hbm, codes_hbm, table_hbm, out_state, out_near,
    lab, pot, codes, table, lab_up, pot_up, raw, pack, strip, even, odd, even_near, odd_near, even_strip, odd_strip,
    in_sems, g_send, g_recv, y_send, y_recv, z_send, z_recv,
):
    g, y, z = lax.axis_index("grow"), lax.axis_index("gy"), lax.axis_index("gz")
    count_g, count_y, count_z = mesh_shape
    rows, tall, planes, shift = plan.rows, plan.tall, plan.planes, plan.shift
    has_below, has_above = g > 0, g < count_g - 1
    is_first, is_last = g == 0, g == count_g - 1
    y_up, y_down = lax.rem(y + 1, count_y), lax.rem(y + count_y - 1, count_y)
    z_other = lax.rem(z + 1, count_z)
    chunks = plan.chunks
    own_chunks, lead, pieces = plan.own_chunks, plan.lead, plan.pieces

    loads = [
        pltpu.make_async_copy(lab_hbm, lab, in_sems.at[0]),
        pltpu.make_async_copy(pot_hbm, pot, in_sems.at[1]),
    ]
    melt_loads = [
        pltpu.make_async_copy(codes_hbm, codes, in_sems.at[2]),
        pltpu.make_async_copy(table_hbm, table, in_sems.at[3]),
    ]
    for copy in loads:
        copy.start()

    @pl.when(is_last)
    def _():
        for copy in melt_loads:
            copy.start()

    barrier = pltpu.get_barrier_semaphore()

    def greet(target):
        pl.semaphore_signal(barrier, inc=1, device_id=target, device_id_type=MESH)

    @pl.when(has_below)
    def _():
        greet((g - 1, y, z))

    @pl.when(has_above)
    def _():
        greet((g + 1, y, z))

    greet((g, y_up, z))
    greet((g, y_down, z))
    greet((g, y, z_other))

    splits = [max(8 * piece - lead, 0) for piece in range(pieces + 1)]

    def g_copies(piece):
        begin, end = splits[piece], splits[piece + 1]
        src, dst = pl.ds(begin * rows, (end - begin) * rows), pl.ds((lead + begin) * rows, (end - begin) * rows)
        copies = []
        for i in range(3):
            source, target = (lab_hbm.at[src], lab_up.at[dst]) if i == 0 else (pot_hbm.at[i - 1, src], pot_up.at[i - 1, dst])
            sem = 3 * piece + i
            copies.append(pltpu.make_async_remote_copy(
                src_ref=source, dst_ref=target, send_sem=g_send.at[sem], recv_sem=g_recv.at[sem],
                device_id=(g - 1, y, z), device_id_type=MESH))
        return copies

    def y_copies(chunk):
        copies = []
        for up in range(2):
            src, dst, target = (rows, 0, y_up) if up else (STEPS, STEPS + rows, y_down)
            sem = 2 * chunk + up
            at = pl.ds(8 * chunk, 8)
            copies.append(pltpu.make_async_remote_copy(
                src_ref=raw.at[:, pl.ds(src, STEPS), at], dst_ref=raw.at[:, pl.ds(dst, STEPS), at],
                send_sem=y_send.at[sem], recv_sem=y_recv.at[sem],
                device_id=(g, target, z), device_id_type=MESH))
        return copies

    def z_copy(chunk):
        at = pl.ds(8 * chunk, 8)
        return pltpu.make_async_remote_copy(
            src_ref=pack.at[:, :, at], dst_ref=strip.at[:, :, at],
            send_sem=z_send.at[chunk], recv_sem=z_recv.at[chunk],
            device_id=(g, y, z_other), device_id_type=MESH)

    def fill(labels, pots, begin, to):
        for row in range(rows):
            at = pl.ds(begin * rows + row, 8, stride=rows)
            raw[0, STEPS + row, pl.ds(to, 8)] = labels[at].astype(jnp.float32)
            for i in range(2):
                raw[1 + i, STEPS + row, pl.ds(to, 8)] = pots[i, at]

    def send_y(chunk):
        for copy in y_copies(chunk):
            copy.start()

    lane = lanes()

    def send_z(chunk):
        for copy in y_copies(chunk):
            copy.wait_recv()
        at = pl.ds(8 * chunk, 8)

        def pack_field(i, carry):
            for group in range(GROUPS):
                packed = jnp.zeros((8, 128), jnp.float32)
                for slot in range(tall // GROUPS):
                    v = raw[i, GROUPS * slot + group, at]
                    first = SLOT * slot
                    packed = jnp.where(lane >= first, pltpu.roll(v, first + HALF // 2 + 1, 1), packed)
                    packed = jnp.where(lane >= first + HALF, pltpu.roll(v, first + HALF + HALF // 2, 1), packed)
                pack[i, group, at] = packed
            return carry

        lax.fori_loop(0, 3, pack_field, 0)
        z_copy(chunk).start()

    place = lane % SLOT
    from_other = (place < HALF // 2 + 1) | (place >= SLOT - HALF // 2 - 1)
    swap = place == HALF // 2 + 1
    at_left, at_right = lane == 0, lane == 127

    def unpack_row(state, slot, row, source, target):
        at = pl.ds(source, 8)
        new = phase_state(raw[0, row, at], [raw[1, row, at], raw[2, row, at]])
        for f in range(FIELDS):
            state[slot, f, row, pl.ds(target, 8)] = new[f]

    def unpack_strips(state, near, slot, source, target):
        at, to = pl.ds(source, 8), pl.ds(target, 8)
        for group in range(GROUPS):
            value = [jnp.where(from_other, strip[i, group, at], pack[i, group, at]) for i in range(3)]
            new = phase_state(value[0], value[1:])
            for f in range(FIELDS):
                state[slot, f, group, to] = new[f]
            for f in range(MOVING):
                near[slot, f, group, to] = near_of(new[f], swap)

    def unpack(chunk):
        to = 8 * chunk

        def body(part, carry):
            for row in range(tall // GROUPS):
                unpack_row(even, 0, tall // GROUPS * part + row, to, to)
            return carry

        lax.fori_loop(0, GROUPS, body, 0)
        unpack_strips(even_strip, even_near, 0, to, to)

    def strip_step(src, src_slot, dst, near, dst_slot, low, tick):
        at = pl.ds(low, 8)
        groups = range(GROUPS)
        sums = []
        for f in range(MOVING):
            v = src[src_slot, f, :, at]
            part = [src[src_slot, f, group, at] for group in groups]
            up = jnp.stack([part[1], part[2], pltpu.roll(part[0], 128 - SLOT, 1)])
            down = jnp.stack([pltpu.roll(part[2], SLOT, 1), part[0], part[1]])
            total = src[src_slot, f, :, pl.ds(low + 1, 8)] + src[src_slot, f, :, pl.ds(low - 1, 8)]
            sums.append((total + (up + down)) + (pltpu.roll(v, 127, 2) + pltpu.roll(v, 1, 2)))
        y = [src[src_slot, MOVING + a, :, at] for a in range(3)]
        rest = [src[src_slot, MOVING + 3 + i, :, at] for i in range(2)]
        new = cell_step(sums, y, rest, src[src_slot, FIELDS - 1, :, at], tick)
        for f in range(FIELDS):
            dst[dst_slot, f, :, at] = new[f]
        for f in range(MOVING):
            near[dst_slot, f, :, at] = jnp.where(swap, pltpu.roll(new[f], 128 - (HALF - 1), 2), new[f])

    def side_steps(state, near, first, count, low, result):
        v, edge, ends = {}, {}, {}

        def near_rolls(f):
            rolled = []
            for i in range(count):
                slot, group = divmod(first + i, GROUPS)
                rolled.append(pltpu.roll(near[f, group, pl.ds(low, 8), :], 128 - (SLOT * slot + HALF // 2 + 1), 1))
            edge[f] = jnp.stack(rolled)
            v[f] = state[f, first : first + count, pl.ds(low, 8), :]

        def z_rolls(f):
            right = pltpu.roll(jnp.where(at_left, edge[f], v[f]), 127, 2)
            left = pltpu.roll(jnp.where(at_right, edge[f], v[f]), 1, 2)
            ends[f] = (right, left)

        def add(f):
            result[f] = ends[f][0] + ends[f][1]

        pieces = []
        for f in range(MOVING + 2):
            if f < MOVING:
                pieces.append(functools.partial(near_rolls, f))
            if f >= 1 and f - 1 < MOVING:
                pieces.append(functools.partial(z_rolls, f - 1))
            if f >= 2:
                pieces.append(functools.partial(add, f - 2))
        return pieces

    def row_steps(src, src_near, src_slot, dst, dst_slot, low, begin, total, strips_first):
        state, near = src.at[src_slot], src_near.at[src_slot]
        sizes = [BATCH] * (total // BATCH) + ([total % BATCH] if total % BATCH else [])
        at = pl.ds(low, 8)
        ready = {}
        pending = side_steps(state, near, begin, sizes[0], low, ready)

        def tick():
            if pending:
                pending.pop(0)()

        def flush():
            while pending:
                pending.pop(0)()

        strips_first(tick)
        flush()
        row = begin
        for k, size in enumerate(sizes):
            around, ready = ready, {}
            if k + 1 < len(sizes):
                pending = side_steps(state, near, row + size, sizes[k + 1], low, ready)

            def rows_of(f, shift=0, step=0):
                return state[f, row + shift : row + shift + size, pl.ds(low + step, 8), :]

            sums = []
            for f in range(MOVING):
                grow = rows_of(f, 0, 1) + rows_of(f, 0, -1)
                side = rows_of(f, 1) + rows_of(f, -1)
                sums.append((grow + side) + around[f])
                tick()
            y = [rows_of(MOVING + a) for a in range(3)]
            rest = [rows_of(MOVING + 3 + i) for i in range(2)]
            new = cell_step(sums, y, rest, rows_of(FIELDS - 1), tick)
            flush()
            for f in range(FIELDS):
                dst[dst_slot, f, row : row + size, at, :] = new[f]
            row += size

    def copy_plane(state, strips, near, slot, source, target):
        src, dst = pl.ds(source, 1), pl.ds(target, 1)

        def body(row, carry):
            for f in range(MOVING):
                state[slot, f, row, dst] = state[slot, f, row, src]
            return carry

        lax.fori_loop(0, tall, body, 0)
        for group in range(GROUPS):
            for f in range(MOVING):
                strips[slot, f, group, dst] = strips[slot, f, group, src]
                near[slot, f, group, dst] = near[slot, f, group, src]

    first_plane, top_plane = plan.at(shift), plan.at(planes)
    last_plane = first_plane + planes - 1
    place_up = lax.broadcasted_iota(jnp.int32, (8, 128), 0)

    def melt_fill(stage):
        source, target = 8 * stage + 8, 8 * stage + 7
        melt = place_up >= top_plane - target
        at, to = pl.ds(source, 8), pl.ds(target, 8)

        def body(row, carry):
            new = phase_state(raw[0, row, at], [raw[1, row, at], raw[2, row, at]])
            for f in range(FIELDS):
                pltpu.store(odd.at[1, f, row, to], new[f], mask=melt)
            return carry

        lax.fori_loop(STEPS_BEFORE, tall - STEPS_BEFORE, body, 0)
        for group in range(GROUPS):
            value = [jnp.where(from_other, strip[i, group, at], pack[i, group, at]) for i in range(3)]
            new = phase_state(value[0], value[1:])
            for f in range(FIELDS):
                pltpu.store(odd_strip.at[1, f, group, to], new[f], mask=melt)
            for f in range(MOVING):
                pltpu.store(odd_near.at[1, f, group, to], near_of(new[f], swap), mask=melt)

    def stage_of(plane, step):
        return (plane - plan.low(0, step)) // 8

    def compute(stage):
        top = stage_of(top_plane, STEPS_BEFORE)
        below_melt = (stage <= top) | jnp.logical_not(is_last)

        def advance(step):
            t = step // 2
            low = plan.low(stage, step)
            count = tall - 2 * step
            if step % 2:
                strips = functools.partial(strip_step, even_strip, t, odd_strip, odd_near, t, low)
                row_steps(even, even_near, t, odd, t, low, step, count, strips)
            else:
                strips = functools.partial(strip_step, odd_strip, t - 1, even_strip, even_near, t, low)
                row_steps(odd, odd_near, t - 1, even, t, low, step, count, strips)

        for step in range(1, STEPS):
            out = (odd, odd_strip, odd_near, step // 2) if step % 2 else (even, even_strip, even_near, step // 2)

            if step <= STEPS_BEFORE:
                pl.when(below_melt)(functools.partial(advance, step))
            else:
                advance(step)

            if step < STEPS_BEFORE:
                @pl.when(is_last & (stage == stage_of(top_plane, step)))
                def _():
                    copy_plane(*out, top_plane - 1, top_plane)
            else:
                @pl.when(is_first & (stage == stage_of(first_plane, step)))
                def _():
                    copy_plane(*out, first_plane, first_plane - 1)

            if step == STEPS_BEFORE:
                @pl.when(is_last & (stage >= top))
                def _():
                    melt_fill(stage)

            if step == STEPS - 1:
                @pl.when(is_last & (stage == stage_of(last_plane, step)))
                def _():
                    copy_plane(*out, last_plane, last_plane + 1)

        at = pl.ds(plan.low(stage, STEPS - 1), 8)
        for f in range(FIELDS):
            for row in range(rows + 2):
                if f < MOVING or 0 < row <= rows:
                    out_state[f, row, at] = even[STEPS // 2, f, STEPS - 1 + row, at]
        for f in range(MOVING):
            for group in range(GROUPS):
                out_near[f, group, at] = even_near[STEPS // 2, f, group, at]

    pl.semaphore_wait(barrier, 3 + has_below.astype(jnp.int32) + has_above.astype(jnp.int32))

    @pl.when(has_below)
    def _():
        for piece in range(pieces):
            for copy in g_copies(piece):
                copy.start()

    for copy in loads:
        copy.wait()

    def fill_own(chunk, carry):
        fill(lab, pot, plan.base + 8 * chunk, 8 * chunk)
        send_y(chunk)
        return carry

    lax.fori_loop(0, own_chunks, fill_own, 0)
    tail = pl.ds((planes - lead) * rows, lead * rows)
    lab_up[0 : lead * rows] = lab[tail]
    for i in range(2):
        pot_up[i, 0 : lead * rows] = pot[i, tail]

    @pl.when(is_last)
    def _():
        for copy in melt_loads:
            copy.wait()
        plane = pl.ds((planes - 1) * rows, rows)
        at = pl.ds(lead * rows, rows)
        lab_up[at] = lab[plane]
        for i in range(2):
            pot_up[i, at] = pot[i, plane]

        def melt_plane(k, carry):
            code = codes[pl.ds(pl.multiple_of(jnp.minimum(k, shift - 1) * rows, rows), rows)]
            at = pl.ds(pl.multiple_of((lead + 1 + k) * rows, rows), rows)
            lab_up[at] = jnp.full((rows, 128), 3, jnp.int32)
            for i in range(2):
                value = jnp.zeros((rows, 128), jnp.float32)
                for level in range(levels):
                    value = jnp.where(code == level, table[i, level], value)
                pot_up[i, at] = value
            return carry

        lax.fori_loop(0, 8 * pieces - lead - 1, melt_plane, 0)

    def beat(it, carry):
        @pl.when(it < chunks)
        def _():
            send_z(it)

        for piece in range(pieces):
            @pl.when(has_above & (it == piece))
            def _():
                for copy in g_copies(piece):
                    copy.wait_recv()

        @pl.when(it < pieces)
        def _():
            fill(lab_up, pot_up, 8 * it, 8 * (own_chunks + it))
            send_y(own_chunks + it)

        @pl.when(it >= 1)
        def _():
            z_copy(it - 1).wait_recv()
            unpack(it - 1)

        @pl.when(it >= 2)
        def _():
            compute(it - 2)

        return carry

    lax.fori_loop(0, plan.stages + 2, beat, 0)

    def drain(chunk, carry):
        for copy in y_copies(chunk):
            copy.wait_send()
        z_copy(chunk).wait_send()
        return carry

    lax.fori_loop(0, chunks, drain, 0)

    @pl.when(has_below)
    def _():
        for piece in range(pieces):
            for copy in g_copies(piece):
                copy.wait_send()


def last_kernel(plan, state, near, phases, potentials, p_out, m_out, sems):
    rows, planes = plan.rows, plan.planes
    at_left, at_right = lanes() == 0, lanes() == 127
    begin, tiles = plan.at(plan.shift), planes // 8

    def out_copies(tile):
        at = pl.ds(8 * tile * rows, 8 * rows)
        return [
            pltpu.make_async_copy(src.at[:, at], dst.at[:, at], sems.at[2 * tile + i])
            for i, (src, dst) in enumerate(((p_out, phases), (m_out, potentials)))
        ]

    def body(tile, carry):
        low = begin + 8 * tile
        for row in range(1, rows + 1):
            sums = main_sums(state, row, low, side_sums(state, near, row, low, at_left, at_right, STEPS - 1))
            p, m = last_step(sums, *center(state, row, low))
            at = pl.ds(8 * tile * rows + row - 1, 8, stride=rows)
            for f in range(4):
                p_out[f, at, :] = p[f]
            for i in range(2):
                m_out[i, at, :] = m[i]
        for copy in out_copies(tile):
            copy.start()
        return carry

    lax.fori_loop(0, tiles, body, 0)
    for tile in range(tiles):
        for copy in out_copies(tile):
            copy.wait()


def on_device(mesh_shape, labels, potential, melt_codes, melt_table):
    planes, rows, width = labels.shape
    shift, levels = melt_codes.shape[0], melt_table.shape[1]
    plan = Plan(planes, rows, shift)
    flat = planes * rows
    vmem = pl.BlockSpec(memory_space=pltpu.VMEM)
    hbm = pl.BlockSpec(memory_space=pltpu.HBM)
    f32 = jnp.float32
    dma = pltpu.SemaphoreType.DMA
    deep, tall, chunks = plan.deep, plan.tall, plan.chunks
    evens, odds = STEPS // 2 + 1, STEPS // 2
    upper = 8 * plan.pieces * rows
    kept = (FIELDS * (rows + 2) + MOVING * GROUPS) * deep * width * 4
    state, near = pl.pallas_call(
        functools.partial(front_kernel, plan, mesh_shape, levels),
        out_shape=(
            pltpu.VMEM((FIELDS, rows + 2, deep, width), f32),
            pltpu.VMEM((MOVING, GROUPS, deep, width), f32),
        ),
        in_specs=[hbm, hbm, hbm, hbm],
        out_specs=(vmem, vmem),
        scratch_shapes=[
            pltpu.VMEM((flat, width), jnp.int32),
            pltpu.VMEM((2, flat, width), f32),
            pltpu.VMEM((shift * rows, width), jnp.int32),
            pltpu.SMEM((2, levels), f32),
            pltpu.VMEM((upper, width), jnp.int32),
            pltpu.VMEM((2, upper, width), f32),
            pltpu.VMEM((3, tall, deep, width), f32),
            pltpu.VMEM((3, GROUPS, deep, width), f32),
            pltpu.VMEM((3, GROUPS, deep, width), f32),
            pltpu.VMEM((evens, FIELDS, tall, deep, width), f32),
            pltpu.VMEM((odds, FIELDS, tall, deep, width), f32),
            pltpu.VMEM((evens, MOVING, GROUPS, deep, width), f32),
            pltpu.VMEM((odds, MOVING, GROUPS, deep, width), f32),
            pltpu.VMEM((evens, FIELDS, GROUPS, deep, width), f32),
            pltpu.VMEM((odds, FIELDS, GROUPS, deep, width), f32),
            dma((4,)), dma((3 * chunks,)), dma((3 * chunks,)),
            dma((2 * chunks,)), dma((2 * chunks,)), dma((chunks,)), dma((chunks,)),
        ],
        compiler_params=pltpu.CompilerParams(collective_id=0, has_side_effects=True, vmem_limit_bytes=(VMEM_BYTES - kept) // 4096 * 4096),
        name="front",
    )(labels.reshape(flat, width), potential.reshape(2, flat, width), melt_codes.reshape(shift * rows, width), melt_table)
    state, near = (pltpu.with_memory_space_constraint(v, pltpu.VMEM) for v in (state, near))
    phases, potentials = pl.pallas_call(
        functools.partial(last_kernel, plan),
        out_shape=(
            jax.ShapeDtypeStruct((4, flat, width), f32),
            jax.ShapeDtypeStruct((2, flat, width), f32),
        ),
        in_specs=[vmem, vmem],
        out_specs=(hbm, hbm),
        scratch_shapes=[
            pltpu.VMEM((4, flat, width), f32),
            pltpu.VMEM((2, flat, width), f32),
            dma((2 * (planes // 8),)),
        ],
        compiler_params=pltpu.CompilerParams(vmem_limit_bytes=8 << 20),
        name="last",
    )(state, near)
    return phases.reshape(4, planes, rows, width), potentials.reshape(2, planes, rows, width)


def solution(mesh):
    mesh_shape = tuple(mesh.shape[axis] for axis in ("grow", "gy", "gz"))
    return jax.shard_map(
        functools.partial(on_device, mesh_shape),
        mesh=mesh,
        in_specs=(P("grow", "gy", "gz"), P(None, "grow", "gy", "gz"), P(None, "gy", "gz"), P()),
        out_specs=(P(None, "grow", "gy", "gz"), P(None, "grow", "gy", "gz")),
        check_vma=False,
    )
```

```python
import functools

import jax
import jax.numpy as jnp
from jax import lax
from jax.experimental import pallas as pl
from jax.experimental.pallas import tpu as pltpu
from jax.sharding import PartitionSpec as P

STEPS_BEFORE = 3
STEPS_AFTER = 2
STEPS = STEPS_BEFORE + STEPS_AFTER
HALF = 9
SLOT = 2 * HALF
GROUPS = 3
LAG = 5
BATCH = 8
FIELDS = 11
MOVING = 5
VMEM_BYTES = 67043328
MESH = pl.DeviceIdType.MESH

LAM = 0.12
BETA = 5.0 / LAM**2
MU = 17.5 / (LAM * BETA)
OWN = (1.0 / LAM - 6.0) / BETA
TILT = 1.25 / (LAM * BETA)
BACK = 0.2 * MU / LAM**3


class Plan:
    def __init__(self, planes, rows, shift):
        self.planes, self.rows, self.shift = planes, rows, shift
        self.base = shift - STEPS + 2 - 8
        self.chunks = planes // 8 + 2
        self.stages = self.chunks - 1
        self.deep = 8 * self.chunks
        self.above = shift + STEPS
        self.tall = rows + 2 * STEPS
        self.own_chunks, self.lead = divmod(planes - self.base, 8)
        self.pieces = self.chunks - self.own_chunks

    def at(self, plane):
        return plane - self.base

    def low(self, stage, step):
        return 8 + 8 * stage - step


def phase_state(label, pot):
    q = [jnp.where(label == float(a), LAM, 0.0) for a in range(3)]
    y = [jnp.where(label == float(a), LAM * BETA * OWN, 0.0) for a in range(3)]
    liquid = label == 3.0
    mob = jnp.where(liquid, 0.15, 0.0075)
    u = [MU * v for v in pot]
    comp = [jnp.where(liquid, 0.35 * MU, jnp.where(label == float(i), 0.8 * MU, 0.1 * MU)) for i in range(2)]
    rest = [(u[i] + comp[i]) - (6.0 * mob) * u[i] for i in range(2)]
    return q + u + y + rest + [mob]


def clip_step(sums, y):
    x = [sums[a] + y[a] for a in range(3)]
    x.append(1.0 - (x[0] + x[1] + x[2]))
    held = [jnp.clip(v, 0.0, 1.0) for v in x]
    return held, 1.0 / ((held[0] + held[1]) + (held[2] + held[3]))


def cell_step(sums, y, rest, mob, tick=lambda: None):
    held, inverse = clip_step(sums, y)
    tick()
    total = [rest[i] + mob * sums[3 + i] for i in range(2)]
    tick()
    scaled = LAM * inverse
    q = [v * scaled for v in held]
    tick()
    square = [v * v for v in q]
    tick()
    h = [square[a] * (1.5 * LAM - q[a]) for a in range(4)]
    tick()
    shared = BACK * ((h[0] + h[1]) + (h[2] + 3.5 * h[3]))
    tick()
    u = [(total[i] - shared) - (7.0 * BACK) * h[i] for i in range(2)]
    tick()
    both = u[0] + u[1]
    well = OWN - ((square[0] + square[1]) + (square[2] + square[3]))
    tick()
    third = both * (1.0 / 7.0) + TILT
    pull = [third + u[0], third + u[1], third, 0.5 * both]
    tick()
    mob = 0.0075 + (0.1425 / LAM) * q[3]
    six = 6.0 * mob
    rest = [total[i] - six * u[i] for i in range(2)]
    tick()
    local = []
    for a in range(4):
        local.append(q[a] * ((well + square[a]) + pull[a] * (LAM - q[a])))
        tick()
    mean = 0.25 * ((local[0] + local[1]) + (local[2] + local[3])) - 0.07 / BETA
    tick()
    y = [BETA * (local[a] - mean) for a in range(3)]
    tick()
    return q[:3] + u + y + rest + [mob]


def last_step(sums, y, rest, mob):
    held, inverse = clip_step(sums, y)
    p = [v * inverse for v in held]
    h = [v * v * (1.5 - v) for v in p]
    shared = 0.2 * ((h[0] + h[1]) + (h[2] + 3.5 * h[3]))
    total = [(rest[i] + mob * sums[3 + i]) * (1.0 / MU) for i in range(2)]
    return p, [(total[i] - shared) - 1.4 * h[i] for i in range(2)]


def lanes():
    return lax.broadcasted_iota(jnp.int32, (8, 128), 1)


def side_sums(state, near, row, low, at_left, at_right, first=0):
    slot = (row + first) // GROUPS if isinstance(row, int) else lax.shift_right_logical(row * 43, 7)
    group = row + first - GROUPS * slot
    turn = 128 - (SLOT * slot + HALF // 2 + 1)
    sums = []
    for f in range(MOVING):
        v = state[f, row, pl.ds(low, 8), :]
        edge = pltpu.roll(near[f, group, pl.ds(low, 8), :], turn, 1)
        right = pltpu.roll(jnp.where(at_left, edge, v), 127, 1)
        left = pltpu.roll(jnp.where(at_right, edge, v), 1, 1)
        sums.append(right + left)
    return sums


def main_sums(state, row, low, sides):
    sums = []
    for f in range(MOVING):
        grow = state[f, row, pl.ds(low + 1, 8), :] + state[f, row, pl.ds(low - 1, 8), :]
        side = state[f, row + 1, pl.ds(low, 8), :] + state[f, row - 1, pl.ds(low, 8), :]
        sums.append((grow + side) + sides[f])
    return sums


def center(state, row, low):
    y = [state[MOVING + a, row, pl.ds(low, 8), :] for a in range(3)]
    rest = [state[MOVING + 3 + i, row, pl.ds(low, 8), :] for i in range(2)]
    return y, rest, state[FIELDS - 1, row, pl.ds(low, 8), :]


def near_of(v, swap):
    return jnp.where(swap, pltpu.roll(v, 128 - (HALF - 1), 1), v)


def front_kernel(
    plan, mesh_shape, levels, lab_hbm, pot_hbm, codes_hbm, table_hbm, out_state, out_near,
    lab, pot, codes, table, lab_up, pot_up, raw, pack, strip, even, odd, even_near, odd_near, even_strip, odd_strip, sides, strip_sides,
    in_sems, g_send, g_recv, y_send, y_recv, z_send, z_recv,
):
    g, y, z = lax.axis_index("grow"), lax.axis_index("gy"), lax.axis_index("gz")
    count_g, count_y, count_z = mesh_shape
    rows, tall, planes, shift = plan.rows, plan.tall, plan.planes, plan.shift
    has_below, has_above = g > 0, g < count_g - 1
    is_first, is_last = g == 0, g == count_g - 1
    y_up, y_down = lax.rem(y + 1, count_y), lax.rem(y + count_y - 1, count_y)
    z_other = lax.rem(z + 1, count_z)
    chunks = plan.chunks
    own_chunks, lead, pieces = plan.own_chunks, plan.lead, plan.pieces

    loads = [
        pltpu.make_async_copy(lab_hbm, lab, in_sems.at[0]),
        pltpu.make_async_copy(pot_hbm, pot, in_sems.at[1]),
    ]
    melt_loads = [
        pltpu.make_async_copy(codes_hbm, codes, in_sems.at[2]),
        pltpu.make_async_copy(table_hbm, table, in_sems.at[3]),
    ]
    for copy in loads:
        copy.start()

    @pl.when(is_last)
    def _():
        for copy in melt_loads:
            copy.start()

    barrier = pltpu.get_barrier_semaphore()

    def greet(target):
        pl.semaphore_signal(barrier, inc=1, device_id=target, device_id_type=MESH)

    @pl.when(has_below)
    def _():
        greet((g - 1, y, z))

    @pl.when(has_above)
    def _():
        greet((g + 1, y, z))

    greet((g, y_up, z))
    greet((g, y_down, z))
    greet((g, y, z_other))

    splits = [max(8 * piece - lead, 0) for piece in range(pieces + 1)]

    def g_copies(piece):
        begin, end = splits[piece], splits[piece + 1]
        src, dst = pl.ds(begin * rows, (end - begin) * rows), pl.ds((lead + begin) * rows, (end - begin) * rows)
        copies = []
        for i in range(3):
            source, target = (lab_hbm.at[src], lab_up.at[dst]) if i == 0 else (pot_hbm.at[i - 1, src], pot_up.at[i - 1, dst])
            sem = 3 * piece + i
            copies.append(pltpu.make_async_remote_copy(
                src_ref=source, dst_ref=target, send_sem=g_send.at[sem], recv_sem=g_recv.at[sem],
                device_id=(g - 1, y, z), device_id_type=MESH))
        return copies

    def y_copies(chunk):
        copies = []
        for up in range(2):
            src, dst, target = (rows, 0, y_up) if up else (STEPS, STEPS + rows, y_down)
            sem = 2 * chunk + up
            at = pl.ds(8 * chunk, 8)
            copies.append(pltpu.make_async_remote_copy(
                src_ref=raw.at[:, pl.ds(src, STEPS), at], dst_ref=raw.at[:, pl.ds(dst, STEPS), at],
                send_sem=y_send.at[sem], recv_sem=y_recv.at[sem],
                device_id=(g, target, z), device_id_type=MESH))
        return copies

    def z_copy(chunk):
        at = pl.ds(8 * chunk, 8)
        return pltpu.make_async_remote_copy(
            src_ref=pack.at[:, :, at], dst_ref=strip.at[:, :, at],
            send_sem=z_send.at[chunk], recv_sem=z_recv.at[chunk],
            device_id=(g, y, z_other), device_id_type=MESH)

    def fill(labels, pots, begin, to):
        for row in range(rows):
            at = pl.ds(begin * rows + row, 8, stride=rows)
            raw[0, STEPS + row, pl.ds(to, 8)] = labels[at].astype(jnp.float32)
            for i in range(2):
                raw[1 + i, STEPS + row, pl.ds(to, 8)] = pots[i, at]

    def send_y(chunk):
        for copy in y_copies(chunk):
            copy.start()

    lane = lanes()

    def send_z(chunk):
        for copy in y_copies(chunk):
            copy.wait_recv()
        at = pl.ds(8 * chunk, 8)

        def pack_field(i, carry):
            for group in range(GROUPS):
                packed = jnp.zeros((8, 128), jnp.float32)
                for slot in range(tall // GROUPS):
                    v = raw[i, GROUPS * slot + group, at]
                    first = SLOT * slot
                    packed = jnp.where(lane >= first, pltpu.roll(v, first + HALF // 2 + 1, 1), packed)
                    packed = jnp.where(lane >= first + HALF, pltpu.roll(v, first + HALF + HALF // 2, 1), packed)
                pack[i, group, at] = packed
            return carry

        lax.fori_loop(0, 3, pack_field, 0)
        z_copy(chunk).start()

    place = lane % SLOT
    from_other = (place < HALF // 2 + 1) | (place >= SLOT - HALF // 2 - 1)
    swap = place == HALF // 2 + 1
    at_left, at_right = lane == 0, lane == 127

    def unpack_row(state, slot, row, source, target):
        at = pl.ds(source, 8)
        new = phase_state(raw[0, row, at], [raw[1, row, at], raw[2, row, at]])
        for f in range(FIELDS):
            state[slot, f, row, pl.ds(target, 8)] = new[f]

    def unpack_strips(state, near, slot, source, target):
        at, to = pl.ds(source, 8), pl.ds(target, 8)
        for group in range(GROUPS):
            value = [jnp.where(from_other, strip[i, group, at], pack[i, group, at]) for i in range(3)]
            new = phase_state(value[0], value[1:])
            for f in range(FIELDS):
                state[slot, f, group, to] = new[f]
            for f in range(MOVING):
                near[slot, f, group, to] = near_of(new[f], swap)

    def unpack(chunk):
        to = 8 * chunk

        def body(part, carry):
            rows_at = pl.ds(tall // GROUPS * part, tall // GROUPS)
            at = pl.ds(to, 8)
            new = phase_state(raw[0, rows_at, at], [raw[1, rows_at, at], raw[2, rows_at, at]])
            for f in range(FIELDS):
                even[0, f, rows_at, at] = new[f]
            return carry

        lax.fori_loop(0, GROUPS, body, 0)
        unpack_strips(even_strip, even_near, 0, to, to)

    def strip_side_steps(src, slot, low, result):
        at = pl.ds(low, 8)

        def piece(f):
            v = src[slot, f, :, at]
            part = [src[slot, f, group, at] for group in range(GROUPS)]
            up = jnp.stack([part[1], part[2], pltpu.roll(part[0], 128 - SLOT, 1)])
            down = jnp.stack([pltpu.roll(part[2], SLOT, 1), part[0], part[1]])
            result[f] = (up + down) + (pltpu.roll(v, 127, 2) + pltpu.roll(v, 1, 2))

        return [functools.partial(piece, f) for f in range(MOVING)]

    def strip_step(src, src_slot, dst, near, dst_slot, low, around, tick):
        at = pl.ds(low, 8)
        sums = []
        for f in range(MOVING):
            total = src[src_slot, f, :, pl.ds(low + 1, 8)] + src[src_slot, f, :, pl.ds(low - 1, 8)]
            sums.append(total + around[f])
            tick()
        y = [src[src_slot, MOVING + a, :, at] for a in range(3)]
        rest = [src[src_slot, MOVING + 3 + i, :, at] for i in range(2)]
        new = cell_step(sums, y, rest, src[src_slot, FIELDS - 1, :, at], tick)
        for f in range(FIELDS):
            dst[dst_slot, f, :, at] = new[f]
        for f in range(MOVING):
            near[dst_slot, f, :, at] = jnp.where(swap, pltpu.roll(new[f], 128 - (HALF - 1), 2), new[f])

    def side_steps(state, near, first, count, low, result):
        v, edge, ends = {}, {}, {}

        def near_rolls(f):
            rolled = []
            for i in range(count):
                slot, group = divmod(first + i, GROUPS)
                rolled.append(pltpu.roll(near[f, group, pl.ds(low, 8), :], 128 - (SLOT * slot + HALF // 2 + 1), 1))
            edge[f] = jnp.stack(rolled)
            v[f] = state[f, first : first + count, pl.ds(low, 8), :]

        def z_rolls(f):
            right = pltpu.roll(jnp.where(at_left, edge[f], v[f]), 127, 2)
            left = pltpu.roll(jnp.where(at_right, edge[f], v[f]), 1, 2)
            ends[f] = (right, left)

        def add(f):
            result[f] = ends[f][0] + ends[f][1]

        pieces = []
        for f in range(MOVING + 2 * LAG):
            if f < MOVING:
                pieces.append(functools.partial(near_rolls, f))
            if LAG <= f < MOVING + LAG:
                pieces.append(functools.partial(z_rolls, f - LAG))
            if f >= 2 * LAG:
                pieces.append(functools.partial(add, f - 2 * LAG))
        return pieces

    class Ahead:
        def __init__(self, pieces=()):
            self.pieces = list(pieces)

        def __call__(self):
            if self.pieces:
                self.pieces.pop(0)()

        def flush(self):
            while self.pieces:
                self()

    def sizes_of(step):
        total = tall - 2 * step
        parts = -(-total // BATCH)
        return [total // parts + (k < total % parts) for k in range(parts)]

    def buffers(step):
        if step % 2:
            return odd, odd_near, odd_strip, step // 2
        return even, even_near, even_strip, step // 2

    def begin_steps(stage, step, around, strip_around):
        state, near, strips, slot = buffers(step - 1)
        low = plan.low(stage, step)
        rows_ahead = side_steps(state.at[slot], near.at[slot], step, sizes_of(step)[0], low, around)
        return rows_ahead, strip_side_steps(strips, slot, low, strip_around)

    def keep(around, strip_around):
        for f in range(MOVING):
            sides[: around[f].shape[0], f] = around[f]
            strip_sides[f] = strip_around[f]

    def begin(stage, step):
        around, strip_around = {}, {}
        rows_ahead, strips_ahead = begin_steps(stage, step, around, strip_around)
        for piece in strips_ahead + rows_ahead:
            piece()
        keep(around, strip_around)

    def row_steps(stage, step):
        src, src_near, src_strip, slot = buffers(step - 1)
        dst, dst_near, dst_strip, dst_slot = buffers(step)
        state, near = src.at[slot], src_near.at[slot]
        low = plan.low(stage, step)
        sizes = sizes_of(step)
        at = pl.ds(low, 8)
        ready, strip_ready = {}, {}
        if step == 1:
            rows_ahead, strips_ahead = begin_steps(stage, step, ready, strip_ready)
            Ahead(strips_ahead).flush()
            ahead = Ahead(rows_ahead)
        else:
            ready = {f: sides[: sizes[0], f] for f in range(MOVING)}
            strip_ready = {f: strip_sides[f] for f in range(MOVING)}
            ahead = Ahead()
        strip_step(src_strip, slot, dst_strip, dst_near, dst_slot, low, strip_ready, ahead)
        ahead.flush()
        row = step
        for k, size in enumerate(sizes):
            around, ready, strip_ready = ready, {}, {}
            if k + 1 < len(sizes):
                ahead = Ahead(side_steps(state, near, row + size, sizes[k + 1], low, ready))
            elif step < STEPS - 1:
                rows_ahead, strips_ahead = begin_steps(stage, step + 1, ready, strip_ready)
                ahead = Ahead(strips_ahead + rows_ahead)

            def rows_of(f, shift=0, step=0):
                return state[f, row + shift : row + shift + size, pl.ds(low + step, 8), :]

            sums = []
            for f in range(MOVING):
                grow = rows_of(f, 0, 1) + rows_of(f, 0, -1)
                side = rows_of(f, 1) + rows_of(f, -1)
                sums.append((grow + side) + around[f])
                ahead()
            y = [rows_of(MOVING + a) for a in range(3)]
            rest = [rows_of(MOVING + 3 + i) for i in range(2)]
            new = cell_step(sums, y, rest, rows_of(FIELDS - 1), ahead)
            ahead.flush()
            for f in range(FIELDS):
                dst[dst_slot, f, row : row + size, at, :] = new[f]
            row += size
        if step < STEPS - 1:
            keep(ready, strip_ready)

    def copy_plane(state, strips, near, slot, source, target):
        src, dst = pl.ds(source, 1), pl.ds(target, 1)

        def body(row, carry):
            for f in range(MOVING):
                state[slot, f, row, dst] = state[slot, f, row, src]
            return carry

        lax.fori_loop(0, tall, body, 0)
        for group in range(GROUPS):
            for f in range(MOVING):
                strips[slot, f, group, dst] = strips[slot, f, group, src]
                near[slot, f, group, dst] = near[slot, f, group, src]

    first_plane, top_plane = plan.at(shift), plan.at(planes)
    last_plane = first_plane + planes - 1
    place_up = lax.broadcasted_iota(jnp.int32, (8, 128), 0)

    def melt_fill(stage):
        source, target = 8 * stage + 8, 8 * stage + 7
        melt = place_up >= top_plane - target
        at, to = pl.ds(source, 8), pl.ds(target, 8)

        def body(row, carry):
            new = phase_state(raw[0, row, at], [raw[1, row, at], raw[2, row, at]])
            for f in range(FIELDS):
                pltpu.store(odd.at[1, f, row, to], new[f], mask=melt)
            return carry

        lax.fori_loop(STEPS_BEFORE, tall - STEPS_BEFORE, body, 0)
        for group in range(GROUPS):
            value = [jnp.where(from_other, strip[i, group, at], pack[i, group, at]) for i in range(3)]
            new = phase_state(value[0], value[1:])
            for f in range(FIELDS):
                pltpu.store(odd_strip.at[1, f, group, to], new[f], mask=melt)
            for f in range(MOVING):
                pltpu.store(odd_near.at[1, f, group, to], near_of(new[f], swap), mask=melt)

    def stage_of(plane, step):
        return (plane - plan.low(0, step)) // 8

    def compute(stage):
        top = stage_of(top_plane, STEPS_BEFORE)
        below_melt = (stage <= top) | jnp.logical_not(is_last)

        for step in range(1, STEPS):
            out = (odd, odd_strip, odd_near, step // 2) if step % 2 else (even, even_strip, even_near, step // 2)

            if step <= STEPS_BEFORE:
                pl.when(below_melt)(functools.partial(row_steps, stage, step))
            else:
                row_steps(stage, step)

            if step < STEPS_BEFORE:
                @pl.when(is_last & (stage == stage_of(top_plane, step)))
                def _():
                    copy_plane(*out, top_plane - 1, top_plane)
            else:
                @pl.when(is_first & (stage == stage_of(first_plane, step)))
                def _():
                    copy_plane(*out, first_plane, first_plane - 1)

            if step == STEPS_BEFORE:
                @pl.when(is_last & (stage >= top))
                def _():
                    melt_fill(stage)
                    begin(stage, step + 1)

            if step == STEPS - 1:
                @pl.when(is_last & (stage == stage_of(last_plane, step)))
                def _():
                    copy_plane(*out, last_plane, last_plane + 1)

        at = pl.ds(plan.low(stage, STEPS - 1), 8)
        for f in range(FIELDS):
            for row in range(rows + 2):
                if f < MOVING or 0 < row <= rows:
                    out_state[f, row, at] = even[STEPS // 2, f, STEPS - 1 + row, at]
        for f in range(MOVING):
            for group in range(GROUPS):
                out_near[f, group, at] = even_near[STEPS // 2, f, group, at]

    pl.semaphore_wait(barrier, 3 + has_below.astype(jnp.int32) + has_above.astype(jnp.int32))

    @pl.when(has_below)
    def _():
        for piece in range(pieces):
            for copy in g_copies(piece):
                copy.start()

    for copy in loads:
        copy.wait()

    def fill_own(chunk, carry):
        fill(lab, pot, plan.base + 8 * chunk, 8 * chunk)
        send_y(chunk)
        return carry

    lax.fori_loop(0, own_chunks, fill_own, 0)
    tail = pl.ds((planes - lead) * rows, lead * rows)
    lab_up[0 : lead * rows] = lab[tail]
    for i in range(2):
        pot_up[i, 0 : lead * rows] = pot[i, tail]

    @pl.when(is_last)
    def _():
        for copy in melt_loads:
            copy.wait()
        plane = pl.ds((planes - 1) * rows, rows)
        at = pl.ds(lead * rows, rows)
        lab_up[at] = lab[plane]
        for i in range(2):
            pot_up[i, at] = pot[i, plane]

        def melt_plane(k, carry):
            code = codes[pl.ds(pl.multiple_of(jnp.minimum(k, shift - 1) * rows, rows), rows)]
            at = pl.ds(pl.multiple_of((lead + 1 + k) * rows, rows), rows)
            lab_up[at] = jnp.full((rows, 128), 3, jnp.int32)
            for i in range(2):
                value = jnp.zeros((rows, 128), jnp.float32)
                for level in range(levels):
                    value = jnp.where(code == level, table[i, level], value)
                pot_up[i, at] = value
            return carry

        lax.fori_loop(0, 8 * pieces - lead - 1, melt_plane, 0)

    def beat(it, carry):
        first_z = jnp.where(it > own_chunks, it - 1, it)
        last_z = jnp.where(it == own_chunks, it, jnp.where(it == own_chunks + 2, chunks, jnp.where(it > own_chunks + 2, first_z, first_z + 1)))

        def z_body(chunk, carry):
            send_z(chunk)
            return carry

        @pl.when((it > own_chunks) & (it == 2 * (pieces - 1)))
        def _():
            take(it)

        lax.fori_loop(first_z, last_z, z_body, 0)

        @pl.when((it < 2 * (pieces - 1)) & (lax.rem(it, 2) == 0))
        def _():
            take(it)

        @pl.when(it >= 2)
        def _():
            z_copy(it - 2).wait_recv()
            unpack(it - 2)

        @pl.when(it >= 3)
        def _():
            compute(it - 3)

        return carry

    def take(it):
        piece = lax.div(it, 2)
        for k in range(pieces):
            @pl.when(has_above & (piece == k))
            def _():
                for copy in g_copies(k):
                    copy.wait_recv()

        fill(lab_up, pot_up, 8 * piece, 8 * (own_chunks + piece))
        send_y(own_chunks + piece)

    lax.fori_loop(0, plan.stages + 3, beat, 0)

    def drain(chunk, carry):
        for copy in y_copies(chunk):
            copy.wait_send()
        z_copy(chunk).wait_send()
        return carry

    lax.fori_loop(0, chunks, drain, 0)

    @pl.when(has_below)
    def _():
        for piece in range(pieces):
            for copy in g_copies(piece):
                copy.wait_send()


def last_kernel(plan, state, near, phases, potentials, p_out, m_out, sems):
    rows, planes = plan.rows, plan.planes
    at_left, at_right = lanes() == 0, lanes() == 127
    begin, tiles = plan.at(plan.shift), planes // 8

    def out_copies(tile):
        at = pl.ds(8 * tile * rows, 8 * rows)
        return [
            pltpu.make_async_copy(src.at[:, at], dst.at[:, at], sems.at[2 * tile + i])
            for i, (src, dst) in enumerate(((p_out, phases), (m_out, potentials)))
        ]

    def body(tile, carry):
        low = begin + 8 * tile
        for row in range(1, rows + 1):
            sums = main_sums(state, row, low, side_sums(state, near, row, low, at_left, at_right, STEPS - 1))
            p, m = last_step(sums, *center(state, row, low))
            at = pl.ds(8 * tile * rows + row - 1, 8, stride=rows)
            for f in range(4):
                p_out[f, at, :] = p[f]
            for i in range(2):
                m_out[i, at, :] = m[i]
        for copy in out_copies(tile):
            copy.start()
        return carry

    lax.fori_loop(0, tiles, body, 0)
    for tile in range(tiles):
        for copy in out_copies(tile):
            copy.wait()


def on_device(mesh_shape, labels, potential, melt_codes, melt_table):
    planes, rows, width = labels.shape
    shift, levels = melt_codes.shape[0], melt_table.shape[1]
    plan = Plan(planes, rows, shift)
    flat = planes * rows
    vmem = pl.BlockSpec(memory_space=pltpu.VMEM)
    hbm = pl.BlockSpec(memory_space=pltpu.HBM)
    f32 = jnp.float32
    dma = pltpu.SemaphoreType.DMA
    deep, tall, chunks = plan.deep, plan.tall, plan.chunks
    evens, odds = STEPS // 2 + 1, STEPS // 2
    upper = 8 * plan.pieces * rows
    kept = (FIELDS * (rows + 2) + MOVING * GROUPS) * deep * width * 4
    state, near = pl.pallas_call(
        functools.partial(front_kernel, plan, mesh_shape, levels),
        out_shape=(
            pltpu.VMEM((FIELDS, rows + 2, deep, width), f32),
            pltpu.VMEM((MOVING, GROUPS, deep, width), f32),
        ),
        in_specs=[hbm, hbm, hbm, hbm],
        out_specs=(vmem, vmem),
        scratch_shapes=[
            pltpu.VMEM((flat, width), jnp.int32),
            pltpu.VMEM((2, flat, width), f32),
            pltpu.VMEM((shift * rows, width), jnp.int32),
            pltpu.SMEM((2, levels), f32),
            pltpu.VMEM((upper, width), jnp.int32),
            pltpu.VMEM((2, upper, width), f32),
            pltpu.VMEM((3, tall, deep, width), f32),
            pltpu.VMEM((3, GROUPS, deep, width), f32),
            pltpu.VMEM((3, GROUPS, deep, width), f32),
            pltpu.VMEM((evens, FIELDS, tall, deep, width), f32),
            pltpu.VMEM((odds, FIELDS, tall, deep, width), f32),
            pltpu.VMEM((evens, MOVING, GROUPS, deep, width), f32),
            pltpu.VMEM((odds, MOVING, GROUPS, deep, width), f32),
            pltpu.VMEM((evens, FIELDS, GROUPS, deep, width), f32),
            pltpu.VMEM((odds, FIELDS, GROUPS, deep, width), f32),
            pltpu.VMEM((BATCH, MOVING, 8, width), f32),
            pltpu.VMEM((MOVING, GROUPS, 8, width), f32),
            dma((4,)), dma((3 * chunks,)), dma((3 * chunks,)),
            dma((2 * chunks,)), dma((2 * chunks,)), dma((chunks,)), dma((chunks,)),
        ],
        compiler_params=pltpu.CompilerParams(collective_id=0, has_side_effects=True, vmem_limit_bytes=(VMEM_BYTES - kept) // 4096 * 4096),
        name="front",
    )(labels.reshape(flat, width), potential.reshape(2, flat, width), melt_codes.reshape(shift * rows, width), melt_table)
    state, near = (pltpu.with_memory_space_constraint(v, pltpu.VMEM) for v in (state, near))
    phases, potentials = pl.pallas_call(
        functools.partial(last_kernel, plan),
        out_shape=(
            jax.ShapeDtypeStruct((4, flat, width), f32),
            jax.ShapeDtypeStruct((2, flat, width), f32),
        ),
        in_specs=[vmem, vmem],
        out_specs=(hbm, hbm),
        scratch_shapes=[
            pltpu.VMEM((4, flat, width), f32),
            pltpu.VMEM((2, flat, width), f32),
            dma((2 * (planes // 8),)),
        ],
        compiler_params=pltpu.CompilerParams(vmem_limit_bytes=8 << 20),
        name="last",
    )(state, near)
    return phases.reshape(4, planes, rows, width), potentials.reshape(2, planes, rows, width)


def solution(mesh):
    mesh_shape = tuple(mesh.shape[axis] for axis in ("grow", "gy", "gz"))
    return jax.shard_map(
        functools.partial(on_device, mesh_shape),
        mesh=mesh,
        in_specs=(P("grow", "gy", "gz"), P(None, "grow", "gy", "gz"), P(None, "gy", "gz"), P()),
        out_specs=(P(None, "grow", "gy", "gz"), P(None, "grow", "gy", "gz")),
        check_vma=False,
    )
```

```python
import functools

import jax
import jax.numpy as jnp
from jax import lax
from jax.experimental import pallas as pl
from jax.experimental.pallas import tpu as pltpu
from jax.sharding import PartitionSpec as P

STEPS_BEFORE = 3
STEPS_AFTER = 2
STEPS = STEPS_BEFORE + STEPS_AFTER
HALF = 9
SLOT = 2 * HALF
GROUPS = 3
LAG = 5
BATCH = 8
FIELDS = 11
MOVING = 5
CODE = 16.0
CODED_AT = (0,) + tuple(range(3, FIELDS))
VMEM_BYTES = 67043328
MESH = pl.DeviceIdType.MESH

LAM = 0.12
BETA = 5.0 / LAM**2
MU = 17.5 / (LAM * BETA)
OWN = (1.0 / LAM - 6.0) / BETA
TILT = 1.25 / (LAM * BETA)
BACK = 0.2 * MU / LAM**3


class Plan:
    def __init__(self, planes, rows, shift):
        self.planes, self.rows, self.shift = planes, rows, shift
        self.base = shift - STEPS + 2 - 8
        self.chunks = planes // 8 + 2
        self.stages = self.chunks - 1
        self.deep = 8 * self.chunks
        self.above = shift + STEPS
        self.tall = rows + 2 * STEPS
        self.own_chunks, self.lead = divmod(planes - self.base, 8)
        self.pieces = self.chunks - self.own_chunks

    def at(self, plane):
        return plane - self.base

    def low(self, stage, step):
        return 8 + 8 * stage - step


def phase_state(label, pot, coded=False):
    if coded:
        q = [jnp.where(label == 0.0, 1.0, jnp.where(label == 1.0, CODE, jnp.where(label == 2.0, CODE * CODE, 0.0)))]
    else:
        q = [jnp.where(label == float(a), LAM, 0.0) for a in range(3)]
    y = [jnp.where(label == float(a), LAM * BETA * OWN, 0.0) for a in range(3)]
    liquid = label == 3.0
    mob = jnp.where(liquid, 0.15, 0.0075)
    u = [MU * v for v in pot]
    comp = [jnp.where(liquid, 0.35 * MU, jnp.where(label == float(i), 0.8 * MU, 0.1 * MU)) for i in range(2)]
    rest = [(u[i] + comp[i]) - (6.0 * mob) * u[i] for i in range(2)]
    return q + u + y + rest + [mob]


def decode(total):
    third = jnp.floor(total * (1.0 / (CODE * CODE)))
    total = total - (CODE * CODE) * third
    second = jnp.floor(total * (1.0 / CODE))
    return [LAM * v for v in (total - CODE * second, second, third)]


def moving_of(step):
    return (0, 3, 4) if step == 1 else tuple(range(MOVING))


def clip_step(sums, y):
    x = [sums[a] + y[a] for a in range(3)]
    x.append(1.0 - (x[0] + x[1] + x[2]))
    held = [jnp.clip(v, 0.0, 1.0) for v in x]
    return held, 1.0 / ((held[0] + held[1]) + (held[2] + held[3]))


def cell_step(sums, y, rest, mob, tick=lambda: None):
    held, inverse = clip_step(sums, y)
    tick()
    total = [rest[i] + mob * sums[3 + i] for i in range(2)]
    tick()
    scaled = LAM * inverse
    q = [v * scaled for v in held]
    tick()
    square = [v * v for v in q]
    tick()
    h = [square[a] * (1.5 * LAM - q[a]) for a in range(4)]
    tick()
    shared = BACK * ((h[0] + h[1]) + (h[2] + 3.5 * h[3]))
    tick()
    u = [(total[i] - shared) - (7.0 * BACK) * h[i] for i in range(2)]
    tick()
    both = u[0] + u[1]
    well = OWN - ((square[0] + square[1]) + (square[2] + square[3]))
    tick()
    third = both * (1.0 / 7.0) + TILT
    pull = [third + u[0], third + u[1], third, 0.5 * both]
    tick()
    mob = 0.0075 + (0.1425 / LAM) * q[3]
    six = 6.0 * mob
    rest = [total[i] - six * u[i] for i in range(2)]
    tick()
    local = []
    for a in range(4):
        local.append(q[a] * ((well + square[a]) + pull[a] * (LAM - q[a])))
        tick()
    mean = 0.25 * ((local[0] + local[1]) + (local[2] + local[3])) - 0.07 / BETA
    tick()
    y = [BETA * (local[a] - mean) for a in range(3)]
    tick()
    return q[:3] + u + y + rest + [mob]


def last_step(sums, y, rest, mob):
    held, inverse = clip_step(sums, y)
    p = [v * inverse for v in held]
    h = [v * v * (1.5 - v) for v in p]
    shared = 0.2 * ((h[0] + h[1]) + (h[2] + 3.5 * h[3]))
    total = [(rest[i] + mob * sums[3 + i]) * (1.0 / MU) for i in range(2)]
    return p, [(total[i] - shared) - 1.4 * h[i] for i in range(2)]


def lanes():
    return lax.broadcasted_iota(jnp.int32, (8, 128), 1)


def side_sums(state, near, row, low, at_left, at_right, first=0):
    slot = (row + first) // GROUPS if isinstance(row, int) else lax.shift_right_logical(row * 43, 7)
    group = row + first - GROUPS * slot
    turn = 128 - (SLOT * slot + HALF // 2 + 1)
    sums = []
    for f in range(MOVING):
        v = state[f, row, pl.ds(low, 8), :]
        edge = pltpu.roll(near[f, group, pl.ds(low, 8), :], turn, 1)
        right = pltpu.roll(jnp.where(at_left, edge, v), 127, 1)
        left = pltpu.roll(jnp.where(at_right, edge, v), 1, 1)
        sums.append(right + left)
    return sums


def main_sums(state, row, low, sides):
    sums = []
    for f in range(MOVING):
        grow = state[f, row, pl.ds(low + 1, 8), :] + state[f, row, pl.ds(low - 1, 8), :]
        side = state[f, row + 1, pl.ds(low, 8), :] + state[f, row - 1, pl.ds(low, 8), :]
        sums.append((grow + side) + sides[f])
    return sums


def center(state, row, low):
    y = [state[MOVING + a, row, pl.ds(low, 8), :] for a in range(3)]
    rest = [state[MOVING + 3 + i, row, pl.ds(low, 8), :] for i in range(2)]
    return y, rest, state[FIELDS - 1, row, pl.ds(low, 8), :]


def near_of(v, swap):
    return jnp.where(swap, pltpu.roll(v, 128 - (HALF - 1), 1), v)


def front_kernel(
    plan, mesh_shape, levels, lab_hbm, pot_hbm, codes_hbm, table_hbm, out_state, out_near,
    lab, pot, codes, table, lab_up, pot_up, raw, pack, strip, even, odd, even_near, odd_near, even_strip, odd_strip, sides, strip_sides,
    in_sems, g_send, g_recv, y_send, y_recv, z_send, z_recv,
):
    g, y, z = lax.axis_index("grow"), lax.axis_index("gy"), lax.axis_index("gz")
    count_g, count_y, count_z = mesh_shape
    rows, tall, planes, shift = plan.rows, plan.tall, plan.planes, plan.shift
    has_below, has_above = g > 0, g < count_g - 1
    is_first, is_last = g == 0, g == count_g - 1
    y_up, y_down = lax.rem(y + 1, count_y), lax.rem(y + count_y - 1, count_y)
    z_other = lax.rem(z + 1, count_z)
    chunks = plan.chunks
    own_chunks, lead, pieces = plan.own_chunks, plan.lead, plan.pieces

    loads = [
        pltpu.make_async_copy(lab_hbm, lab, in_sems.at[0]),
        pltpu.make_async_copy(pot_hbm, pot, in_sems.at[1]),
    ]
    melt_loads = [
        pltpu.make_async_copy(codes_hbm, codes, in_sems.at[2]),
        pltpu.make_async_copy(table_hbm, table, in_sems.at[3]),
    ]
    for copy in loads:
        copy.start()

    @pl.when(is_last)
    def _():
        for copy in melt_loads:
            copy.start()

    barrier = pltpu.get_barrier_semaphore()

    def greet(target):
        pl.semaphore_signal(barrier, inc=1, device_id=target, device_id_type=MESH)

    @pl.when(has_below)
    def _():
        greet((g - 1, y, z))

    @pl.when(has_above)
    def _():
        greet((g + 1, y, z))

    greet((g, y_up, z))
    greet((g, y_down, z))
    greet((g, y, z_other))

    splits = [max(8 * piece - lead, 0) for piece in range(pieces + 1)]

    def g_copies(piece):
        begin, end = splits[piece], splits[piece + 1]
        src, dst = pl.ds(begin * rows, (end - begin) * rows), pl.ds((lead + begin) * rows, (end - begin) * rows)
        copies = []
        for i in range(3):
            source, target = (lab_hbm.at[src], lab_up.at[dst]) if i == 0 else (pot_hbm.at[i - 1, src], pot_up.at[i - 1, dst])
            sem = 3 * piece + i
            copies.append(pltpu.make_async_remote_copy(
                src_ref=source, dst_ref=target, send_sem=g_send.at[sem], recv_sem=g_recv.at[sem],
                device_id=(g - 1, y, z), device_id_type=MESH))
        return copies

    def planes_of(chunk):
        return pl.ds(7, 1) if isinstance(chunk, int) and chunk == 0 else pl.ds(8 * chunk, 8)

    def either(chunk, action):
        pl.when(chunk == 0)(lambda: action(0))
        pl.when(chunk > 0)(lambda: action(chunk))

    def y_copies(chunk):
        copies = []
        for up in range(2):
            src, dst, target = (rows, 0, y_up) if up else (STEPS, STEPS + rows, y_down)
            sem = 2 * chunk + up
            at = planes_of(chunk)
            copies.append(pltpu.make_async_remote_copy(
                src_ref=raw.at[:, pl.ds(src, STEPS), at], dst_ref=raw.at[:, pl.ds(dst, STEPS), at],
                send_sem=y_send.at[sem], recv_sem=y_recv.at[sem],
                device_id=(g, target, z), device_id_type=MESH))
        return copies

    def z_copy(chunk):
        at = planes_of(chunk)
        return pltpu.make_async_remote_copy(
            src_ref=pack.at[:, :, at], dst_ref=strip.at[:, :, at],
            send_sem=z_send.at[chunk], recv_sem=z_recv.at[chunk],
            device_id=(g, y, z_other), device_id_type=MESH)

    def fill(labels, pots, begin, to):
        for row in range(rows):
            at = pl.ds(begin * rows + row, 8, stride=rows)
            raw[0, STEPS + row, pl.ds(to, 8)] = labels[at].astype(jnp.float32)
            for i in range(2):
                raw[1 + i, STEPS + row, pl.ds(to, 8)] = pots[i, at]

    def send_y(chunk):
        for copy in y_copies(chunk):
            copy.start()

    lane = lanes()

    def send_z(chunk):
        either(chunk, lambda k: [copy.wait_recv() for copy in y_copies(k)] and None)
        at = pl.ds(8 * chunk, 8)

        def pack_field(i, carry):
            for group in range(GROUPS):
                packed = jnp.zeros((8, 128), jnp.float32)
                for slot in range(tall // GROUPS):
                    v = raw[i, GROUPS * slot + group, at]
                    first = SLOT * slot
                    packed = jnp.where(lane >= first, pltpu.roll(v, first + HALF // 2 + 1, 1), packed)
                    packed = jnp.where(lane >= first + HALF, pltpu.roll(v, first + HALF + HALF // 2, 1), packed)
                pack[i, group, at] = packed
            return carry

        lax.fori_loop(0, 3, pack_field, 0)
        either(chunk, lambda k: z_copy(k).start())

    place = lane % SLOT
    from_other = (place < HALF // 2 + 1) | (place >= SLOT - HALF // 2 - 1)
    swap = place == HALF // 2 + 1
    at_left, at_right = lane == 0, lane == 127

    def unpack_row(state, slot, row, source, target):
        at = pl.ds(source, 8)
        new = phase_state(raw[0, row, at], [raw[1, row, at], raw[2, row, at]])
        for f in range(FIELDS):
            state[slot, f, row, pl.ds(target, 8)] = new[f]

    def unpack_strips(state, near, slot, source, target):
        at, to = pl.ds(source, 8), pl.ds(target, 8)
        for group in range(GROUPS):
            value = [jnp.where(from_other, strip[i, group, at], pack[i, group, at]) for i in range(3)]
            for f, v in zip(CODED_AT, phase_state(value[0], value[1:], True)):
                state[slot, f, group, to] = v
                if f < MOVING:
                    near[slot, f, group, to] = near_of(v, swap)

    def unpack(chunk):
        to = 8 * chunk

        def body(part, carry):
            rows_at = pl.ds(tall // GROUPS * part, tall // GROUPS)
            at = pl.ds(to, 8)
            new = phase_state(raw[0, rows_at, at], [raw[1, rows_at, at], raw[2, rows_at, at]], True)
            for f, v in zip(CODED_AT, new):
                even[0, f, rows_at, at] = v
            return carry

        lax.fori_loop(0, GROUPS, body, 0)
        unpack_strips(even_strip, even_near, 0, to, to)

    def strip_side_steps(fields, src, slot, low, result):
        at = pl.ds(low, 8)

        def piece(f):
            v = src[slot, f, :, at]
            part = [src[slot, f, group, at] for group in range(GROUPS)]
            up = jnp.stack([part[1], part[2], pltpu.roll(part[0], 128 - SLOT, 1)])
            down = jnp.stack([pltpu.roll(part[2], SLOT, 1), part[0], part[1]])
            result[f] = (up + down) + (pltpu.roll(v, 127, 2) + pltpu.roll(v, 1, 2))

        return [functools.partial(piece, f) for f in fields]

    def strip_step(step, src, src_slot, dst, near, dst_slot, low, around, tick):
        at = pl.ds(low, 8)
        sums = []
        for f in moving_of(step):
            total = src[src_slot, f, :, pl.ds(low + 1, 8)] + src[src_slot, f, :, pl.ds(low - 1, 8)]
            sums.append(total + around[f])
            tick()
        if step == 1:
            sums = decode(sums[0]) + sums[1:]
        y = [src[src_slot, MOVING + a, :, at] for a in range(3)]
        rest = [src[src_slot, MOVING + 3 + i, :, at] for i in range(2)]
        new = cell_step(sums, y, rest, src[src_slot, FIELDS - 1, :, at], tick)
        for f in range(FIELDS):
            dst[dst_slot, f, :, at] = new[f]
        for f in range(MOVING):
            near[dst_slot, f, :, at] = jnp.where(swap, pltpu.roll(new[f], 128 - (HALF - 1), 2), new[f])

    def side_steps(fields, state, near, first, count, low, result):
        v, edge, ends = {}, {}, {}

        def near_rolls(f):
            rolled = []
            for i in range(count):
                slot, group = divmod(first + i, GROUPS)
                rolled.append(pltpu.roll(near[f, group, pl.ds(low, 8), :], 128 - (SLOT * slot + HALF // 2 + 1), 1))
            edge[f] = jnp.stack(rolled)
            v[f] = state[f, first : first + count, pl.ds(low, 8), :]

        def z_rolls(f):
            right = pltpu.roll(jnp.where(at_left, edge[f], v[f]), 127, 2)
            left = pltpu.roll(jnp.where(at_right, edge[f], v[f]), 1, 2)
            ends[f] = (right, left)

        def add(f):
            result[f] = ends[f][0] + ends[f][1]

        pieces = []
        for k in range(len(fields) + 2 * LAG):
            if k < len(fields):
                pieces.append(functools.partial(near_rolls, fields[k]))
            if LAG <= k < len(fields) + LAG:
                pieces.append(functools.partial(z_rolls, fields[k - LAG]))
            if k >= 2 * LAG:
                pieces.append(functools.partial(add, fields[k - 2 * LAG]))
        return pieces

    class Ahead:
        def __init__(self, pieces=()):
            self.pieces = list(pieces)

        def __call__(self):
            if self.pieces:
                self.pieces.pop(0)()

        def flush(self):
            while self.pieces:
                self()

    def sizes_of(step):
        total = tall - 2 * step
        parts = -(-total // BATCH)
        return [total // parts + (k < total % parts) for k in range(parts)]

    def buffers(step):
        if step % 2:
            return odd, odd_near, odd_strip, step // 2
        return even, even_near, even_strip, step // 2

    def begin_steps(stage, step, around, strip_around):
        state, near, strips, slot = buffers(step - 1)
        low = plan.low(stage, step)
        rows_ahead = side_steps(moving_of(step), state.at[slot], near.at[slot], step, sizes_of(step)[0], low, around)
        return rows_ahead, strip_side_steps(moving_of(step), strips, slot, low, strip_around)

    def keep(around, strip_around):
        for f in around:
            sides[: around[f].shape[0], f] = around[f]
            strip_sides[f] = strip_around[f]

    def begin(stage, step):
        around, strip_around = {}, {}
        rows_ahead, strips_ahead = begin_steps(stage, step, around, strip_around)
        for piece in strips_ahead + rows_ahead:
            piece()
        keep(around, strip_around)

    def row_steps(stage, step):
        src, src_near, src_strip, slot = buffers(step - 1)
        dst, dst_near, dst_strip, dst_slot = buffers(step)
        state, near = src.at[slot], src_near.at[slot]
        low = plan.low(stage, step)
        sizes = sizes_of(step)
        at = pl.ds(low, 8)
        ready, strip_ready = {}, {}
        if step == 1:
            rows_ahead, strips_ahead = begin_steps(stage, step, ready, strip_ready)
            Ahead(strips_ahead).flush()
            ahead = Ahead(rows_ahead)
        else:
            ready = {f: sides[: sizes[0], f] for f in moving_of(step)}
            strip_ready = {f: strip_sides[f] for f in moving_of(step)}
            ahead = Ahead()
        strip_step(step, src_strip, slot, dst_strip, dst_near, dst_slot, low, strip_ready, ahead)
        ahead.flush()
        row = step
        for k, size in enumerate(sizes):
            around, ready, strip_ready = ready, {}, {}
            if k + 1 < len(sizes):
                ahead = Ahead(side_steps(moving_of(step), state, near, row + size, sizes[k + 1], low, ready))
            elif step < STEPS - 1:
                rows_ahead, strips_ahead = begin_steps(stage, step + 1, ready, strip_ready)
                ahead = Ahead(strips_ahead + rows_ahead)

            def rows_of(f, shift=0, up=0):
                return state[f, row + shift : row + shift + size, pl.ds(low + up, 8), :]

            sums = []
            for f in moving_of(step):
                grow = rows_of(f, 0, 1) + rows_of(f, 0, -1)
                side = rows_of(f, 1) + rows_of(f, -1)
                sums.append((grow + side) + around[f])
                ahead()
            if step == 1:
                sums = decode(sums[0]) + sums[1:]
            y = [rows_of(MOVING + a) for a in range(3)]
            rest = [rows_of(MOVING + 3 + i) for i in range(2)]
            new = cell_step(sums, y, rest, rows_of(FIELDS - 1), ahead)
            ahead.flush()
            for f in range(FIELDS):
                dst[dst_slot, f, row : row + size, at, :] = new[f]
            row += size
        if step < STEPS - 1:
            keep(ready, strip_ready)

    def copy_plane(state, strips, near, slot, source, target):
        src, dst = pl.ds(source, 1), pl.ds(target, 1)

        def body(row, carry):
            for f in range(MOVING):
                state[slot, f, row, dst] = state[slot, f, row, src]
            return carry

        lax.fori_loop(0, tall, body, 0)
        for group in range(GROUPS):
            for f in range(MOVING):
                strips[slot, f, group, dst] = strips[slot, f, group, src]
                near[slot, f, group, dst] = near[slot, f, group, src]

    first_plane, top_plane = plan.at(shift), plan.at(planes)
    last_plane = first_plane + planes - 1
    place_up = lax.broadcasted_iota(jnp.int32, (8, 128), 0)

    def melt_fill(stage):
        source, target = 8 * stage + 8, 8 * stage + 7
        melt = place_up >= top_plane - target
        at, to = pl.ds(source, 8), pl.ds(target, 8)

        def body(row, carry):
            new = phase_state(raw[0, row, at], [raw[1, row, at], raw[2, row, at]])
            for f in range(FIELDS):
                pltpu.store(odd.at[1, f, row, to], new[f], mask=melt)
            return carry

        lax.fori_loop(STEPS_BEFORE, tall - STEPS_BEFORE, body, 0)
        for group in range(GROUPS):
            value = [jnp.where(from_other, strip[i, group, at], pack[i, group, at]) for i in range(3)]
            new = phase_state(value[0], value[1:])
            for f in range(FIELDS):
                pltpu.store(odd_strip.at[1, f, group, to], new[f], mask=melt)
            for f in range(MOVING):
                pltpu.store(odd_near.at[1, f, group, to], near_of(new[f], swap), mask=melt)

    def stage_of(plane, step):
        return (plane - plan.low(0, step)) // 8

    def compute(stage):
        top = stage_of(top_plane, STEPS_BEFORE)
        below_melt = (stage <= top) | jnp.logical_not(is_last)

        for step in range(1, STEPS):
            out = (odd, odd_strip, odd_near, step // 2) if step % 2 else (even, even_strip, even_near, step // 2)

            if step <= STEPS_BEFORE:
                pl.when(below_melt)(functools.partial(row_steps, stage, step))
            else:
                row_steps(stage, step)

            if step < STEPS_BEFORE:
                @pl.when(is_last & (stage == stage_of(top_plane, step)))
                def _():
                    copy_plane(*out, top_plane - 1, top_plane)
            else:
                @pl.when(is_first & (stage == stage_of(first_plane, step)))
                def _():
                    copy_plane(*out, first_plane, first_plane - 1)

            if step == STEPS_BEFORE:
                @pl.when(is_last & (stage >= top))
                def _():
                    melt_fill(stage)
                    begin(stage, step + 1)

            if step == STEPS - 1:
                @pl.when(is_last & (stage == stage_of(last_plane, step)))
                def _():
                    copy_plane(*out, last_plane, last_plane + 1)

        at = pl.ds(plan.low(stage, STEPS - 1), 8)
        for f in range(FIELDS):
            for row in range(rows + 2):
                if f < MOVING or 0 < row <= rows:
                    out_state[f, row, at] = even[STEPS // 2, f, STEPS - 1 + row, at]
        for f in range(MOVING):
            for group in range(GROUPS):
                out_near[f, group, at] = even_near[STEPS // 2, f, group, at]

    pl.semaphore_wait(barrier, 3 + has_below.astype(jnp.int32) + has_above.astype(jnp.int32))

    @pl.when(has_below)
    def _():
        for piece in range(pieces):
            for copy in g_copies(piece):
                copy.start()

    for copy in loads:
        copy.wait()

    def fill_own(chunk, carry):
        fill(lab, pot, plan.base + 8 * chunk, 8 * chunk)
        either(chunk, send_y)
        return carry

    lax.fori_loop(0, own_chunks, fill_own, 0)
    tail = pl.ds((planes - lead) * rows, lead * rows)
    lab_up[0 : lead * rows] = lab[tail]
    for i in range(2):
        pot_up[i, 0 : lead * rows] = pot[i, tail]

    @pl.when(is_last)
    def _():
        for copy in melt_loads:
            copy.wait()
        plane = pl.ds((planes - 1) * rows, rows)
        at = pl.ds(lead * rows, rows)
        lab_up[at] = lab[plane]
        for i in range(2):
            pot_up[i, at] = pot[i, plane]

        def melt_plane(k, carry):
            code = codes[pl.ds(pl.multiple_of(jnp.minimum(k, shift - 1) * rows, rows), rows)]
            at = pl.ds(pl.multiple_of((lead + 1 + k) * rows, rows), rows)
            lab_up[at] = jnp.full((rows, 128), 3, jnp.int32)
            for i in range(2):
                value = jnp.zeros((rows, 128), jnp.float32)
                for level in range(levels):
                    value = jnp.where(code == level, table[i, level], value)
                pot_up[i, at] = value
            return carry

        lax.fori_loop(0, 8 * pieces - lead - 1, melt_plane, 0)

    def beat(it, carry):
        first_z = jnp.where(it > own_chunks, it - 1, it)
        last_z = jnp.where(it == own_chunks, it, jnp.where(it == own_chunks + 2, chunks, jnp.where(it > own_chunks + 2, first_z, first_z + 1)))

        def z_body(chunk, carry):
            send_z(chunk)
            return carry

        @pl.when((it > own_chunks) & (it == 2 * (pieces - 1)))
        def _():
            take(it)

        lax.fori_loop(first_z, last_z, z_body, 0)

        @pl.when((it < 2 * (pieces - 1)) & (lax.rem(it, 2) == 0))
        def _():
            take(it)

        @pl.when(it >= 2)
        def _():
            either(it - 2, lambda k: z_copy(k).wait_recv())
            unpack(it - 2)

        @pl.when(it >= 3)
        def _():
            compute(it - 3)

        return carry

    def take(it):
        piece = lax.div(it, 2)
        for k in range(pieces):
            @pl.when(has_above & (piece == k))
            def _():
                for copy in g_copies(k):
                    copy.wait_recv()

        fill(lab_up, pot_up, 8 * piece, 8 * (own_chunks + piece))
        send_y(own_chunks + piece)

    lax.fori_loop(0, plan.stages + 3, beat, 0)

    def drain(chunk, carry):
        def wait(k):
            for copy in y_copies(k):
                copy.wait_send()
            z_copy(k).wait_send()

        either(chunk, wait)
        return carry

    lax.fori_loop(0, chunks, drain, 0)

    @pl.when(has_below)
    def _():
        for piece in range(pieces):
            for copy in g_copies(piece):
                copy.wait_send()


def last_kernel(plan, state, near, phases, potentials, p_out, m_out, sems):
    rows, planes = plan.rows, plan.planes
    at_left, at_right = lanes() == 0, lanes() == 127
    begin, tiles = plan.at(plan.shift), planes // 8

    def out_copies(tile):
        at = pl.ds(8 * tile * rows, 8 * rows)
        return [
            pltpu.make_async_copy(src.at[:, at], dst.at[:, at], sems.at[2 * tile + i])
            for i, (src, dst) in enumerate(((p_out, phases), (m_out, potentials)))
        ]

    def body(tile, carry):
        low = begin + 8 * tile
        for row in range(1, rows + 1):
            sums = main_sums(state, row, low, side_sums(state, near, row, low, at_left, at_right, STEPS - 1))
            p, m = last_step(sums, *center(state, row, low))
            at = pl.ds(8 * tile * rows + row - 1, 8, stride=rows)
            for f in range(4):
                p_out[f, at, :] = p[f]
            for i in range(2):
                m_out[i, at, :] = m[i]
        for copy in out_copies(tile):
            copy.start()
        return carry

    lax.fori_loop(0, tiles, body, 0)
    for tile in range(tiles):
        for copy in out_copies(tile):
            copy.wait()


def on_device(mesh_shape, labels, potential, melt_codes, melt_table):
    planes, rows, width = labels.shape
    shift, levels = melt_codes.shape[0], melt_table.shape[1]
    plan = Plan(planes, rows, shift)
    flat = planes * rows
    vmem = pl.BlockSpec(memory_space=pltpu.VMEM)
    hbm = pl.BlockSpec(memory_space=pltpu.HBM)
    f32 = jnp.float32
    dma = pltpu.SemaphoreType.DMA
    deep, tall, chunks = plan.deep, plan.tall, plan.chunks
    evens, odds = STEPS // 2 + 1, STEPS // 2
    upper = 8 * plan.pieces * rows
    kept = (FIELDS * (rows + 2) + MOVING * GROUPS) * deep * width * 4
    state, near = pl.pallas_call(
        functools.partial(front_kernel, plan, mesh_shape, levels),
        out_shape=(
            pltpu.VMEM((FIELDS, rows + 2, deep, width), f32),
            pltpu.VMEM((MOVING, GROUPS, deep, width), f32),
        ),
        in_specs=[hbm, hbm, hbm, hbm],
        out_specs=(vmem, vmem),
        scratch_shapes=[
            pltpu.VMEM((flat, width), jnp.int32),
            pltpu.VMEM((2, flat, width), f32),
            pltpu.VMEM((shift * rows, width), jnp.int32),
            pltpu.SMEM((2, levels), f32),
            pltpu.VMEM((upper, width), jnp.int32),
            pltpu.VMEM((2, upper, width), f32),
            pltpu.VMEM((3, tall, deep, width), f32),
            pltpu.VMEM((3, GROUPS, deep, width), f32),
            pltpu.VMEM((3, GROUPS, deep, width), f32),
            pltpu.VMEM((evens, FIELDS, tall, deep, width), f32),
            pltpu.VMEM((odds, FIELDS, tall, deep, width), f32),
            pltpu.VMEM((evens, MOVING, GROUPS, deep, width), f32),
            pltpu.VMEM((odds, MOVING, GROUPS, deep, width), f32),
            pltpu.VMEM((evens, FIELDS, GROUPS, deep, width), f32),
            pltpu.VMEM((odds, FIELDS, GROUPS, deep, width), f32),
            pltpu.VMEM((BATCH, MOVING, 8, width), f32),
            pltpu.VMEM((MOVING, GROUPS, 8, width), f32),
            dma((4,)), dma((3 * chunks,)), dma((3 * chunks,)),
            dma((2 * chunks,)), dma((2 * chunks,)), dma((chunks,)), dma((chunks,)),
        ],
        compiler_params=pltpu.CompilerParams(collective_id=0, has_side_effects=True, vmem_limit_bytes=(VMEM_BYTES - kept) // 4096 * 4096),
        name="front",
    )(labels.reshape(flat, width), potential.reshape(2, flat, width), melt_codes.reshape(shift * rows, width), melt_table)
    state, near = (pltpu.with_memory_space_constraint(v, pltpu.VMEM) for v in (state, near))
    phases, potentials = pl.pallas_call(
        functools.partial(last_kernel, plan),
        out_shape=(
            jax.ShapeDtypeStruct((4, flat, width), f32),
            jax.ShapeDtypeStruct((2, flat, width), f32),
        ),
        in_specs=[vmem, vmem],
        out_specs=(hbm, hbm),
        scratch_shapes=[
            pltpu.VMEM((4, flat, width), f32),
            pltpu.VMEM((2, flat, width), f32),
            dma((2 * (planes // 8),)),
        ],
        compiler_params=pltpu.CompilerParams(vmem_limit_bytes=8 << 20),
        name="last",
    )(state, near)
    return phases.reshape(4, planes, rows, width), potentials.reshape(2, planes, rows, width)


def solution(mesh):
    mesh_shape = tuple(mesh.shape[axis] for axis in ("grow", "gy", "gz"))
    return jax.shard_map(
        functools.partial(on_device, mesh_shape),
        mesh=mesh,
        in_specs=(P("grow", "gy", "gz"), P(None, "grow", "gy", "gz"), P(None, "gy", "gz"), P()),
        out_specs=(P(None, "grow", "gy", "gz"), P(None, "grow", "gy", "gz")),
        check_vma=False,
    )
```

```python
import functools

import jax
import jax.numpy as jnp
from jax import lax
from jax.experimental import pallas as pl
from jax.experimental.pallas import tpu as pltpu
from jax.sharding import PartitionSpec as P

STEPS_BEFORE = 3
STEPS_AFTER = 2
STEPS = STEPS_BEFORE + STEPS_AFTER
HALF = 9
SLOT = 2 * HALF
GROUPS = 3
LAG = 5
BATCH = 8
FIELDS = 11
MOVING = 5
CODE = 16.0
CODED_AT = (0,) + tuple(range(3, FIELDS))
VMEM_BYTES = 67043328
MESH = pl.DeviceIdType.MESH

LAM = 0.12
BETA = 5.0 / LAM**2
MU = 17.5 / (LAM * BETA)
OWN = (1.0 / LAM - 6.0) / BETA
TILT = 1.25 / (LAM * BETA)
BACK = 0.2 * MU / LAM**3


class Plan:
    def __init__(self, planes, rows, shift):
        self.planes, self.rows, self.shift = planes, rows, shift
        self.base = shift - STEPS + 2 - 8
        self.chunks = planes // 8 + 2
        self.stages = self.chunks - 1
        self.deep = 8 * self.chunks
        self.above = shift + STEPS
        self.tall = rows + 2 * STEPS
        self.own_chunks, self.lead = divmod(planes - self.base, 8)
        self.pieces = self.chunks - self.own_chunks

    def at(self, plane):
        return plane - self.base

    def low(self, stage, step):
        return 8 + 8 * stage - step


def phase_state(label, pot, coded=False):
    if coded:
        q = [jnp.where(label == 0.0, 1.0, jnp.where(label == 1.0, CODE, jnp.where(label == 2.0, CODE * CODE, 0.0)))]
    else:
        q = [jnp.where(label == float(a), LAM, 0.0) for a in range(3)]
    y = [jnp.where(label == float(a), LAM * BETA * OWN, 0.0) for a in range(3)]
    liquid = label == 3.0
    mob = jnp.where(liquid, 0.15, 0.0075)
    u = [MU * v for v in pot]
    comp = [jnp.where(liquid, 0.35 * MU, jnp.where(label == float(i), 0.8 * MU, 0.1 * MU)) for i in range(2)]
    rest = [(u[i] + comp[i]) - (6.0 * mob) * u[i] for i in range(2)]
    return q + u + y + rest + [mob]


def decode(total):
    third = jnp.floor(total * (1.0 / (CODE * CODE)))
    total = total - (CODE * CODE) * third
    second = jnp.floor(total * (1.0 / CODE))
    return [LAM * v for v in (total - CODE * second, second, third)]


def moving_of(step):
    return (0, 3, 4) if step == 1 else tuple(range(MOVING))


def clip_step(sums, y):
    x = [sums[a] + y[a] for a in range(3)]
    x.append(1.0 - (x[0] + x[1] + x[2]))
    held = [jnp.clip(v, 0.0, 1.0) for v in x]
    return held, 1.0 / ((held[0] + held[1]) + (held[2] + held[3]))


def cell_step(sums, y, rest, mob, tick=lambda: None):
    held, inverse = clip_step(sums, y)
    tick()
    total = [rest[i] + mob * sums[3 + i] for i in range(2)]
    tick()
    scaled = LAM * inverse
    q = [v * scaled for v in held]
    tick()
    square = [v * v for v in q]
    tick()
    h = [square[a] * (1.5 * LAM - q[a]) for a in range(4)]
    tick()
    shared = BACK * ((h[0] + h[1]) + (h[2] + 3.5 * h[3]))
    tick()
    u = [(total[i] - shared) - (7.0 * BACK) * h[i] for i in range(2)]
    tick()
    both = u[0] + u[1]
    well = OWN - ((square[0] + square[1]) + (square[2] + square[3]))
    tick()
    third = both * (1.0 / 7.0) + TILT
    pull = [third + u[0], third + u[1], third, 0.5 * both]
    tick()
    mob = 0.0075 + (0.1425 / LAM) * q[3]
    six = 6.0 * mob
    rest = [total[i] - six * u[i] for i in range(2)]
    tick()
    local = []
    for a in range(4):
        local.append(q[a] * ((well + square[a]) + pull[a] * (LAM - q[a])))
        tick()
    mean = 0.25 * ((local[0] + local[1]) + (local[2] + local[3])) - 0.07 / BETA
    tick()
    y = [BETA * (local[a] - mean) for a in range(3)]
    tick()
    return q[:3] + u + y + rest + [mob]


def last_step(sums, y, rest, mob):
    held, inverse = clip_step(sums, y)
    p = [v * inverse for v in held]
    h = [v * v * (1.5 - v) for v in p]
    shared = 0.2 * ((h[0] + h[1]) + (h[2] + 3.5 * h[3]))
    total = [(rest[i] + mob * sums[3 + i]) * (1.0 / MU) for i in range(2)]
    return p, [(total[i] - shared) - 1.4 * h[i] for i in range(2)]


def lanes():
    return lax.broadcasted_iota(jnp.int32, (8, 128), 1)


def side_sums(state, near, row, low, at_left, at_right):
    slot, group = divmod(row, GROUPS)
    turn = 128 - (SLOT * slot + HALF // 2 + 1)
    sums = []
    for f in range(MOVING):
        v = state[f, row, pl.ds(low, 8), :]
        edge = pltpu.roll(near[f, group, pl.ds(low, 8), :], turn, 1)
        right = pltpu.roll(jnp.where(at_left, edge, v), 127, 1)
        left = pltpu.roll(jnp.where(at_right, edge, v), 1, 1)
        sums.append(right + left)
    return sums


def main_sums(state, row, low, sides):
    sums = []
    for f in range(MOVING):
        grow = state[f, row, pl.ds(low + 1, 8), :] + state[f, row, pl.ds(low - 1, 8), :]
        side = state[f, row + 1, pl.ds(low, 8), :] + state[f, row - 1, pl.ds(low, 8), :]
        sums.append((grow + side) + sides[f])
    return sums


def center(state, row, low):
    y = [state[MOVING + a, row, pl.ds(low, 8), :] for a in range(3)]
    rest = [state[MOVING + 3 + i, row, pl.ds(low, 8), :] for i in range(2)]
    return y, rest, state[FIELDS - 1, row, pl.ds(low, 8), :]


def near_of(v, swap):
    return jnp.where(swap, pltpu.roll(v, 128 - (HALF - 1), 1), v)


def front_kernel(
    plan, mesh_shape, levels, lab_hbm, pot_hbm, codes_hbm, table_hbm, out_state, out_near,
    lab, pot, codes, table, lab_up, pot_up, raw, pack, strip, across_pack, across, even, odd, even_near, odd_near, even_strip, odd_strip, out_strip, sides, strip_sides,
    in_sems, g_send, g_recv, y_send, y_recv, z_send, z_recv, a_send, a_recv,
):
    g, y, z = lax.axis_index("grow"), lax.axis_index("gy"), lax.axis_index("gz")
    count_g, count_y, count_z = mesh_shape
    rows, tall, planes, shift = plan.rows, plan.tall, plan.planes, plan.shift
    has_below, has_above = g > 0, g < count_g - 1
    is_first, is_last = g == 0, g == count_g - 1
    y_up, y_down = lax.rem(y + 1, count_y), lax.rem(y + count_y - 1, count_y)
    z_other = lax.rem(z + 1, count_z)
    chunks = plan.chunks
    own_chunks, lead, pieces = plan.own_chunks, plan.lead, plan.pieces

    loads = [
        pltpu.make_async_copy(lab_hbm, lab, in_sems.at[0]),
        pltpu.make_async_copy(pot_hbm, pot, in_sems.at[1]),
    ]
    melt_loads = [
        pltpu.make_async_copy(codes_hbm, codes, in_sems.at[2]),
        pltpu.make_async_copy(table_hbm, table, in_sems.at[3]),
    ]
    for copy in loads:
        copy.start()

    @pl.when(is_last)
    def _():
        for copy in melt_loads:
            copy.start()

    barrier = pltpu.get_barrier_semaphore()

    def greet(target):
        pl.semaphore_signal(barrier, inc=1, device_id=target, device_id_type=MESH)

    @pl.when(has_below)
    def _():
        greet((g - 1, y, z))

    @pl.when(has_above)
    def _():
        greet((g + 1, y, z))

    greet((g, y_up, z))
    greet((g, y_down, z))
    greet((g, y, z_other))
    greet((g, y_up, z_other))
    greet((g, y_down, z_other))

    splits = [max(8 * piece - lead, 0) for piece in range(pieces + 1)]

    def g_copies(piece):
        begin, end = splits[piece], splits[piece + 1]
        src, dst = pl.ds(begin * rows, (end - begin) * rows), pl.ds((lead + begin) * rows, (end - begin) * rows)
        copies = []
        for i in range(3):
            source, target = (lab_hbm.at[src], lab_up.at[dst]) if i == 0 else (pot_hbm.at[i - 1, src], pot_up.at[i - 1, dst])
            sem = 3 * piece + i
            copies.append(pltpu.make_async_remote_copy(
                src_ref=source, dst_ref=target, send_sem=g_send.at[sem], recv_sem=g_recv.at[sem],
                device_id=(g - 1, y, z), device_id_type=MESH))
        return copies

    def planes_of(chunk):
        return pl.ds(7, 1) if isinstance(chunk, int) and chunk == 0 else pl.ds(8 * chunk, 8)

    def either(chunk, action):
        pl.when(chunk == 0)(lambda: action(0))
        pl.when(chunk > 0)(lambda: action(chunk))

    def y_copies(chunk):
        copies = []
        for up in range(2):
            src, dst, target = (rows, 0, y_up) if up else (STEPS, STEPS + rows, y_down)
            sem = 2 * chunk + up
            at = planes_of(chunk)
            copies.append(pltpu.make_async_remote_copy(
                src_ref=raw.at[:, pl.ds(src, STEPS), at], dst_ref=raw.at[:, pl.ds(dst, STEPS), at],
                send_sem=y_send.at[sem], recv_sem=y_recv.at[sem],
                device_id=(g, target, z), device_id_type=MESH))
        return copies

    def z_copy(chunk):
        at = pl.ds(8 * chunk, 8)
        return pltpu.make_async_remote_copy(
            src_ref=pack.at[:, :, at], dst_ref=strip.at[:, :, at],
            send_sem=z_send.at[chunk], recv_sem=z_recv.at[chunk],
            device_id=(g, y, z_other), device_id_type=MESH)

    def across_copies(chunk):
        at = planes_of(chunk)
        copies = []
        for k, row in enumerate((y_up, y, y_down)):
            sem = 3 * chunk + k
            copies.append(pltpu.make_async_remote_copy(
                src_ref=across_pack.at[:, :, at], dst_ref=across.at[k, :, :, at],
                send_sem=a_send.at[sem], recv_sem=a_recv.at[sem],
                device_id=(g, row, z_other), device_id_type=MESH))
        return copies

    def fill(labels, pots, begin, to):
        for row in range(rows):
            at = pl.ds(begin * rows + row, 8, stride=rows)
            raw[0, STEPS + row, pl.ds(to, 8)] = labels[at].astype(jnp.float32)
            for i in range(2):
                raw[1 + i, STEPS + row, pl.ds(to, 8)] = pots[i, at]

    def send_y(chunk):
        for copy in y_copies(chunk):
            copy.start()

    lane = lanes()

    def pack_rows(target, chunk, source):
        at = pl.ds(8 * chunk, 8)

        def pack_field(i, carry):
            for group in range(GROUPS):
                packed = jnp.zeros((8, 128), jnp.float32)
                for slot in range(tall // GROUPS):
                    v = raw[i, source(GROUPS * slot + group), at]
                    first = SLOT * slot
                    packed = jnp.where(lane >= first, pltpu.roll(v, first + HALF // 2 + 1, 1), packed)
                    packed = jnp.where(lane >= first + HALF, pltpu.roll(v, first + HALF + HALF // 2, 1), packed)
                target[i, group, at] = packed
            return carry

        lax.fori_loop(0, 3, pack_field, 0)

    def row_across(row):
        return row + rows if row < STEPS else row - rows if row >= STEPS + rows else row

    def start_all(copies):
        for copy in copies:
            copy.start()

    def send_across(chunk, carry):
        pack_rows(across_pack, chunk, row_across)
        either(chunk, lambda k: start_all(across_copies(k)))
        return carry

    def wait_all(copies):
        for copy in copies:
            copy.wait_recv()

    def send_z(chunk):
        either(chunk, lambda k: wait_all(y_copies(k)))
        pack_rows(pack, chunk, lambda row: row)

        @pl.when(chunk >= own_chunks)
        def _():
            z_copy(chunk).start()

    def receive_z(chunk):
        @pl.when(chunk >= own_chunks)
        def _():
            z_copy(chunk).wait_recv()

        @pl.when(chunk < own_chunks)
        def _():
            either(chunk, lambda k: wait_all(across_copies(k)))
            at = pl.ds(8 * chunk, 8)
            for group in range(GROUPS):
                own, upper = -((group - STEPS) // GROUPS), -((group - STEPS - rows) // GROUPS)
                for i in range(3):
                    value = jnp.where(lane >= SLOT * own, across[1, i, group, at], across[0, i, group, at])
                    strip[i, group, at] = jnp.where(lane >= SLOT * upper, across[2, i, group, at], value)

    place = lane % SLOT
    from_other = (place < HALF // 2 + 1) | (place >= SLOT - HALF // 2 - 1)
    swap = place == HALF // 2 + 1
    at_left, at_right = lane == 0, lane == 127

    def unpack_row(state, slot, row, source, target):
        at = pl.ds(source, 8)
        new = phase_state(raw[0, row, at], [raw[1, row, at], raw[2, row, at]])
        for f in range(FIELDS):
            state[slot, f, row, pl.ds(target, 8)] = new[f]

    def unpack_strips(state, near, slot, source, target):
        at, to = pl.ds(source, 8), pl.ds(target, 8)
        for group in range(GROUPS):
            value = [jnp.where(from_other, strip[i, group, at], pack[i, group, at]) for i in range(3)]
            for f, v in zip(CODED_AT, phase_state(value[0], value[1:], True)):
                state[slot, f, group, to] = v
                if f < MOVING:
                    near[slot, f, group, to] = near_of(v, swap)

    def unpack(chunk):
        to = 8 * chunk

        def body(part, carry):
            rows_at = pl.ds(tall // GROUPS * part, tall // GROUPS)
            at = pl.ds(to, 8)
            new = phase_state(raw[0, rows_at, at], [raw[1, rows_at, at], raw[2, rows_at, at]], True)
            for f, v in zip(CODED_AT, new):
                even[0, f, rows_at, at] = v
            return carry

        lax.fori_loop(0, GROUPS, body, 0)
        unpack_strips(even_strip, even_near, 0, to, to)

    def strip_side_steps(fields, src, slot, low, result):
        at = pl.ds(low, 8)

        def piece(f):
            v = src[slot, f, :, at]
            part = [src[slot, f, group, at] for group in range(GROUPS)]
            up = jnp.stack([part[1], part[2], pltpu.roll(part[0], 128 - SLOT, 1)])
            down = jnp.stack([pltpu.roll(part[2], SLOT, 1), part[0], part[1]])
            result[f] = (up + down) + (pltpu.roll(v, 127, 2) + pltpu.roll(v, 1, 2))

        return [functools.partial(piece, f) for f in fields]

    def strip_step(step, src, src_slot, dst, near, dst_slot, low, around, tick):
        at = pl.ds(low, 8)
        sums = []
        for f in moving_of(step):
            total = src[src_slot, f, :, pl.ds(low + 1, 8)] + src[src_slot, f, :, pl.ds(low - 1, 8)]
            sums.append(total + around[f])
            tick()
        if step == 1:
            sums = decode(sums[0]) + sums[1:]
        y = [src[src_slot, MOVING + a, :, at] for a in range(3)]
        rest = [src[src_slot, MOVING + 3 + i, :, at] for i in range(2)]
        new = cell_step(sums, y, rest, src[src_slot, FIELDS - 1, :, at], tick)
        for f in range(FIELDS):
            dst[dst_slot, f, :, at] = new[f]
        for f in range(MOVING):
            near[dst_slot, f, :, at] = jnp.where(swap, pltpu.roll(new[f], 128 - (HALF - 1), 2), new[f])

    def side_steps(fields, state, near, first, count, low, result):
        v, edge, ends = {}, {}, {}

        def near_rolls(f):
            rolled = []
            for i in range(count):
                slot, group = divmod(first + i, GROUPS)
                rolled.append(pltpu.roll(near[f, group, pl.ds(low, 8), :], 128 - (SLOT * slot + HALF // 2 + 1), 1))
            edge[f] = jnp.stack(rolled)
            v[f] = state[f, first : first + count, pl.ds(low, 8), :]

        def z_rolls(f):
            right = pltpu.roll(jnp.where(at_left, edge[f], v[f]), 127, 2)
            left = pltpu.roll(jnp.where(at_right, edge[f], v[f]), 1, 2)
            ends[f] = (right, left)

        def add(f):
            result[f] = ends[f][0] + ends[f][1]

        pieces = []
        for k in range(len(fields) + 2 * LAG):
            if k < len(fields):
                pieces.append(functools.partial(near_rolls, fields[k]))
            if LAG <= k < len(fields) + LAG:
                pieces.append(functools.partial(z_rolls, fields[k - LAG]))
            if k >= 2 * LAG:
                pieces.append(functools.partial(add, fields[k - 2 * LAG]))
        return pieces

    class Ahead:
        def __init__(self, pieces=()):
            self.pieces = list(pieces)

        def __call__(self):
            if self.pieces:
                self.pieces.pop(0)()

        def flush(self):
            while self.pieces:
                self()

    def sizes_of(step):
        total = tall - 2 * step
        parts = -(-total // BATCH)
        return [total // parts + (k < total % parts) for k in range(parts)]

    def buffers(step):
        if step == STEPS - 1:
            return out_state, out_near, out_strip, 0
        if step % 2:
            return odd, odd_near, odd_strip, step // 2
        return even, even_near, even_strip, step // 2

    def begin_steps(stage, step, around, strip_around):
        state, near, strips, slot = buffers(step - 1)
        low = plan.low(stage, step)
        rows_ahead = side_steps(moving_of(step), state.at[slot], near.at[slot], step, sizes_of(step)[0], low, around)
        return rows_ahead, strip_side_steps(moving_of(step), strips, slot, low, strip_around)

    def keep(around, strip_around):
        for f in around:
            sides[: around[f].shape[0], f] = around[f]
            strip_sides[f] = strip_around[f]

    def begin(stage, step):
        around, strip_around = {}, {}
        rows_ahead, strips_ahead = begin_steps(stage, step, around, strip_around)
        for piece in strips_ahead + rows_ahead:
            piece()
        keep(around, strip_around)

    def row_steps(stage, step):
        src, src_near, src_strip, slot = buffers(step - 1)
        dst, dst_near, dst_strip, dst_slot = buffers(step)
        state, near = src.at[slot], src_near.at[slot]
        low = plan.low(stage, step)
        sizes = sizes_of(step)
        at = pl.ds(low, 8)
        ready, strip_ready = {}, {}
        if step == 1:
            rows_ahead, strips_ahead = begin_steps(stage, step, ready, strip_ready)
            Ahead(strips_ahead).flush()
            ahead = Ahead(rows_ahead)
        else:
            ready = {f: sides[: sizes[0], f] for f in moving_of(step)}
            strip_ready = {f: strip_sides[f] for f in moving_of(step)}
            ahead = Ahead()
        strip_step(step, src_strip, slot, dst_strip, dst_near, dst_slot, low, strip_ready, ahead)
        ahead.flush()
        row = step
        for k, size in enumerate(sizes):
            around, ready, strip_ready = ready, {}, {}
            if k + 1 < len(sizes):
                ahead = Ahead(side_steps(moving_of(step), state, near, row + size, sizes[k + 1], low, ready))
            elif step < STEPS - 1:
                rows_ahead, strips_ahead = begin_steps(stage, step + 1, ready, strip_ready)
                ahead = Ahead(strips_ahead + rows_ahead)

            def rows_of(f, shift=0, up=0):
                return state[f, row + shift : row + shift + size, pl.ds(low + up, 8), :]

            sums = []
            for f in moving_of(step):
                grow = rows_of(f, 0, 1) + rows_of(f, 0, -1)
                side = rows_of(f, 1) + rows_of(f, -1)
                sums.append((grow + side) + around[f])
                ahead()
            if step == 1:
                sums = decode(sums[0]) + sums[1:]
            y = [rows_of(MOVING + a) for a in range(3)]
            rest = [rows_of(MOVING + 3 + i) for i in range(2)]
            new = cell_step(sums, y, rest, rows_of(FIELDS - 1), ahead)
            ahead.flush()
            for f in range(FIELDS):
                dst[dst_slot, f, row : row + size, at, :] = new[f]
            row += size
        if step < STEPS - 1:
            keep(ready, strip_ready)

    def copy_plane(state, strips, near, slot, source, target):
        src, dst = pl.ds(source, 1), pl.ds(target, 1)

        def body(row, carry):
            for f in range(MOVING):
                state[slot, f, row, dst] = state[slot, f, row, src]
            return carry

        lax.fori_loop(0, tall, body, 0)
        for group in range(GROUPS):
            for f in range(MOVING):
                strips[slot, f, group, dst] = strips[slot, f, group, src]
                near[slot, f, group, dst] = near[slot, f, group, src]

    first_plane, top_plane = plan.at(shift), plan.at(planes)
    last_plane = first_plane + planes - 1
    place_up = lax.broadcasted_iota(jnp.int32, (8, 128), 0)

    def melt_fill(stage):
        source, target = 8 * stage + 8, 8 * stage + 7
        melt = place_up >= top_plane - target
        at, to = pl.ds(source, 8), pl.ds(target, 8)

        def body(row, carry):
            new = phase_state(raw[0, row, at], [raw[1, row, at], raw[2, row, at]])
            for f in range(FIELDS):
                pltpu.store(odd.at[1, f, row, to], new[f], mask=melt)
            return carry

        lax.fori_loop(STEPS_BEFORE, tall - STEPS_BEFORE, body, 0)
        for group in range(GROUPS):
            value = [jnp.where(from_other, strip[i, group, at], pack[i, group, at]) for i in range(3)]
            new = phase_state(value[0], value[1:])
            for f in range(FIELDS):
                pltpu.store(odd_strip.at[1, f, group, to], new[f], mask=melt)
            for f in range(MOVING):
                pltpu.store(odd_near.at[1, f, group, to], near_of(new[f], swap), mask=melt)

    def stage_of(plane, step):
        return (plane - plan.low(0, step)) // 8

    def compute(stage):
        top = stage_of(top_plane, STEPS_BEFORE)
        below_melt = (stage <= top) | jnp.logical_not(is_last)

        for step in range(1, STEPS):
            state, near, strips, slot = buffers(step)
            out = (state, strips, near, slot)

            if step <= STEPS_BEFORE:
                pl.when(below_melt)(functools.partial(row_steps, stage, step))
            else:
                row_steps(stage, step)

            if step < STEPS_BEFORE:
                @pl.when(is_last & (stage == stage_of(top_plane, step)))
                def _():
                    copy_plane(*out, top_plane - 1, top_plane)
            else:
                @pl.when(is_first & (stage == stage_of(first_plane, step)))
                def _():
                    copy_plane(*out, first_plane, first_plane - 1)

            if step == 2:
                pass_on(stage)

            if step == STEPS_BEFORE:
                @pl.when(is_last & (stage >= top))
                def _():
                    melt_fill(stage)
                    begin(stage, step + 1)

            if step == STEPS - 1:
                @pl.when(is_last & (stage == stage_of(last_plane, step)))
                def _():
                    copy_plane(*out, last_plane, last_plane + 1)

    pl.semaphore_wait(barrier, 5 + has_below.astype(jnp.int32) + has_above.astype(jnp.int32))

    @pl.when(has_below)
    def _():
        for piece in range(pieces):
            for copy in g_copies(piece):
                copy.start()

    for copy in loads:
        copy.wait()

    def fill_own(chunk, carry):
        fill(lab, pot, plan.base + 8 * chunk, 8 * chunk)
        either(chunk, send_y)
        return carry

    lax.fori_loop(0, own_chunks, fill_own, 0)
    lax.fori_loop(0, own_chunks, send_across, 0)
    tail = pl.ds((planes - lead) * rows, lead * rows)
    lab_up[0 : lead * rows] = lab[tail]
    for i in range(2):
        pot_up[i, 0 : lead * rows] = pot[i, tail]

    @pl.when(is_last)
    def _():
        for copy in melt_loads:
            copy.wait()
        plane = pl.ds((planes - 1) * rows, rows)
        at = pl.ds(lead * rows, rows)
        lab_up[at] = lab[plane]
        for i in range(2):
            pot_up[i, at] = pot[i, plane]

        def melt_plane(k, carry):
            code = codes[pl.ds(pl.multiple_of(jnp.minimum(k, shift - 1) * rows, rows), rows)]
            at = pl.ds(pl.multiple_of((lead + 1 + k) * rows, rows), rows)
            lab_up[at] = jnp.full((rows, 128), 3, jnp.int32)
            for i in range(2):
                value = jnp.zeros((rows, 128), jnp.float32)
                for level in range(levels):
                    value = jnp.where(code == level, table[i, level], value)
                pot_up[i, at] = value
            return carry

        lax.fori_loop(0, 8 * pieces - lead - 1, melt_plane, 0)

    def z_body(chunk, carry):
        send_z(chunk)
        return carry

    def pass_on(stage):
        @pl.when(stage == 0)
        def _():
            take(pieces)

        @pl.when(stage == 1)
        def _():
            lax.fori_loop(own_chunks + 1, chunks, z_body, 0)

    def beat(it, carry):
        lax.fori_loop(jnp.where(it == 3, 2, it), jnp.where(it == 3, 4, jnp.where(it < 2, it + 1, it)), z_body, 0)

        @pl.when((it == 0) | ((it >= 2) & (it < pieces)))
        def _():
            take(it)

        @pl.when(it >= 1)
        def _():
            receive_z(it - 1)
            unpack(it - 1)

        @pl.when(it >= 2)
        def _():
            compute(it - 2)

        return carry

    def take(it):
        piece = jnp.maximum(it - 1, 0)
        for k in range(pieces):
            @pl.when(has_above & (piece == k))
            def _():
                for copy in g_copies(k):
                    copy.wait_recv()

        fill(lab_up, pot_up, 8 * piece, 8 * (own_chunks + piece))
        send_y(own_chunks + piece)

    lax.fori_loop(0, plan.stages + 2, beat, 0)

    def drain(chunk, carry):
        def wait(copies):
            for copy in copies:
                copy.wait_send()

        either(chunk, lambda k: wait(y_copies(k)))

        @pl.when(chunk >= own_chunks)
        def _():
            z_copy(chunk).wait_send()

        @pl.when(chunk < own_chunks)
        def _():
            either(chunk, lambda k: wait(across_copies(k)))

        return carry

    lax.fori_loop(0, chunks, drain, 0)

    @pl.when(has_below)
    def _():
        for piece in range(pieces):
            for copy in g_copies(piece):
                copy.wait_send()


def last_kernel(plan, state, near, phases, potentials, p_out, m_out, sems):
    rows, planes = plan.rows, plan.planes
    at_left, at_right = lanes() == 0, lanes() == 127
    begin, tiles = plan.at(plan.shift), planes // 8

    def out_copies(tile):
        at = pl.ds(8 * tile * rows, 8 * rows)
        return [
            pltpu.make_async_copy(src.at[:, at], dst.at[:, at], sems.at[2 * tile + i])
            for i, (src, dst) in enumerate(((p_out, phases), (m_out, potentials)))
        ]

    def body(tile, carry):
        low = begin + 8 * tile
        for row in range(rows):
            src = state.at[0]
            sums = main_sums(src, STEPS + row, low, side_sums(src, near.at[0], STEPS + row, low, at_left, at_right))
            p, m = last_step(sums, *center(src, STEPS + row, low))
            at = pl.ds(8 * tile * rows + row, 8, stride=rows)
            for f in range(4):
                p_out[f, at, :] = p[f]
            for i in range(2):
                m_out[i, at, :] = m[i]
        for copy in out_copies(tile):
            copy.start()
        return carry

    lax.fori_loop(0, tiles, body, 0)
    for tile in range(tiles):
        for copy in out_copies(tile):
            copy.wait()


def on_device(mesh_shape, labels, potential, melt_codes, melt_table):
    planes, rows, width = labels.shape
    shift, levels = melt_codes.shape[0], melt_table.shape[1]
    plan = Plan(planes, rows, shift)
    flat = planes * rows
    vmem = pl.BlockSpec(memory_space=pltpu.VMEM)
    hbm = pl.BlockSpec(memory_space=pltpu.HBM)
    f32 = jnp.float32
    dma = pltpu.SemaphoreType.DMA
    deep, tall, chunks = plan.deep, plan.tall, plan.chunks
    evens, odds = STEPS // 2, STEPS // 2
    upper = 8 * plan.pieces * rows
    kept = (FIELDS * tall + MOVING * GROUPS) * deep * width * 4
    state, near = pl.pallas_call(
        functools.partial(front_kernel, plan, mesh_shape, levels),
        out_shape=(
            pltpu.VMEM((1, FIELDS, tall, deep, width), f32),
            pltpu.VMEM((1, MOVING, GROUPS, deep, width), f32),
        ),
        in_specs=[hbm, hbm, hbm, hbm],
        out_specs=(vmem, vmem),
        scratch_shapes=[
            pltpu.VMEM((flat, width), jnp.int32),
            pltpu.VMEM((2, flat, width), f32),
            pltpu.VMEM((shift * rows, width), jnp.int32),
            pltpu.SMEM((2, levels), f32),
            pltpu.VMEM((upper, width), jnp.int32),
            pltpu.VMEM((2, upper, width), f32),
            pltpu.VMEM((3, tall, deep, width), f32),
            pltpu.VMEM((3, GROUPS, deep, width), f32),
            pltpu.VMEM((3, GROUPS, deep, width), f32),
            pltpu.VMEM((3, GROUPS, 8 * plan.own_chunks, width), f32),
            pltpu.VMEM((3, 3, GROUPS, 8 * plan.own_chunks, width), f32),
            pltpu.VMEM((evens, FIELDS, tall, deep, width), f32),
            pltpu.VMEM((odds, FIELDS, tall, deep, width), f32),
            pltpu.VMEM((evens, MOVING, GROUPS, deep, width), f32),
            pltpu.VMEM((odds, MOVING, GROUPS, deep, width), f32),
            pltpu.VMEM((evens, FIELDS, GROUPS, deep, width), f32),
            pltpu.VMEM((odds, FIELDS, GROUPS, deep, width), f32),
            pltpu.VMEM((1, FIELDS, GROUPS, deep, width), f32),
            pltpu.VMEM((BATCH, MOVING, 8, width), f32),
            pltpu.VMEM((MOVING, GROUPS, 8, width), f32),
            dma((4,)), dma((3 * chunks,)), dma((3 * chunks,)),
            dma((2 * chunks,)), dma((2 * chunks,)), dma((chunks,)), dma((chunks,)),
            dma((3 * plan.own_chunks,)), dma((3 * plan.own_chunks,)),
        ],
        compiler_params=pltpu.CompilerParams(collective_id=0, has_side_effects=True, vmem_limit_bytes=(VMEM_BYTES - kept) // 4096 * 4096),
        name="front",
    )(labels.reshape(flat, width), potential.reshape(2, flat, width), melt_codes.reshape(shift * rows, width), melt_table)
    state, near = (pltpu.with_memory_space_constraint(v, pltpu.VMEM) for v in (state, near))
    phases, potentials = pl.pallas_call(
        functools.partial(last_kernel, plan),
        out_shape=(
            jax.ShapeDtypeStruct((4, flat, width), f32),
            jax.ShapeDtypeStruct((2, flat, width), f32),
        ),
        in_specs=[vmem, vmem],
        out_specs=(hbm, hbm),
        scratch_shapes=[
            pltpu.VMEM((4, flat, width), f32),
            pltpu.VMEM((2, flat, width), f32),
            dma((2 * (planes // 8),)),
        ],
        compiler_params=pltpu.CompilerParams(vmem_limit_bytes=8 << 20),
        name="last",
    )(state, near)
    return phases.reshape(4, planes, rows, width), potentials.reshape(2, planes, rows, width)


def solution(mesh):
    mesh_shape = tuple(mesh.shape[axis] for axis in ("grow", "gy", "gz"))
    return jax.shard_map(
        functools.partial(on_device, mesh_shape),
        mesh=mesh,
        in_specs=(P("grow", "gy", "gz"), P(None, "grow", "gy", "gz"), P(None, "gy", "gz"), P()),
        out_specs=(P(None, "grow", "gy", "gz"), P(None, "grow", "gy", "gz")),
        check_vma=False,
    )
```

```python
import functools

import jax
import jax.numpy as jnp
from jax import lax
from jax.experimental import pallas as pl
from jax.experimental.pallas import tpu as pltpu
from jax.sharding import PartitionSpec as P

STEPS_BEFORE = 3
STEPS_AFTER = 2
STEPS = STEPS_BEFORE + STEPS_AFTER
HALF = 9
SLOT = 2 * HALF
GROUPS = 3
LAG = 5
HOOK = 2
BATCH = 8
FIELDS = 11
MOVING = 5
CODE = 16.0
CODED_AT = (0,) + tuple(range(3, FIELDS))
VMEM_BYTES = 67043328
MESH = pl.DeviceIdType.MESH

LAM = 0.12
BETA = 5.0 / LAM**2
MU = 17.5 / (LAM * BETA)
OWN = (1.0 / LAM - 6.0) / BETA
TILT = 1.25 / (LAM * BETA)
BACK = 0.2 * MU / LAM**3


class Plan:
    def __init__(self, planes, rows, shift):
        self.planes, self.rows, self.shift = planes, rows, shift
        self.base = shift - STEPS + 2 - 8
        self.chunks = planes // 8 + 2
        self.stages = self.chunks - 1
        self.deep = 8 * self.chunks
        self.above = shift + STEPS
        self.tall = rows + 2 * STEPS
        self.own_chunks, self.lead = divmod(planes - self.base, 8)
        self.pieces = self.chunks - self.own_chunks

    def at(self, plane):
        return plane - self.base

    def low(self, stage, step):
        return 8 + 8 * stage - step


def phase_state(label, pot, coded=False):
    if coded:
        q = [jnp.where(label == 0.0, 1.0, jnp.where(label == 1.0, CODE, jnp.where(label == 2.0, CODE * CODE, 0.0)))]
    else:
        q = [jnp.where(label == float(a), LAM, 0.0) for a in range(3)]
    y = [jnp.where(label == float(a), LAM * BETA * OWN, 0.0) for a in range(3)]
    liquid = label == 3.0
    mob = jnp.where(liquid, 0.15, 0.0075)
    u = [MU * v for v in pot]
    comp = [jnp.where(liquid, 0.35 * MU, jnp.where(label == float(i), 0.8 * MU, 0.1 * MU)) for i in range(2)]
    rest = [(u[i] + comp[i]) - (6.0 * mob) * u[i] for i in range(2)]
    return q + u + y + rest + [mob]


def decode(total):
    third = jnp.floor(total * (1.0 / (CODE * CODE)))
    total = total - (CODE * CODE) * third
    second = jnp.floor(total * (1.0 / CODE))
    return [LAM * v for v in (total - CODE * second, second, third)]


def moving_of(step):
    return (0, 3, 4) if step == 1 else tuple(range(MOVING))


def clip_step(sums, y):
    x = [sums[a] + y[a] for a in range(3)]
    x.append(1.0 - (x[0] + x[1] + x[2]))
    held = [jnp.clip(v, 0.0, 1.0) for v in x]
    return held, 1.0 / ((held[0] + held[1]) + (held[2] + held[3]))


def cell_step(sums, y, rest, mob, tick=lambda: None):
    held, inverse = clip_step(sums, y)
    tick()
    total = [rest[i] + mob * sums[3 + i] for i in range(2)]
    tick()
    scaled = LAM * inverse
    q = [v * scaled for v in held]
    tick()
    square = [v * v for v in q]
    tick()
    h = [square[a] * (1.5 * LAM - q[a]) for a in range(4)]
    tick()
    shared = BACK * ((h[0] + h[1]) + (h[2] + 3.5 * h[3]))
    tick()
    u = [(total[i] - shared) - (7.0 * BACK) * h[i] for i in range(2)]
    tick()
    both = u[0] + u[1]
    well = OWN - ((square[0] + square[1]) + (square[2] + square[3]))
    tick()
    third = both * (1.0 / 7.0) + TILT
    pull = [third + u[0], third + u[1], third, 0.5 * both]
    tick()
    mob = 0.0075 + (0.1425 / LAM) * q[3]
    six = 6.0 * mob
    rest = [total[i] - six * u[i] for i in range(2)]
    tick()
    local = []
    for a in range(4):
        local.append(q[a] * ((well + square[a]) + pull[a] * (LAM - q[a])))
        tick()
    mean = 0.25 * ((local[0] + local[1]) + (local[2] + local[3])) - 0.07 / BETA
    tick()
    y = [BETA * (local[a] - mean) for a in range(3)]
    tick()
    return q[:3] + u + y + rest + [mob]


def last_step(sums, y, rest, mob):
    held, inverse = clip_step(sums, y)
    p = [v * inverse for v in held]
    h = [v * v * (1.5 - v) for v in p]
    shared = 0.2 * ((h[0] + h[1]) + (h[2] + 3.5 * h[3]))
    total = [(rest[i] + mob * sums[3 + i]) * (1.0 / MU) for i in range(2)]
    return p, [(total[i] - shared) - 1.4 * h[i] for i in range(2)]


def lanes():
    return lax.broadcasted_iota(jnp.int32, (8, 128), 1)


def side_sums(state, near, row, low, at_left, at_right):
    slot, group = divmod(row, GROUPS)
    turn = 128 - (SLOT * slot + HALF // 2 + 1)
    sums = []
    for f in range(MOVING):
        v = state[f, row, pl.ds(low, 8), :]
        edge = pltpu.roll(near[f, group, pl.ds(low, 8), :], turn, 1)
        right = pltpu.roll(jnp.where(at_left, edge, v), 127, 1)
        left = pltpu.roll(jnp.where(at_right, edge, v), 1, 1)
        sums.append(right + left)
    return sums


def main_sums(state, row, low, sides):
    sums = []
    for f in range(MOVING):
        grow = state[f, row, pl.ds(low + 1, 8), :] + state[f, row, pl.ds(low - 1, 8), :]
        side = state[f, row + 1, pl.ds(low, 8), :] + state[f, row - 1, pl.ds(low, 8), :]
        sums.append((grow + side) + sides[f])
    return sums


def center(state, row, low):
    y = [state[MOVING + a, row, pl.ds(low, 8), :] for a in range(3)]
    rest = [state[MOVING + 3 + i, row, pl.ds(low, 8), :] for i in range(2)]
    return y, rest, state[FIELDS - 1, row, pl.ds(low, 8), :]


def near_of(v, swap):
    return jnp.where(swap, pltpu.roll(v, 128 - (HALF - 1), 1), v)


def front_kernel(
    plan, mesh_shape, levels, lab_hbm, pot_hbm, codes_hbm, table_hbm, out_state, out_near,
    lab, pot, codes, table, lab_up, pot_up, raw, pack, strip, across_pack, across, even, odd, even_near, odd_near, even_strip, odd_strip, out_strip, sides, strip_sides,
    in_sems, g_send, g_recv, y_send, y_recv, z_send, z_recv, a_send, a_recv,
):
    g, y, z = lax.axis_index("grow"), lax.axis_index("gy"), lax.axis_index("gz")
    count_g, count_y, count_z = mesh_shape
    rows, tall, planes, shift = plan.rows, plan.tall, plan.planes, plan.shift
    has_below, has_above = g > 0, g < count_g - 1
    is_first, is_last = g == 0, g == count_g - 1
    y_up, y_down = lax.rem(y + 1, count_y), lax.rem(y + count_y - 1, count_y)
    z_other = lax.rem(z + 1, count_z)
    chunks = plan.chunks
    own_chunks, lead, pieces = plan.own_chunks, plan.lead, plan.pieces

    loads = [
        pltpu.make_async_copy(lab_hbm, lab, in_sems.at[0]),
        pltpu.make_async_copy(pot_hbm, pot, in_sems.at[1]),
    ]
    melt_loads = [
        pltpu.make_async_copy(codes_hbm, codes, in_sems.at[2]),
        pltpu.make_async_copy(table_hbm, table, in_sems.at[3]),
    ]
    for copy in loads:
        copy.start()

    @pl.when(is_last)
    def _():
        for copy in melt_loads:
            copy.start()

    barrier = pltpu.get_barrier_semaphore()

    def greet(target):
        pl.semaphore_signal(barrier, inc=1, device_id=target, device_id_type=MESH)

    @pl.when(has_below)
    def _():
        greet((g - 1, y, z))

    @pl.when(has_above)
    def _():
        greet((g + 1, y, z))

    greet((g, y_up, z))
    greet((g, y_down, z))
    greet((g, y, z_other))
    greet((g, y_up, z_other))
    greet((g, y_down, z_other))

    splits = [max(8 * piece - lead, 0) for piece in range(pieces + 1)]

    def g_copies(piece):
        begin, end = splits[piece], splits[piece + 1]
        src, dst = pl.ds(begin * rows, (end - begin) * rows), pl.ds((lead + begin) * rows, (end - begin) * rows)
        copies = []
        for i in range(3):
            source, target = (lab_hbm.at[src], lab_up.at[dst]) if i == 0 else (pot_hbm.at[i - 1, src], pot_up.at[i - 1, dst])
            sem = 3 * piece + i
            copies.append(pltpu.make_async_remote_copy(
                src_ref=source, dst_ref=target, send_sem=g_send.at[sem], recv_sem=g_recv.at[sem],
                device_id=(g - 1, y, z), device_id_type=MESH))
        return copies

    def planes_of(chunk):
        return pl.ds(7, 1) if isinstance(chunk, int) and chunk == 0 else pl.ds(8 * chunk, 8)

    def either(chunk, action):
        pl.when(chunk == 0)(lambda: action(0))
        pl.when(chunk > 0)(lambda: action(chunk))

    def y_copies(chunk):
        copies = []
        for up in range(2):
            src, dst, target = (rows, 0, y_up) if up else (STEPS, STEPS + rows, y_down)
            sem = 2 * chunk + up
            at = planes_of(chunk)
            copies.append(pltpu.make_async_remote_copy(
                src_ref=raw.at[:, pl.ds(src, STEPS), at], dst_ref=raw.at[:, pl.ds(dst, STEPS), at],
                send_sem=y_send.at[sem], recv_sem=y_recv.at[sem],
                device_id=(g, target, z), device_id_type=MESH))
        return copies

    def z_copy(chunk):
        at = pl.ds(8 * chunk, 8)
        return pltpu.make_async_remote_copy(
            src_ref=pack.at[:, :, at], dst_ref=strip.at[:, :, at],
            send_sem=z_send.at[chunk], recv_sem=z_recv.at[chunk],
            device_id=(g, y, z_other), device_id_type=MESH)

    def across_copies(chunk):
        at = planes_of(chunk)
        copies = []
        for k, row in enumerate((y_up, y, y_down)):
            sem = 3 * chunk + k
            copies.append(pltpu.make_async_remote_copy(
                src_ref=across_pack.at[:, :, at], dst_ref=across.at[k, :, :, at],
                send_sem=a_send.at[sem], recv_sem=a_recv.at[sem],
                device_id=(g, row, z_other), device_id_type=MESH))
        return copies

    def fill(labels, pots, begin, to):
        for row in range(rows):
            at = pl.ds(begin * rows + row, 8, stride=rows)
            raw[0, STEPS + row, pl.ds(to, 8)] = labels[at].astype(jnp.float32)
            for i in range(2):
                raw[1 + i, STEPS + row, pl.ds(to, 8)] = pots[i, at]

    def send_y(chunk):
        for copy in y_copies(chunk):
            copy.start()

    lane = lanes()

    def pack_rows(target, chunk, source):
        at = pl.ds(8 * chunk, 8)

        def pack_field(i, carry):
            for group in range(GROUPS):
                packed = jnp.zeros((8, 128), jnp.float32)
                for slot in range(tall // GROUPS):
                    v = raw[i, source(GROUPS * slot + group), at]
                    first = SLOT * slot
                    packed = jnp.where(lane >= first, pltpu.roll(v, first + HALF // 2 + 1, 1), packed)
                    packed = jnp.where(lane >= first + HALF, pltpu.roll(v, first + HALF + HALF // 2, 1), packed)
                target[i, group, at] = packed
            return carry

        lax.fori_loop(0, 3, pack_field, 0)

    def row_across(row):
        return row + rows if row < STEPS else row - rows if row >= STEPS + rows else row

    def start_all(copies):
        for copy in copies:
            copy.start()

    def send_across(chunk, carry):
        pack_rows(across_pack, chunk, row_across)
        either(chunk, lambda k: start_all(across_copies(k)))
        return carry

    def wait_all(copies):
        for copy in copies:
            copy.wait_recv()

    def send_z(chunk):
        either(chunk, lambda k: wait_all(y_copies(k)))
        pack_rows(pack, chunk, lambda row: row)

        @pl.when(chunk >= own_chunks)
        def _():
            z_copy(chunk).start()

    def receive_z(chunk):
        @pl.when(chunk >= own_chunks)
        def _():
            z_copy(chunk).wait_recv()

        @pl.when(chunk < own_chunks)
        def _():
            either(chunk, lambda k: wait_all(across_copies(k)))
            at = pl.ds(8 * chunk, 8)
            for group in range(GROUPS):
                own, upper = -((group - STEPS) // GROUPS), -((group - STEPS - rows) // GROUPS)
                for i in range(3):
                    value = jnp.where(lane >= SLOT * own, across[1, i, group, at], across[0, i, group, at])
                    strip[i, group, at] = jnp.where(lane >= SLOT * upper, across[2, i, group, at], value)

    place = lane % SLOT
    from_other = (place < HALF // 2 + 1) | (place >= SLOT - HALF // 2 - 1)
    swap = place == HALF // 2 + 1
    at_left, at_right = lane == 0, lane == 127

    def unpack_row(state, slot, row, source, target):
        at = pl.ds(source, 8)
        new = phase_state(raw[0, row, at], [raw[1, row, at], raw[2, row, at]])
        for f in range(FIELDS):
            state[slot, f, row, pl.ds(target, 8)] = new[f]

    def unpack_strips(state, near, slot, source, target):
        at, to = pl.ds(source, 8), pl.ds(target, 8)
        for group in range(GROUPS):
            value = [jnp.where(from_other, strip[i, group, at], pack[i, group, at]) for i in range(3)]
            for f, v in zip(CODED_AT, phase_state(value[0], value[1:], True)):
                state[slot, f, group, to] = v
                if f < MOVING:
                    near[slot, f, group, to] = near_of(v, swap)

    def unpack(chunk):
        to = 8 * chunk

        def body(part, carry):
            rows_at = pl.ds(tall // GROUPS * part, tall // GROUPS)
            at = pl.ds(to, 8)
            new = phase_state(raw[0, rows_at, at], [raw[1, rows_at, at], raw[2, rows_at, at]], True)
            for f, v in zip(CODED_AT, new):
                even[0, f, rows_at, at] = v
            return carry

        lax.fori_loop(0, GROUPS, body, 0)
        unpack_strips(even_strip, even_near, 0, to, to)

    def strip_side_steps(fields, src, slot, low, result):
        at = pl.ds(low, 8)

        def piece(f):
            v = src[slot, f, :, at]
            part = [src[slot, f, group, at] for group in range(GROUPS)]
            up = jnp.stack([part[1], part[2], pltpu.roll(part[0], 128 - SLOT, 1)])
            down = jnp.stack([pltpu.roll(part[2], SLOT, 1), part[0], part[1]])
            result[f] = (up + down) + (pltpu.roll(v, 127, 2) + pltpu.roll(v, 1, 2))

        return [functools.partial(piece, f) for f in fields]

    def strip_step(step, src, src_slot, dst, near, dst_slot, low, around, tick):
        at = pl.ds(low, 8)
        sums = []
        for f in moving_of(step):
            total = src[src_slot, f, :, pl.ds(low + 1, 8)] + src[src_slot, f, :, pl.ds(low - 1, 8)]
            sums.append(total + around[f])
            tick()
        if step == 1:
            sums = decode(sums[0]) + sums[1:]
        y = [src[src_slot, MOVING + a, :, at] for a in range(3)]
        rest = [src[src_slot, MOVING + 3 + i, :, at] for i in range(2)]
        new = cell_step(sums, y, rest, src[src_slot, FIELDS - 1, :, at], tick)
        for f in range(FIELDS):
            dst[dst_slot, f, :, at] = new[f]
        for f in range(MOVING):
            near[dst_slot, f, :, at] = jnp.where(swap, pltpu.roll(new[f], 128 - (HALF - 1), 2), new[f])

    def side_steps(fields, state, near, first, count, low, result):
        v, edge, ends = {}, {}, {}

        def near_rolls(f):
            rolled = []
            for i in range(count):
                slot, group = divmod(first + i, GROUPS)
                rolled.append(pltpu.roll(near[f, group, pl.ds(low, 8), :], 128 - (SLOT * slot + HALF // 2 + 1), 1))
            edge[f] = jnp.stack(rolled)
            v[f] = state[f, first : first + count, pl.ds(low, 8), :]

        def z_rolls(f):
            right = pltpu.roll(jnp.where(at_left, edge[f], v[f]), 127, 2)
            left = pltpu.roll(jnp.where(at_right, edge[f], v[f]), 1, 2)
            ends[f] = (right, left)

        def add(f):
            result[f] = ends[f][0] + ends[f][1]

        pieces = []
        for k in range(len(fields) + 2 * LAG):
            if k < len(fields):
                pieces.append(functools.partial(near_rolls, fields[k]))
            if LAG <= k < len(fields) + LAG:
                pieces.append(functools.partial(z_rolls, fields[k - LAG]))
            if k >= 2 * LAG:
                pieces.append(functools.partial(add, fields[k - 2 * LAG]))
        return pieces

    class Ahead:
        def __init__(self, pieces=()):
            self.pieces = list(pieces)

        def __call__(self):
            if self.pieces:
                self.pieces.pop(0)()

        def flush(self):
            while self.pieces:
                self()

    def sizes_of(step):
        total = tall - 2 * step
        parts = -(-total // BATCH)
        return [total // parts + (k < total % parts) for k in range(parts)]

    def buffers(step):
        if step == STEPS - 1:
            return out_state, out_near, out_strip, 0
        if step % 2:
            return odd, odd_near, odd_strip, step // 2
        return even, even_near, even_strip, step // 2

    def begin_steps(stage, step, around, strip_around):
        state, near, strips, slot = buffers(step - 1)
        low = plan.low(stage, step)
        rows_ahead = side_steps(moving_of(step), state.at[slot], near.at[slot], step, sizes_of(step)[0], low, around)
        return rows_ahead, strip_side_steps(moving_of(step), strips, slot, low, strip_around)

    def keep(around, strip_around):
        for f in around:
            sides[: around[f].shape[0], f] = around[f]
            strip_sides[f] = strip_around[f]

    def begin(stage, step):
        around, strip_around = {}, {}
        rows_ahead, strips_ahead = begin_steps(stage, step, around, strip_around)
        for piece in strips_ahead + rows_ahead:
            piece()
        keep(around, strip_around)

    def row_steps(stage, step):
        src, src_near, src_strip, slot = buffers(step - 1)
        dst, dst_near, dst_strip, dst_slot = buffers(step)
        state, near = src.at[slot], src_near.at[slot]
        low = plan.low(stage, step)
        sizes = sizes_of(step)
        at = pl.ds(low, 8)
        ready, strip_ready = {}, {}
        if step == 1:
            rows_ahead, strips_ahead = begin_steps(stage, step, ready, strip_ready)
            Ahead(strips_ahead).flush()
            ahead = Ahead(rows_ahead)
        else:
            ready = {f: sides[: sizes[0], f] for f in moving_of(step)}
            strip_ready = {f: strip_sides[f] for f in moving_of(step)}
            ahead = Ahead()
        strip_step(step, src_strip, slot, dst_strip, dst_near, dst_slot, low, strip_ready, ahead)
        ahead.flush()
        row = step
        for k, size in enumerate(sizes):
            around, ready, strip_ready = ready, {}, {}
            if k + 1 < len(sizes):
                ahead = Ahead(side_steps(moving_of(step), state, near, row + size, sizes[k + 1], low, ready))
            elif step < STEPS - 1:
                rows_ahead, strips_ahead = begin_steps(stage, step + 1, ready, strip_ready)
                ahead = Ahead(strips_ahead + rows_ahead)

            def rows_of(f, shift=0, up=0):
                return state[f, row + shift : row + shift + size, pl.ds(low + up, 8), :]

            sums = []
            for f in moving_of(step):
                grow = rows_of(f, 0, 1) + rows_of(f, 0, -1)
                side = rows_of(f, 1) + rows_of(f, -1)
                sums.append((grow + side) + around[f])
                ahead()
            if step == 1:
                sums = decode(sums[0]) + sums[1:]
            y = [rows_of(MOVING + a) for a in range(3)]
            rest = [rows_of(MOVING + 3 + i) for i in range(2)]
            new = cell_step(sums, y, rest, rows_of(FIELDS - 1), ahead)
            ahead.flush()
            for f in range(FIELDS):
                dst[dst_slot, f, row : row + size, at, :] = new[f]
            row += size
        if step < STEPS - 1:
            keep(ready, strip_ready)

    def copy_plane(state, strips, near, slot, source, target):
        src, dst = pl.ds(source, 1), pl.ds(target, 1)

        def body(row, carry):
            for f in range(MOVING):
                state[slot, f, row, dst] = state[slot, f, row, src]
            return carry

        lax.fori_loop(0, tall, body, 0)
        for group in range(GROUPS):
            for f in range(MOVING):
                strips[slot, f, group, dst] = strips[slot, f, group, src]
                near[slot, f, group, dst] = near[slot, f, group, src]

    first_plane, top_plane = plan.at(shift), plan.at(planes)
    last_plane = first_plane + planes - 1
    place_up = lax.broadcasted_iota(jnp.int32, (8, 128), 0)

    def melt_fill(stage):
        source, target = 8 * stage + 8, 8 * stage + 7
        melt = place_up >= top_plane - target
        at, to = pl.ds(source, 8), pl.ds(target, 8)

        def body(row, carry):
            new = phase_state(raw[0, row, at], [raw[1, row, at], raw[2, row, at]])
            for f in range(FIELDS):
                pltpu.store(odd.at[1, f, row, to], new[f], mask=melt)
            return carry

        lax.fori_loop(STEPS_BEFORE, tall - STEPS_BEFORE, body, 0)
        for group in range(GROUPS):
            value = [jnp.where(from_other, strip[i, group, at], pack[i, group, at]) for i in range(3)]
            new = phase_state(value[0], value[1:])
            for f in range(FIELDS):
                pltpu.store(odd_strip.at[1, f, group, to], new[f], mask=melt)
            for f in range(MOVING):
                pltpu.store(odd_near.at[1, f, group, to], near_of(new[f], swap), mask=melt)

    def stage_of(plane, step):
        return (plane - plan.low(0, step)) // 8

    def compute(stage):
        top = stage_of(top_plane, STEPS_BEFORE)
        below_melt = (stage <= top) | jnp.logical_not(is_last)

        eventful = (is_first & (stage == stage_of(first_plane, STEPS_BEFORE))) | (is_last & (stage >= top))

        @pl.when(jnp.logical_not(eventful))
        def _():
            for step in range(1, STEPS):
                row_steps(stage, step)
                if step == HOOK:
                    pass_on(stage)

        @pl.when(eventful)
        def _():
            for step in range(1, STEPS):
                state, near, strips, slot = buffers(step)
                out = (state, strips, near, slot)

                if step <= STEPS_BEFORE:
                    pl.when(below_melt)(functools.partial(row_steps, stage, step))
                else:
                    row_steps(stage, step)

                if step < STEPS_BEFORE:
                    @pl.when(is_last & (stage == stage_of(top_plane, step)))
                    def _():
                        copy_plane(*out, top_plane - 1, top_plane)
                else:
                    @pl.when(is_first & (stage == stage_of(first_plane, step)))
                    def _():
                        copy_plane(*out, first_plane, first_plane - 1)

                if step == HOOK:
                    pass_on(stage)

                if step == STEPS_BEFORE:
                    @pl.when(is_last & (stage >= top))
                    def _():
                        melt_fill(stage)
                        begin(stage, step + 1)

                if step == STEPS - 1:
                    @pl.when(is_last & (stage == stage_of(last_plane, step)))
                    def _():
                        copy_plane(*out, last_plane, last_plane + 1)

    pl.semaphore_wait(barrier, 5 + has_below.astype(jnp.int32) + has_above.astype(jnp.int32))

    @pl.when(has_below)
    def _():
        for piece in range(pieces):
            for copy in g_copies(piece):
                copy.start()

    for copy in loads:
        copy.wait()

    def fill_own(chunk, carry):
        fill(lab, pot, plan.base + 8 * chunk, 8 * chunk)
        either(chunk, send_y)
        return carry

    lax.fori_loop(0, own_chunks, fill_own, 0)
    lax.fori_loop(0, own_chunks, send_across, 0)
    tail = pl.ds((planes - lead) * rows, lead * rows)
    lab_up[0 : lead * rows] = lab[tail]
    for i in range(2):
        pot_up[i, 0 : lead * rows] = pot[i, tail]

    @pl.when(is_last)
    def _():
        for copy in melt_loads:
            copy.wait()
        plane = pl.ds((planes - 1) * rows, rows)
        at = pl.ds(lead * rows, rows)
        lab_up[at] = lab[plane]
        for i in range(2):
            pot_up[i, at] = pot[i, plane]

        def melt_plane(k, carry):
            code = codes[pl.ds(pl.multiple_of(jnp.minimum(k, shift - 1) * rows, rows), rows)]
            at = pl.ds(pl.multiple_of((lead + 1 + k) * rows, rows), rows)
            lab_up[at] = jnp.full((rows, 128), 3, jnp.int32)
            for i in range(2):
                value = jnp.zeros((rows, 128), jnp.float32)
                for level in range(levels):
                    value = jnp.where(code == level, table[i, level], value)
                pot_up[i, at] = value
            return carry

        lax.fori_loop(0, 8 * pieces - lead - 1, melt_plane, 0)

    def z_body(chunk, carry):
        send_z(chunk)
        return carry

    def pass_on(stage):
        @pl.when(stage == 0)
        def _():
            take(pieces)

        @pl.when(stage == 1)
        def _():
            lax.fori_loop(own_chunks + 1, chunks, z_body, 0)

    def beat(it, carry):
        lax.fori_loop(jnp.where(it == 3, 2, it), jnp.where(it == 3, 4, jnp.where(it < 2, it + 1, it)), z_body, 0)

        @pl.when((it == 0) | ((it >= 2) & (it < pieces)))
        def _():
            take(it)

        @pl.when(it >= 1)
        def _():
            receive_z(it - 1)
            unpack(it - 1)

        @pl.when(it >= 2)
        def _():
            compute(it - 2)

        return carry

    def take(it):
        piece = jnp.maximum(it - 1, 0)
        for k in range(pieces):
            @pl.when(has_above & (piece == k))
            def _():
                for copy in g_copies(k):
                    copy.wait_recv()

        fill(lab_up, pot_up, 8 * piece, 8 * (own_chunks + piece))
        send_y(own_chunks + piece)

    lax.fori_loop(0, plan.stages + 2, beat, 0)

    def drain(chunk, carry):
        def wait(copies):
            for copy in copies:
                copy.wait_send()

        either(chunk, lambda k: wait(y_copies(k)))

        @pl.when(chunk >= own_chunks)
        def _():
            z_copy(chunk).wait_send()

        @pl.when(chunk < own_chunks)
        def _():
            either(chunk, lambda k: wait(across_copies(k)))

        return carry

    lax.fori_loop(0, chunks, drain, 0)

    @pl.when(has_below)
    def _():
        for piece in range(pieces):
            for copy in g_copies(piece):
                copy.wait_send()


def last_kernel(plan, state, near, phases, potentials, p_out, m_out, sems):
    rows, planes = plan.rows, plan.planes
    at_left, at_right = lanes() == 0, lanes() == 127
    begin, tiles = plan.at(plan.shift), planes // 8

    def out_copies(tile):
        at = pl.ds(8 * tile * rows, 8 * rows)
        return [
            pltpu.make_async_copy(src.at[:, at], dst.at[:, at], sems.at[2 * tile + i])
            for i, (src, dst) in enumerate(((p_out, phases), (m_out, potentials)))
        ]

    def body(tile, carry):
        low = begin + 8 * tile
        for row in range(rows):
            src = state.at[0]
            sums = main_sums(src, STEPS + row, low, side_sums(src, near.at[0], STEPS + row, low, at_left, at_right))
            p, m = last_step(sums, *center(src, STEPS + row, low))
            at = pl.ds(8 * tile * rows + row, 8, stride=rows)
            for f in range(4):
                p_out[f, at, :] = p[f]
            for i in range(2):
                m_out[i, at, :] = m[i]
        for copy in out_copies(tile):
            copy.start()
        return carry

    lax.fori_loop(0, tiles, body, 0)
    for tile in range(tiles):
        for copy in out_copies(tile):
            copy.wait()


def on_device(mesh_shape, labels, potential, melt_codes, melt_table):
    planes, rows, width = labels.shape
    shift, levels = melt_codes.shape[0], melt_table.shape[1]
    plan = Plan(planes, rows, shift)
    flat = planes * rows
    vmem = pl.BlockSpec(memory_space=pltpu.VMEM)
    hbm = pl.BlockSpec(memory_space=pltpu.HBM)
    f32 = jnp.float32
    dma = pltpu.SemaphoreType.DMA
    deep, tall, chunks = plan.deep, plan.tall, plan.chunks
    evens, odds = STEPS // 2, STEPS // 2
    upper = 8 * plan.pieces * rows
    kept = (FIELDS * tall + MOVING * GROUPS) * deep * width * 4
    state, near = pl.pallas_call(
        functools.partial(front_kernel, plan, mesh_shape, levels),
        out_shape=(
            pltpu.VMEM((1, FIELDS, tall, deep, width), f32),
            pltpu.VMEM((1, MOVING, GROUPS, deep, width), f32),
        ),
        in_specs=[hbm, hbm, hbm, hbm],
        out_specs=(vmem, vmem),
        scratch_shapes=[
            pltpu.VMEM((flat, width), jnp.int32),
            pltpu.VMEM((2, flat, width), f32),
            pltpu.VMEM((shift * rows, width), jnp.int32),
            pltpu.SMEM((2, levels), f32),
            pltpu.VMEM((upper, width), jnp.int32),
            pltpu.VMEM((2, upper, width), f32),
            pltpu.VMEM((3, tall, deep, width), f32),
            pltpu.VMEM((3, GROUPS, deep, width), f32),
            pltpu.VMEM((3, GROUPS, deep, width), f32),
            pltpu.VMEM((3, GROUPS, 8 * plan.own_chunks, width), f32),
            pltpu.VMEM((3, 3, GROUPS, 8 * plan.own_chunks, width), f32),
            pltpu.VMEM((evens, FIELDS, tall, deep, width), f32),
            pltpu.VMEM((odds, FIELDS, tall, deep, width), f32),
            pltpu.VMEM((evens, MOVING, GROUPS, deep, width), f32),
            pltpu.VMEM((odds, MOVING, GROUPS, deep, width), f32),
            pltpu.VMEM((evens, FIELDS, GROUPS, deep, width), f32),
            pltpu.VMEM((odds, FIELDS, GROUPS, deep, width), f32),
            pltpu.VMEM((1, FIELDS, GROUPS, deep, width), f32),
            pltpu.VMEM((BATCH, MOVING, 8, width), f32),
            pltpu.VMEM((MOVING, GROUPS, 8, width), f32),
            dma((4,)), dma((3 * chunks,)), dma((3 * chunks,)),
            dma((2 * chunks,)), dma((2 * chunks,)), dma((chunks,)), dma((chunks,)),
            dma((3 * plan.own_chunks,)), dma((3 * plan.own_chunks,)),
        ],
        compiler_params=pltpu.CompilerParams(collective_id=0, has_side_effects=True, vmem_limit_bytes=(VMEM_BYTES - kept) // 4096 * 4096),
        name="front",
    )(labels.reshape(flat, width), potential.reshape(2, flat, width), melt_codes.reshape(shift * rows, width), melt_table)
    state, near = (pltpu.with_memory_space_constraint(v, pltpu.VMEM) for v in (state, near))
    phases, potentials = pl.pallas_call(
        functools.partial(last_kernel, plan),
        out_shape=(
            jax.ShapeDtypeStruct((4, flat, width), f32),
            jax.ShapeDtypeStruct((2, flat, width), f32),
        ),
        in_specs=[vmem, vmem],
        out_specs=(hbm, hbm),
        scratch_shapes=[
            pltpu.VMEM((4, flat, width), f32),
            pltpu.VMEM((2, flat, width), f32),
            dma((2 * (planes // 8),)),
        ],
        compiler_params=pltpu.CompilerParams(vmem_limit_bytes=8 << 20),
        name="last",
    )(state, near)
    return phases.reshape(4, planes, rows, width), potentials.reshape(2, planes, rows, width)


def solution(mesh):
    mesh_shape = tuple(mesh.shape[axis] for axis in ("grow", "gy", "gz"))
    return jax.shard_map(
        functools.partial(on_device, mesh_shape),
        mesh=mesh,
        in_specs=(P("grow", "gy", "gz"), P(None, "grow", "gy", "gz"), P(None, "gy", "gz"), P()),
        out_specs=(P(None, "grow", "gy", "gz"), P(None, "grow", "gy", "gz")),
        check_vma=False,
    )
```

```python
import functools

import jax
import jax.numpy as jnp
from jax import lax
from jax.experimental import pallas as pl
from jax.experimental.pallas import tpu as pltpu
from jax.sharding import PartitionSpec as P

STEPS_BEFORE = 3
STEPS_AFTER = 2
STEPS = STEPS_BEFORE + STEPS_AFTER
HALF = 9
SLOT = 2 * HALF
GROUPS = 3
LAG = 5
HOOK = 2
BATCH = 8
FIELDS = 11
MOVING = 5
CODE = 16.0
CODED_AT = (0,) + tuple(range(3, FIELDS))
VMEM_BYTES = 67043328
MESH = pl.DeviceIdType.MESH

LAM = 0.12
BETA = 5.0 / LAM**2
MU = 17.5 / (LAM * BETA)
OWN = (1.0 / LAM - 6.0) / BETA
TILT = 1.25 / (LAM * BETA)
BACK = 0.2 * MU / LAM**3


class Plan:
    def __init__(self, planes, rows, shift):
        self.planes, self.rows, self.shift = planes, rows, shift
        self.base = shift - STEPS + 2 - 8
        self.chunks = planes // 8 + 2
        self.stages = self.chunks - 1
        self.deep = 8 * self.chunks
        self.above = shift + STEPS
        self.tall = rows + 2 * STEPS
        self.own_chunks, self.lead = divmod(planes - self.base, 8)
        self.pieces = self.chunks - self.own_chunks

    def at(self, plane):
        return plane - self.base

    def low(self, stage, step):
        return 8 + 8 * stage - step


def phase_state(label, pot, coded=False):
    if coded:
        q = [jnp.where(label == 0.0, 1.0, jnp.where(label == 1.0, CODE, jnp.where(label == 2.0, CODE * CODE, 0.0)))]
    else:
        q = [jnp.where(label == float(a), LAM, 0.0) for a in range(3)]
    y = [jnp.where(label == float(a), LAM * BETA * OWN, 0.0) for a in range(3)]
    liquid = label == 3.0
    mob = jnp.where(liquid, 0.15, 0.0075)
    u = [MU * v for v in pot]
    comp = [jnp.where(liquid, 0.35 * MU, jnp.where(label == float(i), 0.8 * MU, 0.1 * MU)) for i in range(2)]
    rest = [(u[i] + comp[i]) - (6.0 * mob) * u[i] for i in range(2)]
    return q + u + y + rest + [mob]


def decode(total):
    third = jnp.floor(total * (1.0 / (CODE * CODE)))
    total = total - (CODE * CODE) * third
    second = jnp.floor(total * (1.0 / CODE))
    return [LAM * v for v in (total - CODE * second, second, third)]


def moving_of(step):
    return (0, 3, 4) if step == 1 else tuple(range(MOVING))


def clip_step(sums, y):
    x = [sums[a] + y[a] for a in range(3)]
    x.append(1.0 - (x[0] + x[1] + x[2]))
    held = [jnp.clip(v, 0.0, 1.0) for v in x]
    return held, 1.0 / ((held[0] + held[1]) + (held[2] + held[3]))


def cell_step(sums, y, rest, mob, tick=lambda: None):
    held, inverse = clip_step(sums, y)
    tick()
    total = [rest[i] + mob * sums[3 + i] for i in range(2)]
    tick()
    scaled = LAM * inverse
    q = [v * scaled for v in held]
    tick()
    square = [v * v for v in q]
    tick()
    h = [square[a] * (1.5 * LAM - q[a]) for a in range(4)]
    tick()
    shared = BACK * ((h[0] + h[1]) + (h[2] + 3.5 * h[3]))
    tick()
    u = [(total[i] - shared) - (7.0 * BACK) * h[i] for i in range(2)]
    tick()
    both = u[0] + u[1]
    well = OWN - ((square[0] + square[1]) + (square[2] + square[3]))
    tick()
    third = both * (1.0 / 7.0) + TILT
    pull = [third + u[0], third + u[1], third, 0.5 * both]
    tick()
    mob = 0.0075 + (0.1425 / LAM) * q[3]
    six = 6.0 * mob
    rest = [total[i] - six * u[i] for i in range(2)]
    tick()
    local = []
    for a in range(4):
        local.append(q[a] * ((well + square[a]) + pull[a] * (LAM - q[a])))
        tick()
    mean = 0.25 * ((local[0] + local[1]) + (local[2] + local[3])) - 0.07 / BETA
    tick()
    y = [BETA * (local[a] - mean) for a in range(3)]
    tick()
    return q[:3] + u + y + rest + [mob]


def last_step(sums, y, rest, mob):
    held, inverse = clip_step(sums, y)
    p = [v * inverse for v in held]
    h = [v * v * (1.5 - v) for v in p]
    shared = 0.2 * ((h[0] + h[1]) + (h[2] + 3.5 * h[3]))
    total = [(rest[i] + mob * sums[3 + i]) * (1.0 / MU) for i in range(2)]
    return p, [(total[i] - shared) - 1.4 * h[i] for i in range(2)]


def lanes():
    return lax.broadcasted_iota(jnp.int32, (8, 128), 1)


def side_sums(state, near, row, low, at_left, at_right):
    slot, group = divmod(row, GROUPS)
    turn = 128 - (SLOT * slot + HALF // 2 + 1)
    sums = []
    for f in range(MOVING):
        v = state[f, row, pl.ds(low, 8), :]
        edge = pltpu.roll(near[f, group, pl.ds(low, 8), :], turn, 1)
        right = pltpu.roll(jnp.where(at_left, edge, v), 127, 1)
        left = pltpu.roll(jnp.where(at_right, edge, v), 1, 1)
        sums.append(right + left)
    return sums


def main_sums(state, row, low, sides):
    sums = []
    for f in range(MOVING):
        grow = state[f, row, pl.ds(low + 1, 8), :] + state[f, row, pl.ds(low - 1, 8), :]
        side = state[f, row + 1, pl.ds(low, 8), :] + state[f, row - 1, pl.ds(low, 8), :]
        sums.append((grow + side) + sides[f])
    return sums


def center(state, row, low):
    y = [state[MOVING + a, row, pl.ds(low, 8), :] for a in range(3)]
    rest = [state[MOVING + 3 + i, row, pl.ds(low, 8), :] for i in range(2)]
    return y, rest, state[FIELDS - 1, row, pl.ds(low, 8), :]


def near_of(v, swap):
    return jnp.where(swap, pltpu.roll(v, 128 - (HALF - 1), 1), v)


def front_kernel(
    plan, mesh_shape, levels, lab_hbm, pot_hbm, codes_hbm, table_hbm, out_state, out_near,
    lab, pot, codes, table, lab_up, pot_up, raw, pack, strip, across_pack, across, even, odd, even_near, odd_near, even_strip, odd_strip, out_strip, sides, strip_sides,
    in_sems, g_send, g_recv, y_send, y_recv, z_send, z_recv, a_send, a_recv,
):
    g, y, z = lax.axis_index("grow"), lax.axis_index("gy"), lax.axis_index("gz")
    count_g, count_y, count_z = mesh_shape
    rows, tall, planes, shift = plan.rows, plan.tall, plan.planes, plan.shift
    has_below, has_above = g > 0, g < count_g - 1
    is_first, is_last = g == 0, g == count_g - 1
    y_up, y_down = lax.rem(y + 1, count_y), lax.rem(y + count_y - 1, count_y)
    z_other = lax.rem(z + 1, count_z)
    chunks = plan.chunks
    own_chunks, lead, pieces = plan.own_chunks, plan.lead, plan.pieces

    loads = [
        pltpu.make_async_copy(lab_hbm, lab, in_sems.at[0]),
        pltpu.make_async_copy(pot_hbm, pot, in_sems.at[1]),
    ]
    melt_loads = [
        pltpu.make_async_copy(codes_hbm, codes, in_sems.at[2]),
        pltpu.make_async_copy(table_hbm, table, in_sems.at[3]),
    ]
    for copy in loads:
        copy.start()

    @pl.when(is_last)
    def _():
        for copy in melt_loads:
            copy.start()

    barrier = pltpu.get_barrier_semaphore()

    def greet(target):
        pl.semaphore_signal(barrier, inc=1, device_id=target, device_id_type=MESH)

    @pl.when(has_below)
    def _():
        greet((g - 1, y, z))

    @pl.when(has_above)
    def _():
        greet((g + 1, y, z))

    greet((g, y_up, z))
    greet((g, y_down, z))
    greet((g, y, z_other))
    greet((g, y_up, z_other))
    greet((g, y_down, z_other))

    splits = [max(8 * piece - lead, 0) for piece in range(pieces + 1)]

    def g_copies(piece):
        begin, end = splits[piece], splits[piece + 1]
        src, dst = pl.ds(begin * rows, (end - begin) * rows), pl.ds((lead + begin) * rows, (end - begin) * rows)
        copies = []
        for i in range(3):
            source, target = (lab_hbm.at[src], lab_up.at[dst]) if i == 0 else (pot_hbm.at[i - 1, src], pot_up.at[i - 1, dst])
            sem = 3 * piece + i
            copies.append(pltpu.make_async_remote_copy(
                src_ref=source, dst_ref=target, send_sem=g_send.at[sem], recv_sem=g_recv.at[sem],
                device_id=(g - 1, y, z), device_id_type=MESH))
        return copies

    def planes_of(chunk):
        return pl.ds(7, 1) if isinstance(chunk, int) and chunk == 0 else pl.ds(8 * chunk, 8)

    def either(chunk, action):
        pl.when(chunk == 0)(lambda: action(0))
        pl.when(chunk > 0)(lambda: action(chunk))

    def y_copies(chunk):
        copies = []
        for up in range(2):
            src, dst, target = (rows, 0, y_up) if up else (STEPS, STEPS + rows, y_down)
            sem = 2 * chunk + up
            at = planes_of(chunk)
            copies.append(pltpu.make_async_remote_copy(
                src_ref=raw.at[:, pl.ds(src, STEPS), at], dst_ref=raw.at[:, pl.ds(dst, STEPS), at],
                send_sem=y_send.at[sem], recv_sem=y_recv.at[sem],
                device_id=(g, target, z), device_id_type=MESH))
        return copies

    def z_copy(chunk):
        at = pl.ds(8 * chunk, 8)
        return pltpu.make_async_remote_copy(
            src_ref=pack.at[:, :, at], dst_ref=strip.at[:, :, at],
            send_sem=z_send.at[chunk], recv_sem=z_recv.at[chunk],
            device_id=(g, y, z_other), device_id_type=MESH)

    def across_copies(chunk):
        at = planes_of(chunk)
        copies = []
        for k, row in enumerate((y_up, y, y_down)):
            sem = 3 * chunk + k
            copies.append(pltpu.make_async_remote_copy(
                src_ref=across_pack.at[:, :, at], dst_ref=across.at[k, :, :, at],
                send_sem=a_send.at[sem], recv_sem=a_recv.at[sem],
                device_id=(g, row, z_other), device_id_type=MESH))
        return copies

    def fill(labels, pots, begin, to):
        for row in range(rows):
            at = pl.ds(begin * rows + row, 8, stride=rows)
            raw[0, STEPS + row, pl.ds(to, 8)] = labels[at].astype(jnp.float32)
            for i in range(2):
                raw[1 + i, STEPS + row, pl.ds(to, 8)] = pots[i, at]

    def send_y(chunk):
        for copy in y_copies(chunk):
            copy.start()

    lane = lanes()

    def pack_rows(target, chunk, source):
        at = pl.ds(8 * chunk, 8)

        def pack_field(i, carry):
            for group in range(GROUPS):
                packed = jnp.zeros((8, 128), jnp.float32)
                for slot in range(tall // GROUPS):
                    v = raw[i, source(GROUPS * slot + group), at]
                    first = SLOT * slot
                    packed = jnp.where(lane >= first, pltpu.roll(v, first + HALF // 2 + 1, 1), packed)
                    packed = jnp.where(lane >= first + HALF, pltpu.roll(v, first + HALF + HALF // 2, 1), packed)
                target[i, group, at] = packed
            return carry

        lax.fori_loop(0, 3, pack_field, 0)

    def row_across(row):
        return row + rows if row < STEPS else row - rows if row >= STEPS + rows else row

    def start_all(copies):
        for copy in copies:
            copy.start()

    def send_across(chunk, carry):
        pack_rows(across_pack, chunk, row_across)
        either(chunk, lambda k: start_all(across_copies(k)))
        return carry

    def wait_all(copies):
        for copy in copies:
            copy.wait_recv()

    def send_z(chunk):
        either(chunk, lambda k: wait_all(y_copies(k)))
        pack_rows(pack, chunk, lambda row: row)

        @pl.when(chunk >= own_chunks)
        def _():
            z_copy(chunk).start()

    def receive_z(chunk):
        @pl.when(chunk >= own_chunks)
        def _():
            z_copy(chunk).wait_recv()

        @pl.when(chunk < own_chunks)
        def _():
            either(chunk, lambda k: wait_all(across_copies(k)))
            at = pl.ds(8 * chunk, 8)
            for group in range(GROUPS):
                own, upper = -((group - STEPS) // GROUPS), -((group - STEPS - rows) // GROUPS)
                for i in range(3):
                    value = jnp.where(lane >= SLOT * own, across[1, i, group, at], across[0, i, group, at])
                    strip[i, group, at] = jnp.where(lane >= SLOT * upper, across[2, i, group, at], value)

    place = lane % SLOT
    from_other = (place < HALF // 2 + 1) | (place >= SLOT - HALF // 2 - 1)
    swap = place == HALF // 2 + 1
    at_left, at_right = lane == 0, lane == 127

    def unpack_row(state, slot, row, source, target):
        at = pl.ds(source, 8)
        new = phase_state(raw[0, row, at], [raw[1, row, at], raw[2, row, at]])
        for f in range(FIELDS):
            state[slot, f, row, pl.ds(target, 8)] = new[f]

    def unpack_strips(state, near, slot, source, target):
        at, to = pl.ds(source, 8), pl.ds(target, 8)
        for group in range(GROUPS):
            value = [jnp.where(from_other, strip[i, group, at], pack[i, group, at]) for i in range(3)]
            for f, v in zip(CODED_AT, phase_state(value[0], value[1:], True)):
                state[slot, f, group, to] = v
                if f < MOVING:
                    near[slot, f, group, to] = near_of(v, swap)

    def unpack(chunk):
        to = 8 * chunk

        def body(part, carry):
            rows_at = pl.ds(tall // GROUPS * part, tall // GROUPS)
            at = pl.ds(to, 8)
            new = phase_state(raw[0, rows_at, at], [raw[1, rows_at, at], raw[2, rows_at, at]], True)
            for f, v in zip(CODED_AT, new):
                even[0, f, rows_at, at] = v
            return carry

        lax.fori_loop(0, GROUPS, body, 0)
        unpack_strips(even_strip, even_near, 0, to, to)

    def strip_side_steps(fields, src, slot, low, result):
        at = pl.ds(low, 8)

        def piece(f):
            v = src[slot, f, :, at]
            part = [src[slot, f, group, at] for group in range(GROUPS)]
            up = jnp.stack([part[1], part[2], pltpu.roll(part[0], 128 - SLOT, 1)])
            down = jnp.stack([pltpu.roll(part[2], SLOT, 1), part[0], part[1]])
            result[f] = (up + down) + (pltpu.roll(v, 127, 2) + pltpu.roll(v, 1, 2))

        return [functools.partial(piece, f) for f in fields]

    def strip_step(step, src, src_slot, dst, near, dst_slot, low, around, tick):
        at = pl.ds(low, 8)
        sums = []
        for f in moving_of(step):
            total = src[src_slot, f, :, pl.ds(low + 1, 8)] + src[src_slot, f, :, pl.ds(low - 1, 8)]
            sums.append(total + around[f])
            tick()
        if step == 1:
            sums = decode(sums[0]) + sums[1:]
        y = [src[src_slot, MOVING + a, :, at] for a in range(3)]
        rest = [src[src_slot, MOVING + 3 + i, :, at] for i in range(2)]
        new = cell_step(sums, y, rest, src[src_slot, FIELDS - 1, :, at], tick)
        for f in range(FIELDS):
            dst[dst_slot, f, :, at] = new[f]
        for f in range(MOVING):
            near[dst_slot, f, :, at] = jnp.where(swap, pltpu.roll(new[f], 128 - (HALF - 1), 2), new[f])

    def side_steps(fields, state, near, first, count, low, result):
        v, edge, ends = {}, {}, {}

        def near_rolls(f):
            rolled = []
            for i in range(count):
                slot, group = divmod(first + i, GROUPS)
                rolled.append(pltpu.roll(near[f, group, pl.ds(low, 8), :], 128 - (SLOT * slot + HALF // 2 + 1), 1))
            edge[f] = jnp.stack(rolled)
            v[f] = state[f, first : first + count, pl.ds(low, 8), :]

        def z_rolls(f):
            right = pltpu.roll(jnp.where(at_left, edge[f], v[f]), 127, 2)
            left = pltpu.roll(jnp.where(at_right, edge[f], v[f]), 1, 2)
            ends[f] = (right, left)

        def add(f):
            result[f] = ends[f][0] + ends[f][1]

        pieces = []
        for k in range(len(fields) + 2 * LAG):
            if k < len(fields):
                pieces.append(functools.partial(near_rolls, fields[k]))
            if LAG <= k < len(fields) + LAG:
                pieces.append(functools.partial(z_rolls, fields[k - LAG]))
            if k >= 2 * LAG:
                pieces.append(functools.partial(add, fields[k - 2 * LAG]))
        return pieces

    class Ahead:
        def __init__(self, pieces=()):
            self.pieces = list(pieces)

        def __call__(self):
            if self.pieces:
                self.pieces.pop(0)()

        def flush(self):
            while self.pieces:
                self()

    def sizes_of(step):
        total = tall - 2 * step
        parts = -(-total // BATCH)
        return [total // parts + (k < total % parts) for k in range(parts)]

    def buffers(step):
        if step == STEPS - 1:
            return out_state, out_near, out_strip, 0
        if step % 2:
            return odd, odd_near, odd_strip, step // 2
        return even, even_near, even_strip, step // 2

    def begin_steps(stage, step, around, strip_around):
        state, near, strips, slot = buffers(step - 1)
        low = plan.low(stage, step)
        rows_ahead = side_steps(moving_of(step), state.at[slot], near.at[slot], step, sizes_of(step)[0], low, around)
        return rows_ahead, strip_side_steps(moving_of(step), strips, slot, low, strip_around)

    def keep(around, strip_around):
        for f in around:
            sides[: around[f].shape[0], f] = around[f]
            strip_sides[f] = strip_around[f]

    def begin(stage, step):
        around, strip_around = {}, {}
        rows_ahead, strips_ahead = begin_steps(stage, step, around, strip_around)
        for piece in strips_ahead + rows_ahead:
            piece()
        keep(around, strip_around)

    def row_steps(stage, step):
        src, src_near, src_strip, slot = buffers(step - 1)
        dst, dst_near, dst_strip, dst_slot = buffers(step)
        state, near = src.at[slot], src_near.at[slot]
        low = plan.low(stage, step)
        sizes = sizes_of(step)
        at = pl.ds(low, 8)
        ready, strip_ready = {}, {}
        if step == 1:
            rows_ahead, strips_ahead = begin_steps(stage, step, ready, strip_ready)
            Ahead(strips_ahead).flush()
            ahead = Ahead(rows_ahead)
        else:
            ready = {f: sides[: sizes[0], f] for f in moving_of(step)}
            strip_ready = {f: strip_sides[f] for f in moving_of(step)}
            ahead = Ahead()
        strip_step(step, src_strip, slot, dst_strip, dst_near, dst_slot, low, strip_ready, ahead)
        ahead.flush()
        row = step
        for k, size in enumerate(sizes):
            around, ready, strip_ready = ready, {}, {}
            if k + 1 < len(sizes):
                ahead = Ahead(side_steps(moving_of(step), state, near, row + size, sizes[k + 1], low, ready))
            elif step < STEPS - 1:
                rows_ahead, strips_ahead = begin_steps(stage, step + 1, ready, strip_ready)
                ahead = Ahead(strips_ahead + rows_ahead)

            def rows_of(f, shift=0, up=0):
                return state[f, row + shift : row + shift + size, pl.ds(low + up, 8), :]

            sums = []
            for f in moving_of(step):
                grow = rows_of(f, 0, 1) + rows_of(f, 0, -1)
                side = rows_of(f, 1) + rows_of(f, -1)
                sums.append((grow + side) + around[f])
                ahead()
            if step == 1:
                sums = decode(sums[0]) + sums[1:]
            y = [rows_of(MOVING + a) for a in range(3)]
            rest = [rows_of(MOVING + 3 + i) for i in range(2)]
            new = cell_step(sums, y, rest, rows_of(FIELDS - 1), ahead)
            ahead.flush()
            for f in range(FIELDS):
                dst[dst_slot, f, row : row + size, at, :] = new[f]
            row += size
        if step < STEPS - 1:
            keep(ready, strip_ready)

    def copy_plane(state, strips, near, slot, source, target):
        src, dst = pl.ds(source, 1), pl.ds(target, 1)

        def body(row, carry):
            for f in range(MOVING):
                state[slot, f, row, dst] = state[slot, f, row, src]
            return carry

        lax.fori_loop(0, tall, body, 0)
        for group in range(GROUPS):
            for f in range(MOVING):
                strips[slot, f, group, dst] = strips[slot, f, group, src]
                near[slot, f, group, dst] = near[slot, f, group, src]

    first_plane, top_plane = plan.at(shift), plan.at(planes)
    last_plane = first_plane + planes - 1
    place_up = lax.broadcasted_iota(jnp.int32, (8, 128), 0)

    def melt_fill(stage):
        source, target = 8 * stage + 8, 8 * stage + 7
        melt = place_up >= top_plane - target
        at, to = pl.ds(source, 8), pl.ds(target, 8)

        def body(row, carry):
            new = phase_state(raw[0, row, at], [raw[1, row, at], raw[2, row, at]])
            for f in range(FIELDS):
                pltpu.store(odd.at[1, f, row, to], new[f], mask=melt)
            return carry

        lax.fori_loop(STEPS_BEFORE, tall - STEPS_BEFORE, body, 0)
        for group in range(GROUPS):
            value = [jnp.where(from_other, strip[i, group, at], pack[i, group, at]) for i in range(3)]
            new = phase_state(value[0], value[1:])
            for f in range(FIELDS):
                pltpu.store(odd_strip.at[1, f, group, to], new[f], mask=melt)
            for f in range(MOVING):
                pltpu.store(odd_near.at[1, f, group, to], near_of(new[f], swap), mask=melt)

    def stage_of(plane, step):
        return (plane - plan.low(0, step)) // 8

    def compute(stage):
        top = stage_of(top_plane, STEPS_BEFORE)
        below_melt = (stage <= top) | jnp.logical_not(is_last)

        eventful = (is_first & (stage == stage_of(first_plane, STEPS_BEFORE))) | (is_last & (stage >= top))

        @pl.when(jnp.logical_not(eventful) & (stage < 2))
        def _():
            for step in range(1, STEPS):
                row_steps(stage, step)
                if step == HOOK:
                    pass_on(stage)

        @pl.when(jnp.logical_not(eventful) & (stage >= 2))
        def _():
            for step in range(1, STEPS):
                row_steps(stage, step)

        @pl.when(eventful)
        def _():
            for step in range(1, STEPS):
                state, near, strips, slot = buffers(step)
                out = (state, strips, near, slot)

                if step <= STEPS_BEFORE:
                    pl.when(below_melt)(functools.partial(row_steps, stage, step))
                else:
                    row_steps(stage, step)

                if step < STEPS_BEFORE:
                    @pl.when(is_last & (stage == stage_of(top_plane, step)))
                    def _():
                        copy_plane(*out, top_plane - 1, top_plane)
                else:
                    @pl.when(is_first & (stage == stage_of(first_plane, step)))
                    def _():
                        copy_plane(*out, first_plane, first_plane - 1)

                if step == HOOK:
                    pass_on(stage)

                if step == STEPS_BEFORE:
                    @pl.when(is_last & (stage >= top))
                    def _():
                        melt_fill(stage)
                        begin(stage, step + 1)

                if step == STEPS - 1:
                    @pl.when(is_last & (stage == stage_of(last_plane, step)))
                    def _():
                        copy_plane(*out, last_plane, last_plane + 1)

    pl.semaphore_wait(barrier, 5 + has_below.astype(jnp.int32) + has_above.astype(jnp.int32))

    @pl.when(has_below)
    def _():
        for piece in range(pieces):
            for copy in g_copies(piece):
                copy.start()

    for copy in loads:
        copy.wait()

    def fill_own(chunk, carry):
        fill(lab, pot, plan.base + 8 * chunk, 8 * chunk)
        either(chunk, send_y)
        return carry

    lax.fori_loop(0, own_chunks, fill_own, 0)
    lax.fori_loop(0, own_chunks, send_across, 0)
    tail = pl.ds((planes - lead) * rows, lead * rows)
    lab_up[0 : lead * rows] = lab[tail]
    for i in range(2):
        pot_up[i, 0 : lead * rows] = pot[i, tail]

    @pl.when(is_last)
    def _():
        for copy in melt_loads:
            copy.wait()
        plane = pl.ds((planes - 1) * rows, rows)
        at = pl.ds(lead * rows, rows)
        lab_up[at] = lab[plane]
        for i in range(2):
            pot_up[i, at] = pot[i, plane]

        def melt_plane(k, carry):
            code = codes[pl.ds(pl.multiple_of(jnp.minimum(k, shift - 1) * rows, rows), rows)]
            at = pl.ds(pl.multiple_of((lead + 1 + k) * rows, rows), rows)
            lab_up[at] = jnp.full((rows, 128), 3, jnp.int32)
            for i in range(2):
                value = jnp.zeros((rows, 128), jnp.float32)
                for level in range(levels):
                    value = jnp.where(code == level, table[i, level], value)
                pot_up[i, at] = value
            return carry

        lax.fori_loop(0, 8 * pieces - lead - 1, melt_plane, 0)

    def z_body(chunk, carry):
        send_z(chunk)
        return carry

    def pass_on(stage):
        @pl.when(stage == 0)
        def _():
            take(pieces)

        @pl.when(stage == 1)
        def _():
            lax.fori_loop(own_chunks + 1, chunks, z_body, 0)

    def beat(it, carry):
        lax.fori_loop(jnp.where(it == 3, 2, it), jnp.where(it == 3, 4, jnp.where(it < 2, it + 1, it)), z_body, 0)

        @pl.when((it == 0) | ((it >= 2) & (it < pieces)))
        def _():
            take(it)

        @pl.when(it >= 1)
        def _():
            receive_z(it - 1)
            unpack(it - 1)

        @pl.when(it >= 2)
        def _():
            compute(it - 2)

        return carry

    def take(it):
        piece = jnp.maximum(it - 1, 0)
        for k in range(pieces):
            @pl.when(has_above & (piece == k))
            def _():
                for copy in g_copies(k):
                    copy.wait_recv()

        fill(lab_up, pot_up, 8 * piece, 8 * (own_chunks + piece))
        send_y(own_chunks + piece)

    lax.fori_loop(0, plan.stages + 2, beat, 0)

    def drain(chunk, carry):
        def wait(copies):
            for copy in copies:
                copy.wait_send()

        either(chunk, lambda k: wait(y_copies(k)))

        @pl.when(chunk >= own_chunks)
        def _():
            z_copy(chunk).wait_send()

        @pl.when(chunk < own_chunks)
        def _():
            either(chunk, lambda k: wait(across_copies(k)))

        return carry

    lax.fori_loop(0, chunks, drain, 0)

    @pl.when(has_below)
    def _():
        for piece in range(pieces):
            for copy in g_copies(piece):
                copy.wait_send()


def last_kernel(plan, state, near, phases, potentials, p_out, m_out, sems):
    rows, planes = plan.rows, plan.planes
    at_left, at_right = lanes() == 0, lanes() == 127
    begin, tiles = plan.at(plan.shift), planes // 8

    def out_copies(tile):
        at = pl.ds(8 * tile * rows, 8 * rows)
        return [
            pltpu.make_async_copy(src.at[:, at], dst.at[:, at], sems.at[2 * tile + i])
            for i, (src, dst) in enumerate(((p_out, phases), (m_out, potentials)))
        ]

    def body(tile, carry):
        low = begin + 8 * tile
        for row in range(rows):
            src = state.at[0]
            sums = main_sums(src, STEPS + row, low, side_sums(src, near.at[0], STEPS + row, low, at_left, at_right))
            p, m = last_step(sums, *center(src, STEPS + row, low))
            at = pl.ds(8 * tile * rows + row, 8, stride=rows)
            for f in range(4):
                p_out[f, at, :] = p[f]
            for i in range(2):
                m_out[i, at, :] = m[i]
        for copy in out_copies(tile):
            copy.start()
        return carry

    lax.fori_loop(0, tiles, body, 0)
    for tile in range(tiles):
        for copy in out_copies(tile):
            copy.wait()


def on_device(mesh_shape, labels, potential, melt_codes, melt_table):
    planes, rows, width = labels.shape
    shift, levels = melt_codes.shape[0], melt_table.shape[1]
    plan = Plan(planes, rows, shift)
    flat = planes * rows
    vmem = pl.BlockSpec(memory_space=pltpu.VMEM)
    hbm = pl.BlockSpec(memory_space=pltpu.HBM)
    f32 = jnp.float32
    dma = pltpu.SemaphoreType.DMA
    deep, tall, chunks = plan.deep, plan.tall, plan.chunks
    evens, odds = STEPS // 2, STEPS // 2
    upper = 8 * plan.pieces * rows
    kept = (FIELDS * tall + MOVING * GROUPS) * deep * width * 4
    state, near = pl.pallas_call(
        functools.partial(front_kernel, plan, mesh_shape, levels),
        out_shape=(
            pltpu.VMEM((1, FIELDS, tall, deep, width), f32),
            pltpu.VMEM((1, MOVING, GROUPS, deep, width), f32),
        ),
        in_specs=[hbm, hbm, hbm, hbm],
        out_specs=(vmem, vmem),
        scratch_shapes=[
            pltpu.VMEM((flat, width), jnp.int32),
            pltpu.VMEM((2, flat, width), f32),
            pltpu.VMEM((shift * rows, width), jnp.int32),
            pltpu.SMEM((2, levels), f32),
            pltpu.VMEM((upper, width), jnp.int32),
            pltpu.VMEM((2, upper, width), f32),
            pltpu.VMEM((3, tall, deep, width), f32),
            pltpu.VMEM((3, GROUPS, deep, width), f32),
            pltpu.VMEM((3, GROUPS, deep, width), f32),
            pltpu.VMEM((3, GROUPS, 8 * plan.own_chunks, width), f32),
            pltpu.VMEM((3, 3, GROUPS, 8 * plan.own_chunks, width), f32),
            pltpu.VMEM((evens, FIELDS, tall, deep, width), f32),
            pltpu.VMEM((odds, FIELDS, tall, deep, width), f32),
            pltpu.VMEM((evens, MOVING, GROUPS, deep, width), f32),
            pltpu.VMEM((odds, MOVING, GROUPS, deep, width), f32),
            pltpu.VMEM((evens, FIELDS, GROUPS, deep, width), f32),
            pltpu.VMEM((odds, FIELDS, GROUPS, deep, width), f32),
            pltpu.VMEM((1, FIELDS, GROUPS, deep, width), f32),
            pltpu.VMEM((BATCH, MOVING, 8, width), f32),
            pltpu.VMEM((MOVING, GROUPS, 8, width), f32),
            dma((4,)), dma((3 * chunks,)), dma((3 * chunks,)),
            dma((2 * chunks,)), dma((2 * chunks,)), dma((chunks,)), dma((chunks,)),
            dma((3 * plan.own_chunks,)), dma((3 * plan.own_chunks,)),
        ],
        compiler_params=pltpu.CompilerParams(collective_id=0, has_side_effects=True, vmem_limit_bytes=(VMEM_BYTES - kept) // 4096 * 4096),
        name="front",
    )(labels.reshape(flat, width), potential.reshape(2, flat, width), melt_codes.reshape(shift * rows, width), melt_table)
    state, near = (pltpu.with_memory_space_constraint(v, pltpu.VMEM) for v in (state, near))
    phases, potentials = pl.pallas_call(
        functools.partial(last_kernel, plan),
        out_shape=(
            jax.ShapeDtypeStruct((4, flat, width), f32),
            jax.ShapeDtypeStruct((2, flat, width), f32),
        ),
        in_specs=[vmem, vmem],
        out_specs=(hbm, hbm),
        scratch_shapes=[
            pltpu.VMEM((4, flat, width), f32),
            pltpu.VMEM((2, flat, width), f32),
            dma((2 * (planes // 8),)),
        ],
        compiler_params=pltpu.CompilerParams(vmem_limit_bytes=8 << 20),
        name="last",
    )(state, near)
    return phases.reshape(4, planes, rows, width), potentials.reshape(2, planes, rows, width)


def solution(mesh):
    mesh_shape = tuple(mesh.shape[axis] for axis in ("grow", "gy", "gz"))
    return jax.shard_map(
        functools.partial(on_device, mesh_shape),
        mesh=mesh,
        in_specs=(P("grow", "gy", "gz"), P(None, "grow", "gy", "gz"), P(None, "gy", "gz"), P()),
        out_specs=(P(None, "grow", "gy", "gz"), P(None, "grow", "gy", "gz")),
        check_vma=False,
    )
```

```python
import functools

import jax
import jax.numpy as jnp
from jax import lax
from jax.experimental import pallas as pl
from jax.experimental.pallas import tpu as pltpu
from jax.sharding import PartitionSpec as P

STEPS_BEFORE = 3
STEPS_AFTER = 2
STEPS = STEPS_BEFORE + STEPS_AFTER
HALF = 9
SLOT = 2 * HALF
GROUPS = 3
LAG = 5
HOOK = 2
BATCH = 8
FIELDS = 11
MOVING = 5
CODE = 16.0
CODED_AT = (0,) + tuple(range(3, FIELDS))
VMEM_BYTES = 67043328
MESH = pl.DeviceIdType.MESH

LAM = 0.12
BETA = 5.0 / LAM**2
MU = 17.5 / (LAM * BETA)
OWN = (1.0 / LAM - 6.0) / BETA
TILT = 1.25 / (LAM * BETA)
BACK = 0.2 * MU / LAM**3


class Plan:
    def __init__(self, planes, rows, shift):
        self.planes, self.rows, self.shift = planes, rows, shift
        self.base = shift - STEPS + 2 - 8
        self.chunks = planes // 8 + 2
        self.stages = self.chunks - 1
        self.deep = 8 * self.chunks
        self.above = shift + STEPS
        self.tall = rows + 2 * STEPS
        self.own_chunks, self.lead = divmod(planes - self.base, 8)
        self.pieces = self.chunks - self.own_chunks

    def at(self, plane):
        return plane - self.base

    def low(self, stage, step):
        return 8 + 8 * stage - step


def phase_state(label, pot, coded=False):
    if coded:
        q = [jnp.where(label == 0.0, 1.0, jnp.where(label == 1.0, CODE, jnp.where(label == 2.0, CODE * CODE, 0.0)))]
    else:
        q = [jnp.where(label == float(a), LAM, 0.0) for a in range(3)]
    y = [jnp.where(label == float(a), LAM * BETA * OWN, 0.0) for a in range(3)]
    liquid = label == 3.0
    mob = jnp.where(liquid, 0.15, 0.0075)
    u = [MU * v for v in pot]
    comp = [jnp.where(liquid, 0.35 * MU, jnp.where(label == float(i), 0.8 * MU, 0.1 * MU)) for i in range(2)]
    rest = [(u[i] + comp[i]) - (6.0 * mob) * u[i] for i in range(2)]
    return q + u + y + rest + [mob]


def decode(total):
    third = jnp.floor(total * (1.0 / (CODE * CODE)))
    total = total - (CODE * CODE) * third
    second = jnp.floor(total * (1.0 / CODE))
    return [LAM * v for v in (total - CODE * second, second, third)]


def moving_of(step):
    return (0, 3, 4) if step == 1 else tuple(range(MOVING))


def clip_step(sums, y):
    x = [sums[a] + y[a] for a in range(3)]
    x.append(1.0 - (x[0] + x[1] + x[2]))
    held = [jnp.clip(v, 0.0, 1.0) for v in x]
    return held, 1.0 / ((held[0] + held[1]) + (held[2] + held[3]))


def cell_step(sums, y, rest, mob, tick=lambda: None):
    held, inverse = clip_step(sums, y)
    tick()
    total = [rest[i] + mob * sums[3 + i] for i in range(2)]
    tick()
    scaled = LAM * inverse
    q = [v * scaled for v in held]
    tick()
    square = [v * v for v in q]
    tick()
    h = [square[a] * (1.5 * LAM - q[a]) for a in range(4)]
    tick()
    shared = BACK * ((h[0] + h[1]) + (h[2] + 3.5 * h[3]))
    tick()
    u = [(total[i] - shared) - (7.0 * BACK) * h[i] for i in range(2)]
    tick()
    both = u[0] + u[1]
    well = OWN - ((square[0] + square[1]) + (square[2] + square[3]))
    tick()
    third = both * (1.0 / 7.0) + TILT
    pull = [third + u[0], third + u[1], third, 0.5 * both]
    tick()
    mob = 0.0075 + (0.1425 / LAM) * q[3]
    six = 6.0 * mob
    rest = [total[i] - six * u[i] for i in range(2)]
    tick()
    local = []
    for a in range(4):
        local.append(q[a] * ((well + square[a]) + pull[a] * (LAM - q[a])))
        tick()
    mean = 0.25 * ((local[0] + local[1]) + (local[2] + local[3])) - 0.07 / BETA
    tick()
    y = [BETA * (local[a] - mean) for a in range(3)]
    tick()
    return q[:3] + u + y + rest + [mob]


def last_step(sums, y, rest, mob):
    held, inverse = clip_step(sums, y)
    p = [v * inverse for v in held]
    h = [v * v * (1.5 - v) for v in p]
    shared = 0.2 * ((h[0] + h[1]) + (h[2] + 3.5 * h[3]))
    total = [(rest[i] + mob * sums[3 + i]) * (1.0 / MU) for i in range(2)]
    return p, [(total[i] - shared) - 1.4 * h[i] for i in range(2)]


def lanes():
    return lax.broadcasted_iota(jnp.int32, (8, 128), 1)


def side_sums(state, near, row, low, at_left, at_right):
    slot, group = divmod(row, GROUPS)
    turn = 128 - (SLOT * slot + HALF // 2 + 1)
    sums = []
    for f in range(MOVING):
        v = state[f, row, pl.ds(low, 8), :]
        edge = pltpu.roll(near[f, group, pl.ds(low, 8), :], turn, 1)
        right = pltpu.roll(jnp.where(at_left, edge, v), 127, 1)
        left = pltpu.roll(jnp.where(at_right, edge, v), 1, 1)
        sums.append(right + left)
    return sums


def main_sums(state, row, low, sides):
    sums = []
    for f in range(MOVING):
        grow = state[f, row, pl.ds(low + 1, 8), :] + state[f, row, pl.ds(low - 1, 8), :]
        side = state[f, row + 1, pl.ds(low, 8), :] + state[f, row - 1, pl.ds(low, 8), :]
        sums.append((grow + side) + sides[f])
    return sums


def center(state, row, low):
    y = [state[MOVING + a, row, pl.ds(low, 8), :] for a in range(3)]
    rest = [state[MOVING + 3 + i, row, pl.ds(low, 8), :] for i in range(2)]
    return y, rest, state[FIELDS - 1, row, pl.ds(low, 8), :]


def near_of(v, swap):
    return jnp.where(swap, pltpu.roll(v, 128 - (HALF - 1), 1), v)


def front_kernel(
    plan, mesh_shape, levels, lab_hbm, pot_hbm, codes_hbm, table_hbm, out_state, out_near,
    lab, pot, codes, table, lab_up, pot_up, raw, pack, strip, across_pack, across, even, odd, even_near, odd_near, even_strip, odd_strip, out_strip, sides, strip_sides,
    in_sems, g_send, g_recv, y_send, y_recv, z_send, z_recv, a_send, a_recv,
):
    g, y, z = lax.axis_index("grow"), lax.axis_index("gy"), lax.axis_index("gz")
    count_g, count_y, count_z = mesh_shape
    rows, tall, planes, shift = plan.rows, plan.tall, plan.planes, plan.shift
    has_below, has_above = g > 0, g < count_g - 1
    is_first, is_last = g == 0, g == count_g - 1
    y_up, y_down = lax.rem(y + 1, count_y), lax.rem(y + count_y - 1, count_y)
    z_other = lax.rem(z + 1, count_z)
    chunks = plan.chunks
    own_chunks, lead, pieces = plan.own_chunks, plan.lead, plan.pieces

    loads = [
        pltpu.make_async_copy(lab_hbm, lab, in_sems.at[0]),
        pltpu.make_async_copy(pot_hbm, pot, in_sems.at[1]),
    ]
    melt_loads = [
        pltpu.make_async_copy(codes_hbm, codes, in_sems.at[2]),
        pltpu.make_async_copy(table_hbm, table, in_sems.at[3]),
    ]
    for copy in loads:
        copy.start()

    @pl.when(is_last)
    def _():
        for copy in melt_loads:
            copy.start()

    barrier = pltpu.get_barrier_semaphore()

    def greet(target):
        pl.semaphore_signal(barrier, inc=1, device_id=target, device_id_type=MESH)

    @pl.when(has_below)
    def _():
        greet((g - 1, y, z))

    @pl.when(has_above)
    def _():
        greet((g + 1, y, z))

    greet((g, y_up, z))
    greet((g, y_down, z))
    greet((g, y, z_other))
    greet((g, y_up, z_other))
    greet((g, y_down, z_other))

    splits = [max(8 * piece - lead, 0) for piece in range(pieces + 1)]

    def g_copies(piece):
        begin, end = splits[piece], splits[piece + 1]
        src, dst = pl.ds(begin * rows, (end - begin) * rows), pl.ds((lead + begin) * rows, (end - begin) * rows)
        copies = []
        for i in range(3):
            source, target = (lab_hbm.at[src], lab_up.at[dst]) if i == 0 else (pot_hbm.at[i - 1, src], pot_up.at[i - 1, dst])
            sem = 3 * piece + i
            copies.append(pltpu.make_async_remote_copy(
                src_ref=source, dst_ref=target, send_sem=g_send.at[sem], recv_sem=g_recv.at[sem],
                device_id=(g - 1, y, z), device_id_type=MESH))
        return copies

    def planes_of(chunk):
        return pl.ds(7, 1) if isinstance(chunk, int) and chunk == 0 else pl.ds(8 * chunk, 8)

    def either(chunk, action):
        pl.when(chunk == 0)(lambda: action(0))
        pl.when(chunk > 0)(lambda: action(chunk))

    def y_copies(chunk):
        copies = []
        for up in range(2):
            src, dst, target = (rows, 0, y_up) if up else (STEPS, STEPS + rows, y_down)
            sem = 2 * chunk + up
            at = planes_of(chunk)
            copies.append(pltpu.make_async_remote_copy(
                src_ref=raw.at[:, pl.ds(src, STEPS), at], dst_ref=raw.at[:, pl.ds(dst, STEPS), at],
                send_sem=y_send.at[sem], recv_sem=y_recv.at[sem],
                device_id=(g, target, z), device_id_type=MESH))
        return copies

    def z_copy(chunk):
        at = pl.ds(8 * chunk, 8)
        return pltpu.make_async_remote_copy(
            src_ref=pack.at[:, :, at], dst_ref=strip.at[:, :, at],
            send_sem=z_send.at[chunk], recv_sem=z_recv.at[chunk],
            device_id=(g, y, z_other), device_id_type=MESH)

    def across_copies(chunk):
        at = planes_of(chunk)
        copies = []
        for k, row in enumerate((y_up, y, y_down)):
            sem = 3 * chunk + k
            copies.append(pltpu.make_async_remote_copy(
                src_ref=across_pack.at[:, :, at], dst_ref=across.at[k, :, :, at],
                send_sem=a_send.at[sem], recv_sem=a_recv.at[sem],
                device_id=(g, row, z_other), device_id_type=MESH))
        return copies

    def fill(labels, pots, begin, to):
        for row in range(rows):
            at = pl.ds(begin * rows + row, 8, stride=rows)
            raw[0, STEPS + row, pl.ds(to, 8)] = labels[at].astype(jnp.float32)
            for i in range(2):
                raw[1 + i, STEPS + row, pl.ds(to, 8)] = pots[i, at]

    def send_y(chunk):
        for copy in y_copies(chunk):
            copy.start()

    lane = lanes()

    def pack_rows(target, chunk, source):
        at = pl.ds(8 * chunk, 8)

        def pack_field(i, carry):
            for group in range(GROUPS):
                packed = jnp.zeros((8, 128), jnp.float32)
                for slot in range(tall // GROUPS):
                    v = raw[i, source(GROUPS * slot + group), at]
                    first = SLOT * slot
                    packed = jnp.where(lane >= first, pltpu.roll(v, first + HALF // 2 + 1, 1), packed)
                    packed = jnp.where(lane >= first + HALF, pltpu.roll(v, first + HALF + HALF // 2, 1), packed)
                target[i, group, at] = packed
            return carry

        lax.fori_loop(0, 3, pack_field, 0)

    def row_across(row):
        return row + rows if row < STEPS else row - rows if row >= STEPS + rows else row

    def start_all(copies):
        for copy in copies:
            copy.start()

    def send_across(chunk, carry):
        pack_rows(across_pack, chunk, row_across)
        either(chunk, lambda k: start_all(across_copies(k)))
        return carry

    def wait_all(copies):
        for copy in copies:
            copy.wait_recv()

    def send_z(chunk):
        either(chunk, lambda k: wait_all(y_copies(k)))
        pack_rows(pack, chunk, lambda row: row)

        @pl.when(chunk >= own_chunks)
        def _():
            z_copy(chunk).start()

    def receive_z(chunk):
        @pl.when(chunk >= own_chunks)
        def _():
            z_copy(chunk).wait_recv()

        @pl.when(chunk < own_chunks)
        def _():
            either(chunk, lambda k: wait_all(across_copies(k)))
            at = pl.ds(8 * chunk, 8)
            for group in range(GROUPS):
                own, upper = -((group - STEPS) // GROUPS), -((group - STEPS - rows) // GROUPS)
                for i in range(3):
                    value = jnp.where(lane >= SLOT * own, across[1, i, group, at], across[0, i, group, at])
                    strip[i, group, at] = jnp.where(lane >= SLOT * upper, across[2, i, group, at], value)

    place = lane % SLOT
    from_other = (place < HALF // 2 + 1) | (place >= SLOT - HALF // 2 - 1)
    swap = place == HALF // 2 + 1
    at_left, at_right = lane == 0, lane == 127

    def unpack_row(state, slot, row, source, target):
        at = pl.ds(source, 8)
        new = phase_state(raw[0, row, at], [raw[1, row, at], raw[2, row, at]])
        for f in range(FIELDS):
            state[slot, f, row, pl.ds(target, 8)] = new[f]

    def unpack_strips(state, near, slot, source, target):
        at, to = pl.ds(source, 8), pl.ds(target, 8)
        for group in range(GROUPS):
            value = [jnp.where(from_other, strip[i, group, at], pack[i, group, at]) for i in range(3)]
            for f, v in zip(CODED_AT, phase_state(value[0], value[1:], True)):
                state[slot, f, group, to] = v
                if f < MOVING:
                    near[slot, f, group, to] = near_of(v, swap)

    def unpack(chunk):
        to = 8 * chunk

        def body(part, carry):
            rows_at = pl.ds(tall // GROUPS * part, tall // GROUPS)
            at = pl.ds(to, 8)
            new = phase_state(raw[0, rows_at, at], [raw[1, rows_at, at], raw[2, rows_at, at]], True)
            for f, v in zip(CODED_AT, new):
                even[0, f, rows_at, at] = v
            return carry

        lax.fori_loop(0, GROUPS, body, 0)
        unpack_strips(even_strip, even_near, 0, to, to)

    def strip_side_steps(fields, src, slot, low, result):
        at = pl.ds(low, 8)

        def piece(f):
            v = src[slot, f, :, at]
            part = [src[slot, f, group, at] for group in range(GROUPS)]
            up = jnp.stack([part[1], part[2], pltpu.roll(part[0], 128 - SLOT, 1)])
            down = jnp.stack([pltpu.roll(part[2], SLOT, 1), part[0], part[1]])
            result[f] = (up + down) + (pltpu.roll(v, 127, 2) + pltpu.roll(v, 1, 2))

        return [functools.partial(piece, f) for f in fields]

    def strip_step(step, src, src_slot, dst, near, dst_slot, low, around, tick):
        at = pl.ds(low, 8)
        sums = []
        for f in moving_of(step):
            total = src[src_slot, f, :, pl.ds(low + 1, 8)] + src[src_slot, f, :, pl.ds(low - 1, 8)]
            sums.append(total + around[f])
            tick()
        if step == 1:
            sums = decode(sums[0]) + sums[1:]
        y = [src[src_slot, MOVING + a, :, at] for a in range(3)]
        rest = [src[src_slot, MOVING + 3 + i, :, at] for i in range(2)]
        new = cell_step(sums, y, rest, src[src_slot, FIELDS - 1, :, at], tick)
        for f in range(FIELDS):
            dst[dst_slot, f, :, at] = new[f]
        for f in range(MOVING):
            near[dst_slot, f, :, at] = jnp.where(swap, pltpu.roll(new[f], 128 - (HALF - 1), 2), new[f])

    def side_steps(fields, state, near, first, count, low, result):
        v, edge, ends = {}, {}, {}

        def near_rolls(f):
            rolled = []
            for i in range(count):
                slot, group = divmod(first + i, GROUPS)
                rolled.append(pltpu.roll(near[f, group, pl.ds(low, 8), :], 128 - (SLOT * slot + HALF // 2 + 1), 1))
            edge[f] = jnp.stack(rolled)
            v[f] = state[f, first : first + count, pl.ds(low, 8), :]

        def z_rolls(f):
            right = pltpu.roll(jnp.where(at_left, edge[f], v[f]), 127, 2)
            left = pltpu.roll(jnp.where(at_right, edge[f], v[f]), 1, 2)
            ends[f] = (right, left)

        def add(f):
            result[f] = ends[f][0] + ends[f][1]

        pieces = []
        for k in range(len(fields) + 2 * LAG):
            if k < len(fields):
                pieces.append(functools.partial(near_rolls, fields[k]))
            if LAG <= k < len(fields) + LAG:
                pieces.append(functools.partial(z_rolls, fields[k - LAG]))
            if k >= 2 * LAG:
                pieces.append(functools.partial(add, fields[k - 2 * LAG]))
        return pieces

    class Ahead:
        def __init__(self, pieces=()):
            self.pieces = list(pieces)

        def __call__(self):
            if self.pieces:
                self.pieces.pop(0)()

        def flush(self):
            while self.pieces:
                self()

    def sizes_of(step):
        total = tall - 2 * step
        parts = -(-total // BATCH)
        return [total // parts + (k < total % parts) for k in range(parts)]

    def buffers(step):
        if step == STEPS - 1:
            return out_state, out_near, out_strip, 0
        if step % 2:
            return odd, odd_near, odd_strip, step // 2
        return even, even_near, even_strip, step // 2

    def begin_steps(stage, step, around, strip_around):
        state, near, strips, slot = buffers(step - 1)
        low = plan.low(stage, step)
        rows_ahead = side_steps(moving_of(step), state.at[slot], near.at[slot], step, sizes_of(step)[0], low, around)
        return rows_ahead, strip_side_steps(moving_of(step), strips, slot, low, strip_around)

    def keep(around, strip_around):
        for f in around:
            sides[: around[f].shape[0], f] = around[f]
            strip_sides[f] = strip_around[f]

    def begin(stage, step):
        around, strip_around = {}, {}
        rows_ahead, strips_ahead = begin_steps(stage, step, around, strip_around)
        for piece in strips_ahead + rows_ahead:
            piece()
        keep(around, strip_around)

    def row_steps(stage, step):
        src, src_near, src_strip, slot = buffers(step - 1)
        dst, dst_near, dst_strip, dst_slot = buffers(step)
        state, near = src.at[slot], src_near.at[slot]
        low = plan.low(stage, step)
        sizes = sizes_of(step)
        at = pl.ds(low, 8)
        ready, strip_ready = {}, {}
        if step == 1:
            rows_ahead, strips_ahead = begin_steps(stage, step, ready, strip_ready)
            Ahead(strips_ahead).flush()
            ahead = Ahead(rows_ahead)
        else:
            ready = {f: sides[: sizes[0], f] for f in moving_of(step)}
            strip_ready = {f: strip_sides[f] for f in moving_of(step)}
            ahead = Ahead()
        strip_step(step, src_strip, slot, dst_strip, dst_near, dst_slot, low, strip_ready, ahead)
        ahead.flush()
        row = step
        for k, size in enumerate(sizes):
            around, ready, strip_ready = ready, {}, {}
            if k + 1 < len(sizes):
                ahead = Ahead(side_steps(moving_of(step), state, near, row + size, sizes[k + 1], low, ready))
            elif step < STEPS - 1:
                rows_ahead, strips_ahead = begin_steps(stage, step + 1, ready, strip_ready)
                ahead = Ahead(strips_ahead + rows_ahead)

            def rows_of(f, shift=0, up=0):
                return state[f, row + shift : row + shift + size, pl.ds(low + up, 8), :]

            sums = []
            for f in moving_of(step):
                grow = rows_of(f, 0, 1) + rows_of(f, 0, -1)
                side = rows_of(f, 1) + rows_of(f, -1)
                sums.append((grow + side) + around[f])
                ahead()
            if step == 1:
                sums = decode(sums[0]) + sums[1:]
            y = [rows_of(MOVING + a) for a in range(3)]
            rest = [rows_of(MOVING + 3 + i) for i in range(2)]
            new = cell_step(sums, y, rest, rows_of(FIELDS - 1), ahead)
            ahead.flush()
            for f in range(FIELDS):
                dst[dst_slot, f, row : row + size, at, :] = new[f]
            row += size
        if step < STEPS - 1:
            keep(ready, strip_ready)

    def copy_plane(state, strips, near, slot, source, target):
        src, dst = pl.ds(source, 1), pl.ds(target, 1)

        def body(row, carry):
            for f in range(MOVING):
                state[slot, f, row, dst] = state[slot, f, row, src]
            return carry

        lax.fori_loop(0, tall, body, 0)
        for group in range(GROUPS):
            for f in range(MOVING):
                strips[slot, f, group, dst] = strips[slot, f, group, src]
                near[slot, f, group, dst] = near[slot, f, group, src]

    first_plane, top_plane = plan.at(shift), plan.at(planes)
    last_plane = first_plane + planes - 1
    place_up = lax.broadcasted_iota(jnp.int32, (8, 128), 0)

    def melt_fill(stage):
        source, target = 8 * stage + 8, 8 * stage + 7
        melt = place_up >= top_plane - target
        at, to = pl.ds(source, 8), pl.ds(target, 8)

        def body(row, carry):
            new = phase_state(raw[0, row, at], [raw[1, row, at], raw[2, row, at]])
            for f in range(FIELDS):
                pltpu.store(odd.at[1, f, row, to], new[f], mask=melt)
            return carry

        lax.fori_loop(STEPS_BEFORE, tall - STEPS_BEFORE, body, 0)
        for group in range(GROUPS):
            value = [jnp.where(from_other, strip[i, group, at], pack[i, group, at]) for i in range(3)]
            new = phase_state(value[0], value[1:])
            for f in range(FIELDS):
                pltpu.store(odd_strip.at[1, f, group, to], new[f], mask=melt)
            for f in range(MOVING):
                pltpu.store(odd_near.at[1, f, group, to], near_of(new[f], swap), mask=melt)

    def stage_of(plane, step):
        return (plane - plan.low(0, step)) // 8

    def compute(stage):
        top = stage_of(top_plane, STEPS_BEFORE)
        below_melt = (stage <= top) | jnp.logical_not(is_last)

        eventful = (is_first & (stage == stage_of(first_plane, STEPS_BEFORE))) | (is_last & (stage >= top))

        @pl.when(jnp.logical_not(eventful) & (stage < 2))
        def _():
            for step in range(1, STEPS):
                row_steps(stage, step)
                if step == HOOK:
                    pass_on(stage)

        @pl.when(jnp.logical_not(eventful) & (stage >= 2))
        def _():
            for step in range(1, STEPS):
                row_steps(stage, step)

        @pl.when(eventful)
        def _():
            for step in range(1, STEPS):
                state, near, strips, slot = buffers(step)
                out = (state, strips, near, slot)

                if step <= STEPS_BEFORE:
                    pl.when(below_melt)(functools.partial(row_steps, stage, step))
                else:
                    row_steps(stage, step)

                if step < STEPS_BEFORE:
                    @pl.when(is_last & (stage == stage_of(top_plane, step)))
                    def _():
                        copy_plane(*out, top_plane - 1, top_plane)
                else:
                    @pl.when(is_first & (stage == stage_of(first_plane, step)))
                    def _():
                        copy_plane(*out, first_plane, first_plane - 1)

                if step == HOOK:
                    pass_on(stage)

                if step == STEPS_BEFORE:
                    @pl.when(is_last & (stage >= top))
                    def _():
                        melt_fill(stage)
                        begin(stage, step + 1)

                if step == STEPS - 1:
                    @pl.when(is_last & (stage == stage_of(last_plane, step)))
                    def _():
                        copy_plane(*out, last_plane, last_plane + 1)

    pl.semaphore_wait(barrier, 5 + has_below.astype(jnp.int32) + has_above.astype(jnp.int32))

    @pl.when(has_below)
    def _():
        for piece in range(pieces):
            for copy in g_copies(piece):
                copy.start()

    for copy in loads:
        copy.wait()

    def fill_own(chunk, carry):
        fill(lab, pot, plan.base + 8 * chunk, 8 * chunk)
        either(chunk, send_y)
        return send_across(chunk, carry)

    lax.fori_loop(0, own_chunks, fill_own, 0)
    tail = pl.ds((planes - lead) * rows, lead * rows)
    lab_up[0 : lead * rows] = lab[tail]
    for i in range(2):
        pot_up[i, 0 : lead * rows] = pot[i, tail]

    @pl.when(is_last)
    def _():
        for copy in melt_loads:
            copy.wait()
        plane = pl.ds((planes - 1) * rows, rows)
        at = pl.ds(lead * rows, rows)
        lab_up[at] = lab[plane]
        for i in range(2):
            pot_up[i, at] = pot[i, plane]

        def melt_plane(k, carry):
            code = codes[pl.ds(pl.multiple_of(jnp.minimum(k, shift - 1) * rows, rows), rows)]
            at = pl.ds(pl.multiple_of((lead + 1 + k) * rows, rows), rows)
            lab_up[at] = jnp.full((rows, 128), 3, jnp.int32)
            for i in range(2):
                value = jnp.zeros((rows, 128), jnp.float32)
                for level in range(levels):
                    value = jnp.where(code == level, table[i, level], value)
                pot_up[i, at] = value
            return carry

        lax.fori_loop(0, 8 * pieces - lead - 1, melt_plane, 0)

    def z_body(chunk, carry):
        send_z(chunk)
        return carry

    def pass_on(stage):
        @pl.when(stage == 0)
        def _():
            take(pieces)

        @pl.when(stage == 1)
        def _():
            lax.fori_loop(own_chunks + 1, chunks, z_body, 0)

    def beat(it, carry):
        lax.fori_loop(jnp.where(it == 3, 2, it), jnp.where(it == 3, 4, jnp.where(it < 2, it + 1, it)), z_body, 0)

        @pl.when((it == 0) | ((it >= 2) & (it < pieces)))
        def _():
            take(it)

        @pl.when(it >= 1)
        def _():
            receive_z(it - 1)
            unpack(it - 1)

        @pl.when(it >= 2)
        def _():
            compute(it - 2)

        return carry

    def take(it):
        piece = jnp.maximum(it - 1, 0)
        for k in range(pieces):
            @pl.when(has_above & (piece == k))
            def _():
                for copy in g_copies(k):
                    copy.wait_recv()

        fill(lab_up, pot_up, 8 * piece, 8 * (own_chunks + piece))
        send_y(own_chunks + piece)

    lax.fori_loop(0, plan.stages + 2, beat, 0)

    def drain(chunk, carry):
        def wait(copies):
            for copy in copies:
                copy.wait_send()

        either(chunk, lambda k: wait(y_copies(k)))

        @pl.when(chunk >= own_chunks)
        def _():
            z_copy(chunk).wait_send()

        @pl.when(chunk < own_chunks)
        def _():
            either(chunk, lambda k: wait(across_copies(k)))

        return carry

    lax.fori_loop(0, chunks, drain, 0)

    @pl.when(has_below)
    def _():
        for piece in range(pieces):
            for copy in g_copies(piece):
                copy.wait_send()


def last_kernel(plan, state, near, phases, potentials, p_out, m_out, sems):
    rows, planes = plan.rows, plan.planes
    at_left, at_right = lanes() == 0, lanes() == 127
    begin, tiles = plan.at(plan.shift), planes // 8

    def out_copies(tile):
        at = pl.ds(8 * tile * rows, 8 * rows)
        return [
            pltpu.make_async_copy(src.at[:, at], dst.at[:, at], sems.at[2 * tile + i])
            for i, (src, dst) in enumerate(((p_out, phases), (m_out, potentials)))
        ]

    def body(tile, carry):
        low = begin + 8 * tile
        for row in range(rows):
            src = state.at[0]
            sums = main_sums(src, STEPS + row, low, side_sums(src, near.at[0], STEPS + row, low, at_left, at_right))
            p, m = last_step(sums, *center(src, STEPS + row, low))
            at = pl.ds(8 * tile * rows + row, 8, stride=rows)
            for f in range(4):
                p_out[f, at, :] = p[f]
            for i in range(2):
                m_out[i, at, :] = m[i]
        for copy in out_copies(tile):
            copy.start()
        return carry

    lax.fori_loop(0, tiles, body, 0)
    for tile in range(tiles):
        for copy in out_copies(tile):
            copy.wait()


def on_device(mesh_shape, labels, potential, melt_codes, melt_table):
    planes, rows, width = labels.shape
    shift, levels = melt_codes.shape[0], melt_table.shape[1]
    plan = Plan(planes, rows, shift)
    flat = planes * rows
    vmem = pl.BlockSpec(memory_space=pltpu.VMEM)
    hbm = pl.BlockSpec(memory_space=pltpu.HBM)
    f32 = jnp.float32
    dma = pltpu.SemaphoreType.DMA
    deep, tall, chunks = plan.deep, plan.tall, plan.chunks
    evens, odds = STEPS // 2, STEPS // 2
    upper = 8 * plan.pieces * rows
    kept = (FIELDS * tall + MOVING * GROUPS) * deep * width * 4
    state, near = pl.pallas_call(
        functools.partial(front_kernel, plan, mesh_shape, levels),
        out_shape=(
            pltpu.VMEM((1, FIELDS, tall, deep, width), f32),
            pltpu.VMEM((1, MOVING, GROUPS, deep, width), f32),
        ),
        in_specs=[hbm, hbm, hbm, hbm],
        out_specs=(vmem, vmem),
        scratch_shapes=[
            pltpu.VMEM((flat, width), jnp.int32),
            pltpu.VMEM((2, flat, width), f32),
            pltpu.VMEM((shift * rows, width), jnp.int32),
            pltpu.SMEM((2, levels), f32),
            pltpu.VMEM((upper, width), jnp.int32),
            pltpu.VMEM((2, upper, width), f32),
            pltpu.VMEM((3, tall, deep, width), f32),
            pltpu.VMEM((3, GROUPS, deep, width), f32),
            pltpu.VMEM((3, GROUPS, deep, width), f32),
            pltpu.VMEM((3, GROUPS, 8 * plan.own_chunks, width), f32),
            pltpu.VMEM((3, 3, GROUPS, 8 * plan.own_chunks, width), f32),
            pltpu.VMEM((evens, FIELDS, tall, deep, width), f32),
            pltpu.VMEM((odds, FIELDS, tall, deep, width), f32),
            pltpu.VMEM((evens, MOVING, GROUPS, deep, width), f32),
            pltpu.VMEM((odds, MOVING, GROUPS, deep, width), f32),
            pltpu.VMEM((evens, FIELDS, GROUPS, deep, width), f32),
            pltpu.VMEM((odds, FIELDS, GROUPS, deep, width), f32),
            pltpu.VMEM((1, FIELDS, GROUPS, deep, width), f32),
            pltpu.VMEM((BATCH, MOVING, 8, width), f32),
            pltpu.VMEM((MOVING, GROUPS, 8, width), f32),
            dma((4,)), dma((3 * chunks,)), dma((3 * chunks,)),
            dma((2 * chunks,)), dma((2 * chunks,)), dma((chunks,)), dma((chunks,)),
            dma((3 * plan.own_chunks,)), dma((3 * plan.own_chunks,)),
        ],
        compiler_params=pltpu.CompilerParams(collective_id=0, has_side_effects=True, vmem_limit_bytes=(VMEM_BYTES - kept) // 4096 * 4096),
        name="front",
    )(labels.reshape(flat, width), potential.reshape(2, flat, width), melt_codes.reshape(shift * rows, width), melt_table)
    state, near = (pltpu.with_memory_space_constraint(v, pltpu.VMEM) for v in (state, near))
    phases, potentials = pl.pallas_call(
        functools.partial(last_kernel, plan),
        out_shape=(
            jax.ShapeDtypeStruct((4, flat, width), f32),
            jax.ShapeDtypeStruct((2, flat, width), f32),
        ),
        in_specs=[vmem, vmem],
        out_specs=(hbm, hbm),
        scratch_shapes=[
            pltpu.VMEM((4, flat, width), f32),
            pltpu.VMEM((2, flat, width), f32),
            dma((2 * (planes // 8),)),
        ],
        compiler_params=pltpu.CompilerParams(vmem_limit_bytes=8 << 20),
        name="last",
    )(state, near)
    return phases.reshape(4, planes, rows, width), potentials.reshape(2, planes, rows, width)


def solution(mesh):
    mesh_shape = tuple(mesh.shape[axis] for axis in ("grow", "gy", "gz"))
    return jax.shard_map(
        functools.partial(on_device, mesh_shape),
        mesh=mesh,
        in_specs=(P("grow", "gy", "gz"), P(None, "grow", "gy", "gz"), P(None, "gy", "gz"), P()),
        out_specs=(P(None, "grow", "gy", "gz"), P(None, "grow", "gy", "gz")),
        check_vma=False,
    )
```
